32 devices in a mesh: dp: 4 (over y, core), seq: 8 (over z, x).
Axes of the slice: x: 2, y: 2, z: 4, core: 2. Of those that a mesh axis runs over, the one named last changes fastest.
Arguments:
- hidden_in: bfloat16 [4, 1024, 2048], P('dp', 'seq'), may hold values from -6 to 6
- in_weight: bfloat16 [2048, 6160], P(('dp', 'seq')), may hold values from -0.125 to 0.125
- out_weight: bfloat16 [2048, 2048], P(('dp', 'seq')), may hold values from -0.125 to 0.125
- decay_up: bfloat16 [16, 1024], P(None, ('dp', 'seq')), may hold values from -1.5 to 1.5
- decay_bias: bfloat16 [1024], P(('dp', 'seq')), may hold values from 0.5 to 6
- mixer_gain: bfloat16 [2048], P(('dp', 'seq')), may hold values from 0.099609375 to 1.8984375
- head_gain: bfloat16 [512], P(('dp', 'seq')), may hold values from 0.099609375 to 1.8984375
- ffn_in: bfloat16 [2048, 11264], P(('dp', 'seq')), may hold values from -0.125 to 0.125
- ffn_out: bfloat16 [5632, 2048], P(('dp', 'seq')), may hold values from -0.078125 to 0.078125
- ffn_gain: bfloat16 [2048], P(('dp', 'seq')), may hold values from 0.099609375 to 1.8984375
- out_grad: bfloat16 [4, 1024, 2048], P('dp', 'seq'), may hold values from -6 to 6
- seg_ids: int32 [4, 1024], P('dp', 'seq'), may hold values from 0 to 7, never falling along the last dimension, each value on 1 to 512 neighbouring positions
- valid_mask: int32 [4, 1024], P('dp', 'seq'), may hold values from 0 to 1
Outputs:
- block_out: bfloat16 [4, 1024, 2048], P('dp', 'seq')
- input_grad: float32 [4, 1024, 2048], P('dp', 'seq')
- inproj_grad: float32 [2048, 6160], P(('dp', 'seq'))
- outproj_grad: float32 [2048, 2048], P(('dp', 'seq'))
- decayup_grad: float32 [16, 1024], P(None, ('dp', 'seq'))
- decaybias_grad: float32 [1024], P(('dp', 'seq'))
- mixgain_grad: float32 [2048], P(('dp', 'seq'))
- headgain_grad: float32 [512], P(('dp', 'seq'))
- ffnin_grad: float32 [2048, 11264], P(('dp', 'seq'))
- ffnout_grad: float32 [5632, 2048], P(('dp', 'seq'))
- ffngain_grad: float32 [2048], P(('dp', 'seq'))
- root_means: float32 [3], replicated
The draws below stay inside these ranges and needn't reach their ends.
Inputs may be any that keep to these rules, and one draw needn't show every extreme that they name: `seg_ids`: a sequence's segment numbers never fall; a segment holds at most 512 tokens, and one segment of each sequence exactly that many.
All inputs are finite; a program needn't handle non-finite values.
Results may differ from the reference program's by a relative error of at most 0.012.
Values may be sent and summed in bfloat16 or wider, within the bound.
No kernel may reach another device: no remote copies, remote signals or barrier semaphores. Data moves between devices by JAX's collectives and lax.ppermute only.
A program may use at most 384 MiB of HBM per device.

```python
import math
import jax
import jax.numpy as jnp
import numpy as np
from jax import lax

D = 2048
HEADS = 4
KEY = 256
VAL = 512
RANK = 16
FF = 5632
SPAN = 64
SEQS = 4
LEN = 1024
PROJ = 6160


def draw_hidden_in(key, part):
    place = jnp.arange(SEQS, dtype=jnp.float32)[:, None] * LEN + jnp.arange(LEN, dtype=jnp.float32)[None, :]
    fraction = place / (SEQS * LEN)
    first_key = jax.random.fold_in(key, 0)
    position_scale = 0.5 + fraction
    noise_base = jnp.clip(jax.random.normal(first_key, (SEQS, LEN, D), jnp.float32), -4.0, 4.0)
    return (noise_base * position_scale[:, :, None]).astype(jnp.bfloat16)


def draw_valid_mask(key, part):
    place = jnp.arange(SEQS, dtype=jnp.int32)[:, None] * LEN + jnp.arange(LEN, dtype=jnp.int32)[None, :]
    threshold = 250 + 700 * place // (SEQS * LEN)
    ticket = jax.random.randint(jax.random.fold_in(key, 17), (SEQS, LEN), 0, 1000, jnp.int32)
    return (ticket < threshold).astype(jnp.int32)


def levels(own_key, dims, cuts, low, largest):
    def one(dim, shards_of):
        steps = jax.random.uniform(jax.random.fold_in(jax.random.fold_in(own_key, 6), dim), (shards_of,), jnp.float32, low / len(cuts), largest / len(cuts))
        return jnp.repeat(jnp.exp(steps), dims[dim] // shards_of).reshape((-1,) + (1,) * (len(dims) - dim - 1))

    level = one(*cuts[0])
    for cut in cuts[1:]:
        level = level * one(*cut)
    return level


def length_profile(amount, total, reach, skew):
    portions = [(1 << 20) // math.isqrt(grade ** skew) + 1 for grade in range(2, amount + 1)]
    surplus, counts = total - reach - (amount - 1), [1] * (amount - 1)
    while surplus > 0:
        movable = [i for i in range(amount - 1) if counts[i] < reach]
        mass, remaining = sum([portions[i] for i in movable]), surplus
        for i in movable:
            extra = min(reach - counts[i], max(1, remaining * portions[i] // mass), surplus)
            counts[i] = counts[i] + extra
            surplus = surplus - extra
    return np.array([reach] + counts)


def uneven(key, number_of, total, limit, skew):
    if number_of == 2:
        one = jax.random.randint(key, (), max(1, total - limit), min(limit, total - 1) + 1)
        return jnp.stack([one, total - one])
    lengths = jnp.asarray(length_profile(number_of, total, limit, skew), jnp.int32)
    pairs = (number_of - 1) // 2
    source_of, sink = lengths[1:1 + 2 * pairs:2], lengths[2:2 + 2 * pairs:2]
    slack = jnp.minimum(source_of - 1, limit - sink)
    shifted = jax.random.randint(jax.random.fold_in(key, 1), (pairs,), 0, 1 << 20) % (slack + 1)
    lengths = lengths.at[1:1 + 2 * pairs:2].set(source_of - shifted).at[2:2 + 2 * pairs:2].set(sink + shifted)
    return lengths[jax.random.permutation(jax.random.fold_in(key, 2), number_of)]


def normal_values(own_key, dims, deviation, most, cuts=(), held_as=jnp.bfloat16):
    level = levels(own_key, dims, cuts, -0.22, 0.18) if cuts else 1.0
    entries = jax.random.normal(own_key, dims, jnp.float32) * deviation * level
    return jnp.minimum(jnp.maximum(entries, -most), most).astype(held_as)


def setup_inputs(seed: int = 0) -> dict:
    splits = jax.random.split(jax.random.key(seed), 14)
    return {
        "hidden_in": draw_hidden_in(jax.random.fold_in(splits[13], 71), 0),
        "in_weight": normal_values(splits[1], (D, PROJ), D ** -0.5, 0.125, ((0, 32),)),
        "out_weight": normal_values(splits[2], (HEADS * VAL, D), (HEADS * VAL) ** -0.5, 0.125, ((0, 32),)),
        "decay_up": normal_values(splits[3], (RANK, HEADS * KEY), RANK ** -0.5, 1.5, ((1, 32),)),
        "decay_bias": jnp.clip(0.5 + 5.5 * jax.random.uniform(splits[4], (HEADS * KEY,), jnp.float32) ** levels(splits[4], (HEADS * KEY,), ((0, 32),), -0.2, 0.2), 0.5, 6.0).astype(jnp.bfloat16),
        "mixer_gain": jnp.clip(1.0 + 0.18 * jax.random.normal(splits[5], (D,), jnp.float32), 0.099609375, 1.8984375).astype(jnp.bfloat16),
        "head_gain": jnp.clip(1.0 + 0.18 * jax.random.normal(splits[6], (VAL,), jnp.float32), 0.099609375, 1.8984375).astype(jnp.bfloat16),
        "ffn_in": normal_values(splits[7], (D, 2 * FF), D ** -0.5, 0.125, ((0, 32),)),
        "ffn_out": normal_values(splits[8], (FF, D), FF ** -0.5, 0.078125, ((0, 32),)),
        "ffn_gain": jnp.clip(1.0 + 0.18 * jax.random.normal(splits[9], (D,), jnp.float32), 0.099609375, 1.8984375).astype(jnp.bfloat16),
        "out_grad": normal_values(splits[10], (SEQS, LEN, D), 1.0, 6.0, ((0, 4), (1, 8))),
        "seg_ids": jax.vmap(lambda own: jnp.searchsorted(jnp.cumsum(uneven(own, 8, LEN, LEN // 2, 2)), jnp.arange(LEN), side="right"))(jax.random.split(splits[11], SEQS)).reshape((SEQS, LEN)).astype(jnp.int32),
        "valid_mask": draw_valid_mask(jax.random.fold_in(splits[13], 71), 0),
    }


@jax.custom_vjp
def low(v):
    return lax.optimization_barrier(v.astype(jnp.bfloat16)).astype(jnp.float32)

@jax.custom_vjp
def low_back(v):
    return v

def low_keep(v):
    return (low(v), None)

def low_pass(kept, grad):
    return (grad,)

def back_keep(v):
    return (v, None)

def back_low(kept, grad):
    return (low(grad),)
low.defvjp(low_keep, low_pass)
low_back.defvjp(back_keep, back_low)
HIGHEST = lax.Precision.HIGHEST
epsilon = 1e-05
head_floor = 1.0

def matmul(left, right):
    return jnp.einsum('...d,de->...e', left, right, precision=HIGHEST)

def rms_norm(values, gain_in):
    return values * lax.rsqrt(lax.optimization_barrier(jnp.mean(values * values, axis=-1, keepdims=True)) + epsilon) * gain_in

def head_norm(values, gain_in):
    return values * lax.rsqrt(lax.optimization_barrier(jnp.mean(values * values, axis=-1, keepdims=True)) + head_floor) * gain_in

def span_masks(segments, seg_before):
    span_len = segments.shape[-1]
    positions = jnp.arange(span_len, dtype=jnp.int32)
    causal = positions[:, None] >= positions[None, :]
    same_seg = (segments[:, :, None] == segments[:, None, :]) & causal[None]
    enter_mask = segments == seg_before[:, None]
    carry_end = segments == segments[:, -1:]
    keep_all = segments[:, -1] == seg_before
    one = jnp.float32(1.0)
    zero = jnp.float32(0.0)
    return (jnp.where(same_seg, one, zero), jnp.where(enter_mask, one, zero), jnp.where(carry_end, one, zero), jnp.where(keep_all, one, zero))

def span_local(query_in, key_in, value_in, log_in, same_seg, carry_end, keep_all):
    span_len = log_in.shape[1]
    positions = jnp.arange(span_len, dtype=jnp.int32)
    triangle = jnp.where(positions[:, None] >= positions[None, :], jnp.float32(1.0), jnp.float32(0.0))
    summed = jnp.einsum('ij,njhk->nihk', triangle, log_in, precision=HIGHEST)
    last_sum = summed[:, -1]
    q_decay = query_in * jnp.exp(summed)
    k_decay = key_in * jnp.exp(-summed)
    k_final = key_in * jnp.exp(last_sum[:, None] - summed) * carry_end[:, :, None, None]
    scores = jnp.einsum('nihk,njhk->nhij', q_decay, k_decay, precision=HIGHEST) * same_seg[:, None]
    inner_out = jnp.einsum('nhij,njhv->nihv', scores, value_in, precision=HIGHEST)
    delta_state = jnp.einsum('nihk,nihv->nhkv', k_final, value_in, precision=HIGHEST)
    decay_rows = keep_all[:, None, None] * jnp.exp(last_sum)
    return (q_decay, inner_out, delta_state, decay_rows)

def gla_mixer(queries, key_rows, value_rows, log_decay, segments):
    seqs_all, length = segments.shape
    blocks = length // SPAN
    segments = segments.astype(jnp.int32)

    def to_blocks(array):
        return jnp.moveaxis(array.reshape((seqs_all, blocks, SPAN) + array.shape[2:]), 1, 0)
    span_ends = segments[:, SPAN - 1::SPAN].astype(jnp.int32)
    before = jnp.concatenate([jnp.full((seqs_all, 1), -1, jnp.int32), span_ends[:, :-1]], axis=1).astype(jnp.int32)

    @jax.checkpoint
    def advance(state, block_in):
        query_blk, key_blk, value_blk, log_blk, seg_blk, before_blk = block_in
        same_seg, enter_mask, carry_end, keep_all = span_masks(seg_blk, before_blk)
        q_decay, inner_out, delta_state, decay_rows = span_local(query_blk, key_blk, value_blk, log_blk, same_seg, carry_end, keep_all)
        outer_out = jnp.einsum('nihk,nhkv->nihv', q_decay, state, precision=HIGHEST) * enter_mask[:, :, None, None]
        return (decay_rows[..., None] * state + delta_state, inner_out + outer_out)
    zero_state = jnp.zeros((seqs_all, HEADS, KEY, VAL), jnp.float32)
    _, pieces = lax.scan(advance, zero_state, (to_blocks(queries), to_blocks(key_rows), to_blocks(value_rows), to_blocks(log_decay), to_blocks(segments), jnp.moveaxis(before, 1, 0)))
    return jnp.moveaxis(pieces, 0, 1).reshape(seqs_all, length, HEADS, VAL)

def block_layer(params, seg_ids, valid_mask):
    hidden_in, in_weight, out_weight, decay_up, decay_bias, mixer_gain, head_gain, ffn_in, ffn_out, ffn_gain = params
    seqs_all, length, model_width = hidden_in.shape
    qk_cols = HEADS * KEY
    v_cols = HEADS * VAL
    normed = low(rms_norm(hidden_in, mixer_gain))
    projected = low_back(matmul(normed, in_weight))
    queries = low(projected[..., :qk_cols])
    key_rows = low(projected[..., qk_cols:2 * qk_cols])
    value_rows = low(projected[..., 2 * qk_cols:2 * qk_cols + v_cols])
    out_gate = projected[..., 2 * qk_cols + v_cols:2 * qk_cols + 2 * v_cols]
    low_rank = low(projected[..., 2 * qk_cols + 2 * v_cols:])
    log_decay = jax.nn.log_sigmoid(matmul(low_rank, decay_up) + decay_bias) / 16.0
    shape_k = (seqs_all, length, HEADS, KEY)
    live_rows = valid_mask.astype(jnp.float32)[..., None]
    mixed_out = gla_mixer((queries * KEY ** (-0.5)).reshape(shape_k), (key_rows * live_rows).reshape(shape_k), value_rows.reshape(seqs_all, length, HEADS, VAL), log_decay.reshape(shape_k), seg_ids)
    gate_heads = out_gate.reshape(seqs_all, length, HEADS, VAL)
    head_normed = head_norm(mixed_out, head_gain) * gate_heads * jax.nn.sigmoid(gate_heads)
    gated_out = low(head_normed.reshape(seqs_all, length, v_cols))
    mix_out = low_back(matmul(gated_out, out_weight))
    middle = hidden_in + mix_out
    normed_two = low(rms_norm(middle, ffn_gain))
    gate_up = low_back(matmul(normed_two, ffn_in))
    hidden = low(jax.nn.silu(gate_up[..., :FF]) * gate_up[..., FF:])
    ffn_result = low_back(matmul(hidden, ffn_out))
    return (middle + ffn_result, (mix_out, ffn_result))

def reference(hidden_in, in_weight, out_weight, decay_up, decay_bias, mixer_gain, head_gain, ffn_in, ffn_out, ffn_gain, out_grad, seg_ids, valid_mask):
    params = tuple((array.astype(jnp.float32) for array in (hidden_in, in_weight, out_weight, decay_up, decay_bias, mixer_gain, head_gain, ffn_in, ffn_out, ffn_gain)))

    def forward(*inputs):
        return block_layer(inputs, seg_ids, valid_mask)
    result, pullback, extras = jax.vjp(forward, *params, has_aux=True)
    grads = pullback(out_grad.astype(jnp.float32))
    live_rows = valid_mask.astype(jnp.float32)[..., None]
    live_count = jnp.maximum(jnp.sum(valid_mask.astype(jnp.float32)), jnp.float32(1.0))

    def root_mean(values):
        return jnp.sqrt(jnp.sum(live_rows * values * values) / (live_count * values.shape[-1]))
    statistics = jnp.stack([root_mean(result), root_mean(extras[0]), root_mean(extras[1])])
    return (result.astype(jnp.bfloat16), grads[0], grads[1], grads[2], grads[3], grads[4], grads[5], grads[6], grads[7], grads[8], grads[9], statistics)
```

```python
import jax
import jax.numpy as jnp
from jax import lax
from jax.experimental import pallas as pl
from jax.experimental.pallas import tpu as pltpu
from jax.sharding import Mesh, PartitionSpec as P

HEADS = 4
KEY = 256
VAL = 512
SPAN = 64
RANK = 16
EPS = 1e-05
FLOOR = 1.0
QSCALE = KEY**-0.5

AXES = ("y", "c", "h", "p", "q")
COPIES = ("y", "c", "h")

bf16 = jnp.bfloat16
f32 = jnp.float32


def after(value, *deps):
    return lax.optimization_barrier((value, deps))[0]


def swap(value, axis):
    return lax.ppermute(value, axis, [(0, 1), (1, 0)])


def across(value, mask):
    return lax.ppermute(value, ("p", "q"), [(i, i ^ mask) for i in range(4)])


def gather_group(value):
    return [value] + [across(value, mask) for mask in (1, 2, 3)]


def scatter_group(parts):
    received = [across(parts[mask].astype(bf16), mask) for mask in (1, 2, 3)]
    return parts[0] + received[0].astype(f32) + received[1].astype(f32) + received[2].astype(f32)


def stack_axis(value, axis):
    if lax.axis_size(axis) != 2:
        return lax.all_gather(value, axis)
    other = swap(value, axis)
    first = lax.axis_index(axis) == 0
    return jnp.where(first, jnp.stack([value, other]), jnp.stack([other, value]))


def gather_all(value):
    for axis in AXES[::-1]:
        value = stack_axis(value, axis)
    return value


def sum_all(value):
    for axis in ("q", "p", "c", "h", "y"):
        if lax.axis_size(axis) == 2:
            value = value + swap(value, axis)
        else:
            value = lax.psum(value, axis)
    return value


def binary_copies():
    return all(lax.axis_size(axis) == 2 for axis in COPIES)


def join(first, one, two):
    return jnp.where(first, jnp.concatenate([one, two]), jnp.concatenate([two, one]))


def gather_copies(block, chain):
    if not binary_copies():
        return lax.all_gather(block, COPIES, axis=0, tiled=True), chain
    block = after(block, chain) if chain is not None else block
    from_h = swap(block, "h")
    from_y = swap(block, "y")
    from_hy = swap(from_h, "y")
    mine = [block, from_h, from_y, from_hy]
    core = [swap(part, "c") for part in mine]
    h0, c0, y0 = (lax.axis_index(axis) == 0 for axis in ("h", "c", "y"))
    near = join(c0, join(h0, mine[0], mine[1]), join(h0, core[0], core[1]))
    far = join(c0, join(h0, mine[2], mine[3]), join(h0, core[2], core[3]))
    return join(y0, near, far), from_h


def pick(value, index, axis):
    return lax.dynamic_index_in_dim(value, index, axis, keepdims=False)


def scatter_copies(grad, order=("c", "y", "h")):
    sizes = [lax.axis_size(axis) for axis in COPIES]
    rows = grad.shape[0] // (sizes[0] * sizes[1] * sizes[2])
    value = grad.reshape(*sizes, rows, grad.shape[1])
    left = list(COPIES)
    for axis in order:
        dim = left.index(axis)
        if lax.axis_size(axis) == 2:
            mine = lax.axis_index(axis)
            keep = pick(value, mine, dim).astype(f32)
            value = keep + swap(pick(value, 1 - mine, dim).astype(bf16), axis).astype(f32)
        else:
            value = lax.psum_scatter(value.astype(bf16), axis, scatter_dimension=dim).astype(f32)
        left.remove(axis)
    return value


def share_columns(weight, place, columns):
    pieces = [columns(weight, t) for t in range(4)]
    got = []
    for mask in range(4):
        piece = lax.select_n(place, *[pieces[t ^ mask] for t in range(4)])
        got.append(piece if mask == 0 else across(piece, mask))
    return jnp.concatenate(
        [lax.select_n(place, *[got[t ^ spot] for t in range(4)]) for spot in range(4)]
    )


def return_columns(grad, place):
    value = grad.reshape(4, grad.shape[0] // 4, grad.shape[1])
    got = [pick(value, place, 0)]
    for mask in (1, 2, 3):
        got.append(across(pick(value, place ^ mask, 0).astype(bf16), mask).astype(f32))
    return [lax.select_n(place, *[got[t ^ spot] for t in range(4)]) for spot in range(4)]


def row_owner_moves():
    total = 1
    for axis in AXES:
        total *= lax.axis_size(axis)
    copies = total // 4
    return [(g, (g % copies) * 4 + g // copies) for g in range(total)]


def dot_nn(a, b):
    return lax.dot_general(a, b, (((1,), (0,)), ((), ())), preferred_element_type=f32)


def dot_nt(a, b):
    return lax.dot_general(a, b, (((1,), (1,)), ((), ())), preferred_element_type=f32)


def dot_tn(a, b):
    return lax.dot_general(a, b, (((0,), (0,)), ((), ())), preferred_element_type=f32)


def two_parts(value):
    high = value.astype(bf16)
    return high, (value - high.astype(f32)).astype(bf16)


def triangle(lower):
    row = lax.broadcasted_iota(jnp.int32, (SPAN, SPAN), 0)
    col = lax.broadcasted_iota(jnp.int32, (SPAN, SPAN), 1)
    return jnp.where(row >= col if lower else row <= col, 1.0, 0.0)


def running_sum(value, lower):
    ones = triangle(lower).astype(bf16)
    high, low = two_parts(value)
    return dot_nn(ones, high) + dot_nn(ones, low)


def pair_mask(meta, rows):
    return jnp.where(meta[:, 0:1] == rows[0:1, :], triangle(True), 0.0)


def states_kernel(
    place, kvr, up, bias, meta, rows, sums, raw, prior, through, end, decay, state, total
):
    @pl.when(pl.program_id(0) == 0)
    def _():
        state[...] = jnp.zeros_like(state)
        total[...] = jnp.ones_like(total)

    keys = kvr[:, :KEY].astype(f32)
    gate = dot_nn(kvr[:, KEY + VAL :], up[...]) + bias[...]
    log_decay = (jnp.minimum(gate, 0.0) - jnp.log1p(jnp.exp(-jnp.abs(gate)))) * (1.0 / 16.0)
    run = running_sum(log_decay, True)
    raw[...] = gate
    sums[...] = run
    last = run[SPAN - 1 :, :]
    info = meta[...]
    k_final = (keys * jnp.exp(last - run) * (info[:, 1:2] * info[:, 3:4])).astype(bf16)
    step = rows[0, 1:2, 0:1] * jnp.exp(last)
    prior[0] = state[...].astype(bf16)
    through[0] = total[...]
    state[...] = step * state[...] + dot_tn(kvr[:, KEY : KEY + VAL], k_final)
    total[...] = step * total[...]
    end[...] = state[...].astype(bf16)
    decay[...] = total[...]


def mixed_kernel(place, kvr, qog, sums, prior, through, entering, gain, meta, rows, gated, mixed):
    info = meta[...]
    run = sums[...]
    query = qog[:, :KEY].astype(bf16).astype(f32)
    q_decay = (query * QSCALE * jnp.exp(run)).astype(bf16)
    k_decay = (kvr[:, :KEY].astype(f32) * info[:, 1:2] * jnp.exp(-run)).astype(bf16)
    scores = (dot_nt(q_decay, k_decay) * pair_mask(info, rows[0])).astype(bf16)
    state = (prior[0].astype(f32) + through[0] * entering[...].astype(f32)).astype(bf16)
    out = dot_nn(scores, kvr[:, KEY : KEY + VAL]) + info[:, 2:3] * dot_nt(q_decay, state)
    mixed[...] = out
    gate = qog[:, KEY:]
    scale = lax.rsqrt(jnp.mean(out * out, axis=-1, keepdims=True) + FLOOR)
    gated[...] = (out * scale * gain[...] * gate * jax.nn.sigmoid(gate)).astype(bf16)


def gate_grad_kernel(
    place,
    grad_gated,
    qog,
    mixed,
    sums,
    gain,
    meta,
    rows,
    grad_out,
    grad_gate,
    later,
    beyond,
    start,
    decay,
    grad_gain,
    state,
    total,
):
    @pl.when(pl.program_id(0) == 0)
    def _():
        state[...] = jnp.zeros_like(state)
        total[...] = jnp.ones_like(total)
        grad_gain[...] = jnp.zeros_like(grad_gain)

    info = meta[...]
    run = sums[...]
    out = mixed[...]
    gate = qog[:, KEY:]
    grad = grad_gated[...]
    sig = jax.nn.sigmoid(gate)
    scale = lax.rsqrt(jnp.mean(out * out, axis=-1, keepdims=True) + FLOOR)
    scaled = out * scale
    swish = gate * sig
    weighted = grad * gain[...] * swish
    inner = jnp.mean(scaled * weighted, axis=-1, keepdims=True)
    grad_o = (scale * (weighted - scaled * inner)).astype(bf16)
    grad_out[...] = grad_o
    grad_gate[...] = (grad * scaled * gain[...] * sig * (1.0 + gate * (1.0 - sig))).astype(bf16)
    grad_gain[...] += jnp.sum(grad * scaled * swish, axis=0, keepdims=True)
    query = qog[:, :KEY].astype(bf16).astype(f32)
    q_enter = (query * QSCALE * jnp.exp(run)).astype(bf16)
    o_enter = jnp.where(info[:, 2:3] > 0.0, grad_o.astype(f32), 0.0).astype(bf16)
    step = rows[0, 1:2, 0:1] * jnp.exp(run[SPAN - 1 :, :])
    later[0] = state[...].astype(bf16)
    beyond[0] = total[...]
    state[...] = step * state[...] + dot_tn(o_enter, q_enter)
    total[...] = step * total[...]
    start[...] = state[...].astype(bf16)
    decay[...] = total[...]


def inputs_grad_kernel(
    place,
    kvr,
    qog,
    sums,
    raw,
    grad_out,
    grad_gate,
    prior,
    through,
    entering,
    later,
    beyond,
    leaving,
    up,
    meta,
    rows,
    grad_kvr,
    grad_qog,
    grad_up,
    grad_bias,
):
    @pl.when(pl.program_id(0) == 0)
    def _():
        grad_up[...] = jnp.zeros_like(grad_up)
        grad_bias[...] = jnp.zeros_like(grad_bias)

    info = meta[...]
    run = sums[...]
    last = run[SPAN - 1 :, :]
    valid, enter, carry = info[:, 1:2], info[:, 2:3], info[:, 3:4]
    grow, shrink, tail = jnp.exp(run), jnp.exp(-run), jnp.exp(last - run) * carry
    query = qog[:, :KEY].astype(bf16).astype(f32)
    keys = kvr[:, :KEY].astype(f32) * valid
    values = kvr[:, KEY : KEY + VAL]
    q_decay = (query * QSCALE * grow).astype(bf16)
    k_decay = (keys * shrink).astype(bf16)
    k_final = (keys * tail).astype(bf16)
    mask = pair_mask(info, rows[0])
    state = prior[0].astype(f32) + through[0] * entering[...].astype(f32)
    state_grad = later[0].astype(f32) + beyond[0] * leaving[...].astype(f32)
    state_b, state_grad_b = state.astype(bf16), state_grad.astype(bf16)
    grad_o = grad_out[...]
    scores = (dot_nt(q_decay, k_decay) * mask).astype(bf16)
    grad_scores = (dot_nt(grad_o, values) * mask).astype(bf16)
    grad_v = dot_tn(scores, grad_o) + dot_nt(k_final, state_grad_b)
    grad_qd = dot_nn(grad_scores, k_decay) + enter * dot_nn(grad_o, state_b)
    grad_kd = dot_tn(grad_scores, q_decay)
    grad_kf = dot_nn(values, state_grad_b)
    step = rows[0, 1:2, 0:1] * jnp.exp(last)
    through_last = step * jnp.sum(state * state_grad, axis=0, keepdims=True)
    final_part = grad_kf * k_final.astype(f32)
    grad_run = grad_qd * q_decay.astype(f32) - grad_kd * k_decay.astype(f32) - final_part
    grad_last = through_last + jnp.sum(final_part, axis=0, keepdims=True)
    grad_log = running_sum(grad_run, False) + grad_last
    grad_raw = grad_log * jax.nn.sigmoid(-raw[...]) * (1.0 / 16.0)
    high, low = two_parts(grad_raw)
    rank = kvr[:, KEY + VAL :]
    grad_up[...] += dot_tn(rank, high) + dot_tn(rank, low)
    grad_bias[...] += jnp.sum(grad_raw, axis=0, keepdims=True)
    grad_rank = dot_nt(high, up[...]) + dot_nt(low, up[...])
    grad_k = (grad_kd * shrink + grad_kf * tail) * valid
    grad_kvr[:, :KEY] = grad_k.astype(bf16)
    grad_kvr[:, KEY : KEY + VAL] = grad_v.astype(bf16)
    grad_kvr[:, KEY + VAL :] = grad_rank.astype(bf16)
    grad_qog[:, :KEY] = (grad_qd * grow * QSCALE).astype(bf16)
    grad_qog[:, KEY:] = grad_gate[...]


class Mixer:
    def __init__(self, place, blocks, per_device):
        self.place = place.reshape(1)
        self.blocks = blocks
        self.per_device = per_device

    def call(self, kernel, specs, args, outs, scratch=(), reverse=False, flops=0):
        count, per_device = self.blocks, self.per_device

        def at(step):
            return count - 1 - step if reverse else step

        def spec(kind, shape):
            if kind == "rows":
                return pl.BlockSpec(
                    (SPAN, shape[1]),
                    lambda n, place: (
                        lax.bitwise_xor(at(n) // per_device, place[0]) * per_device
                        + at(n) % per_device,
                        0,
                    ),
                )
            if kind == "tokens":
                return pl.BlockSpec((SPAN, shape[1]), lambda n, place: (at(n), 0))
            if kind == "blocks":
                return pl.BlockSpec((1,) + shape[1:], lambda n, place: (at(n), 0, 0))
            return pl.BlockSpec(shape, lambda n, place: (0,) * len(shape))

        size = sum(a.size * a.dtype.itemsize for a in args)
        return pl.pallas_call(
            kernel,
            grid_spec=pltpu.PrefetchScalarGridSpec(
                num_scalar_prefetch=1,
                grid=(count,),
                in_specs=[spec(kind, a.shape) for kind, a in zip(specs, args)],
                out_specs=[spec(kind, shape) for kind, shape, _ in outs],
                scratch_shapes=list(scratch),
            ),
            out_shape=[jax.ShapeDtypeStruct(shape, kind) for _, shape, kind in outs],
            compiler_params=pltpu.CompilerParams(
                dimension_semantics=("arbitrary",), vmem_limit_bytes=48 * 1024 * 1024
            ),
            cost_estimate=pl.CostEstimate(
                flops=flops, bytes_accessed=2 * size, transcendentals=4 * SPAN * KEY * count
            ),
        )(self.place, *args)


def normed(values, gain):
    return values * lax.rsqrt(jnp.mean(values * values, axis=-1, keepdims=True) + EPS) * gain


def normed_grad(values, gain, grad):
    scale = lax.rsqrt(jnp.mean(values * values, axis=-1, keepdims=True) + EPS)
    weighted = grad * gain
    inner = jnp.mean(weighted * values, axis=-1, keepdims=True)
    return (
        scale * weighted - scale * scale * scale * values * inner,
        jnp.sum(grad * values * scale, axis=0),
    )


def mm(left, right, out=f32):
    return jnp.dot(left, right, preferred_element_type=f32).astype(out)


def mm_tn(left, right, out=f32):
    return dot_tn(left, right).astype(out)


def kvr_columns(weight, t):
    wide = HEADS * KEY
    return jnp.concatenate(
        [
            weight[:, wide + t * KEY : wide + (t + 1) * KEY],
            weight[:, 2 * wide + t * VAL : 2 * wide + (t + 1) * VAL],
            weight[:, 2 * wide + 2 * HEADS * VAL :],
        ],
        axis=1,
    )


def qog_columns(weight, t):
    start = 2 * HEADS * KEY + HEADS * VAL
    return jnp.concatenate(
        [
            weight[:, t * KEY : (t + 1) * KEY],
            weight[:, start + t * VAL : start + (t + 1) * VAL],
        ],
        axis=1,
    )


def from_earlier(end, decay):
    count = lax.axis_size("h")
    if count == 2:
        return lax.ppermute(end, "h", [(0, 1)])
    ends, decays = lax.all_gather(end, "h"), lax.all_gather(decay, "h")
    mine = lax.axis_index("h")
    state = jnp.zeros(end.shape, f32)
    for h in range(count - 1):
        state = jnp.where(h < mine, decays[h] * state + ends[h].astype(f32), state)
    return state.astype(bf16)


def from_later(start, decay):
    count = lax.axis_size("h")
    if count == 2:
        return lax.ppermute(start, "h", [(1, 0)])
    starts, decays = lax.all_gather(start, "h"), lax.all_gather(decay, "h")
    mine = lax.axis_index("h")
    state = jnp.zeros(start.shape, f32)
    for h in range(count - 1, 0, -1):
        state = jnp.where(h > mine, decays[h] * state + starts[h].astype(f32), state)
    return state.astype(bf16)


def local(
    hidden_in,
    in_weight,
    out_weight,
    decay_up,
    decay_bias,
    mixer_gain,
    head_gain,
    ffn_in,
    ffn_out,
    ffn_gain,
    out_grad,
    seg_ids,
    valid_mask,
):
    tokens, width = hidden_in.shape[1:]
    place = 2 * lax.axis_index("p") + lax.axis_index("q")
    half = lax.axis_index("h")
    sizes = [lax.axis_size(axis) for axis in AXES]
    devices = sizes[0] * sizes[1] * sizes[2] * 4
    me = place
    stride = 4
    for axis in ("h", "c", "y"):
        me = me + stride * lax.axis_index(axis)
        stride *= lax.axis_size(axis)
    ff = ffn_in.shape[1] // 2
    quarter = ff // 4
    rows_all = 4 * tokens
    count = rows_all // SPAN
    x_own = hidden_in.reshape(tokens, width)
    dy_own = out_grad.reshape(tokens, width)

    small = [
        decay_up.reshape(-1),
        decay_bias,
        mixer_gain,
        head_gain,
        ffn_gain,
        seg_ids.reshape(-1).astype(bf16),
        valid_mask.reshape(-1).astype(bf16),
    ]
    lengths = [part.shape[0] for part in small]
    packed = jnp.concatenate(small)
    padded = -(-packed.shape[0] // 1024) * 1024
    packed = jnp.pad(packed, (0, padded - packed.shape[0])).reshape(-1, 128)
    everyone = gather_all(packed).reshape(sizes[0], sizes[1], -1, padded)
    offset = [sum(lengths[:i]) for i in range(len(lengths) + 1)]

    def small_part(i):
        return everyone[..., offset[i] : offset[i + 1]]

    up_cols = decay_up.shape[1]
    up_all = small_part(0).reshape(devices, RANK, up_cols).transpose(1, 0, 2).reshape(RANK, HEADS, KEY)
    up_head = pick(up_all, place, 1)
    bias_head = pick(small_part(1).reshape(HEADS, 1, KEY), place, 0).astype(f32)
    gain_one = small_part(2).reshape(-1).astype(f32)
    gain_head = small_part(3).reshape(1, -1).astype(f32)
    gain_two = small_part(4).reshape(-1).astype(f32)

    def of_sequence(value):
        return pick(pick(value, lax.axis_index("y"), 0), lax.axis_index("c"), 0).reshape(-1)

    seg_all = of_sequence(small_part(5)).astype(f32)
    valid_all = of_sequence(small_part(6)).astype(f32)
    valid_count = jnp.sum(small_part(6).astype(f32))
    seg_here = lax.dynamic_slice(
        jnp.concatenate([jnp.full((1,), -1.0, f32), seg_all]), (half * rows_all,), (rows_all + 1,)
    )
    valid_here = lax.dynamic_slice(valid_all, (half * rows_all,), (rows_all,))
    seg_blocks = seg_here[1:].reshape(count, SPAN)
    before = seg_here[:-1].reshape(count, SPAN)[:, :1]
    final = seg_blocks[:, -1:]
    meta = jnp.stack(
        [
            seg_here[1:],
            valid_here,
            (seg_blocks == before).astype(f32).reshape(-1),
            (seg_blocks == final).astype(f32).reshape(-1),
        ]
        + [jnp.zeros((rows_all,), f32)] * 4,
        axis=1,
    )
    keep = jnp.broadcast_to((final == before).astype(f32), (count, SPAN))
    rows = jnp.stack([seg_blocks, keep] + [jnp.zeros((count, SPAN), f32)] * 6, axis=1)

    kvr_rows = share_columns(in_weight, place, kvr_columns)
    qog_rows = share_columns(in_weight, place, qog_columns)
    w_kvr, chain = gather_copies(kvr_rows, None)
    w_qog, chain = gather_copies(qog_rows, chain)
    x_group = jnp.concatenate(gather_group(after(x_own, qog_rows)))
    moves = row_owner_moves()
    back = [(b, a) for a, b in moves]
    w_out, chain = gather_copies(lax.ppermute(out_weight, AXES, moves), chain)
    dy_group = jnp.concatenate(gather_group(after(dy_own, x_group)))
    ffn_late = after(ffn_in, x_group)
    gate_rows = share_columns(ffn_late, place, lambda w, t: w[:, t * quarter : (t + 1) * quarter])
    up_rows = share_columns(
        ffn_late, place, lambda w, t: w[:, ff + t * quarter : ff + (t + 1) * quarter]
    )
    down_rows = lax.ppermute(ffn_out, AXES, moves)
    w_down, chain = gather_copies(down_rows, chain)
    w_gate, chain = gather_copies(gate_rows, chain)
    w_up, chain = gather_copies(up_rows, chain)

    n1 = normed(x_group.astype(f32), gain_one).astype(bf16)
    kvr = mm(n1, w_kvr, bf16)
    mixer = Mixer(place, count, tokens // SPAN)
    state_shape = (VAL, KEY)
    scratch = [pltpu.VMEM(state_shape, f32), pltpu.VMEM((1, KEY), f32)]
    sums, raw, prior, through, end, decay = mixer.call(
        states_kernel,
        ["rows", "whole", "whole", "tokens", "blocks"],
        [kvr, up_head, bias_head, meta, rows],
        [
            ("rows", (rows_all, KEY), f32),
            ("rows", (rows_all, KEY), f32),
            ("blocks", (count,) + state_shape, bf16),
            ("blocks", (count, 1, KEY), f32),
            ("whole", state_shape, bf16),
            ("whole", (1, KEY), f32),
        ],
        scratch,
        flops=2 * rows_all * KEY * VAL,
    )
    entering = from_earlier(end, decay)
    qog = mm(n1, w_qog)
    gated, mixed = mixer.call(
        mixed_kernel,
        ["rows", "rows", "rows", "blocks", "blocks", "whole", "whole", "tokens", "blocks"],
        [kvr, qog, sums, prior, through, entering, gain_head, meta, rows],
        [("rows", (rows_all, VAL), bf16), ("rows", (rows_all, VAL), f32)],
        flops=2 * rows_all * (KEY * VAL + SPAN * (KEY + VAL)),
    )
    mix_parts = mm(gated, w_out).reshape(4, tokens, width)
    mix = scatter_group([mix_parts[m] for m in range(4)])
    h1 = x_own.astype(f32) + mix

    grad_hidden = mm_nt(dy_group, w_down)
    n2 = normed(h1, gain_two).astype(bf16)
    n2_group = jnp.concatenate(gather_group(n2))
    gate = mm(n2_group, w_gate)
    up = mm(n2_group, w_up)
    sig = jax.nn.sigmoid(gate)
    hidden = (gate * sig * up).astype(bf16)
    y_parts = mm(hidden, w_down).reshape(4, tokens, width)
    grad_g = (grad_hidden * up * sig * (1.0 + gate * (1.0 - sig))).astype(bf16)
    grad_u = (grad_hidden * gate * sig).astype(bf16)
    n2_grad_parts = (mm_nt(grad_g, w_gate) + mm_nt(grad_u, w_up)).reshape(4, tokens, width)
    n2_grad = scatter_group([n2_grad_parts[m] for m in range(4)])
    h1_grad_part, gain_two_grad = normed_grad(h1, gain_two, n2_grad)
    h1_grad = dy_own.astype(f32) + h1_grad_part
    mix_grad = jnp.concatenate(gather_group(h1_grad.astype(bf16)))

    down_grad = mm_tn(hidden, dy_group, bf16)
    gate_w_grad = mm_tn(n2_group, grad_g, bf16)
    up_w_grad = mm_tn(n2_group, grad_u, bf16)
    down_sum = scatter_copies(down_grad)
    gate_sum = scatter_copies(gate_w_grad)
    up_sum = scatter_copies(up_w_grad, ("c", "h", "y"))
    ffnout_grad = lax.ppermute(down_sum.astype(bf16), AXES, back).astype(f32)
    ffnin_grad = jnp.concatenate(return_columns(gate_sum, place) + return_columns(up_sum, place), axis=1)

    grad_gated = mm_nt(mix_grad, w_out)
    grad_o, grad_gate, later, beyond, start, decay_b, head_grad = mixer.call(
        gate_grad_kernel,
        ["rows", "rows", "rows", "rows", "whole", "tokens", "blocks"],
        [grad_gated, qog, mixed, sums, gain_head, meta, rows],
        [
            ("rows", (rows_all, VAL), bf16),
            ("rows", (rows_all, VAL), bf16),
            ("blocks", (count,) + state_shape, bf16),
            ("blocks", (count, 1, KEY), f32),
            ("whole", state_shape, bf16),
            ("whole", (1, KEY), f32),
            ("whole", (1, VAL), f32),
        ],
        scratch,
        reverse=True,
        flops=2 * rows_all * KEY * VAL,
    )
    leaving = from_later(start, decay_b)
    out_w_grad = mm_tn(gated, mix_grad, bf16)
    outproj_grad = lax.ppermute(scatter_copies(out_w_grad).astype(bf16), AXES, back).astype(f32)

    y = scatter_group([after(y_parts[m], mix_grad) for m in range(4)])
    result = h1 + y
    block_out = result.astype(bf16).reshape(1, tokens, width)
    live = valid_mask.reshape(tokens, 1).astype(f32)
    squares = jnp.stack(
        [jnp.sum(live * result * result), jnp.sum(live * mix * mix), jnp.sum(live * y * y)]
    )

    grad_kvr, grad_qog, up_grad, bias_grad = mixer.call(
        inputs_grad_kernel,
        ["rows"] * 6 + ["blocks", "blocks", "whole", "blocks", "blocks", "whole", "whole", "tokens", "blocks"],
        [
            kvr,
            qog,
            sums,
            raw,
            grad_o,
            grad_gate,
            prior,
            through,
            entering,
            later,
            beyond,
            leaving,
            up_head,
            meta,
            rows,
        ],
        [
            ("rows", kvr.shape, bf16),
            ("rows", qog.shape, bf16),
            ("whole", (RANK, KEY), f32),
            ("whole", (1, KEY), f32),
        ],
        flops=2 * rows_all * (3 * KEY * VAL + SPAN * (3 * KEY + 2 * VAL)),
    )
    n1_grad_parts = (mm_nt(grad_kvr, w_kvr) + mm_nt(grad_qog, w_qog)).reshape(4, tokens, width)
    n1_grad = scatter_group([n1_grad_parts[m] for m in range(4)])
    input_part, gain_one_grad = normed_grad(x_own.astype(f32), gain_one, n1_grad)
    input_grad = (h1_grad + input_part).reshape(1, tokens, width)
    kvr_sum = scatter_copies(mm_tn(n1, grad_kvr, bf16))
    qog_sum = scatter_copies(mm_tn(n1, grad_qog, bf16), ("c", "h", "y"))
    kvr_back = return_columns(kvr_sum, place)
    qog_back = return_columns(qog_sum, place)
    inproj_grad = jnp.concatenate(
        [part[:, :KEY] for part in qog_back]
        + [part[:, :KEY] for part in kvr_back]
        + [part[:, KEY : KEY + VAL] for part in kvr_back]
        + [part[:, KEY:] for part in qog_back]
        + [sum(part[:, KEY + VAL :] for part in kvr_back)],
        axis=1,
    )

    head_slot = (lax.broadcasted_iota(jnp.int32, (HEADS, 1, 1), 0) == place).astype(f32)
    decay_part = head_slot * jnp.concatenate([up_grad, bias_grad], axis=0)[None]
    early = [squares, head_grad.reshape(-1), gain_two_grad, decay_part.reshape(-1)]
    total = jnp.concatenate(early)
    short = -total.shape[0] % 1024
    total = sum_all(jnp.pad(total, (0, short)).reshape(-1, 128)).reshape(-1)
    gain_one_sum = sum_all(gain_one_grad.reshape(-1, 128)).reshape(-1)
    ends = [0]
    for part in early:
        ends.append(ends[-1] + part.shape[0])
    squares = total[: ends[1]]
    root_means = jnp.sqrt(squares / (jnp.maximum(valid_count, 1.0) * width))

    def own(value, length):
        return lax.dynamic_slice(value, (me * length,), (length,))

    headgain_grad = own(total[ends[1] : ends[2]], head_gain.shape[0])
    ffngain_grad = own(total[ends[2] : ends[3]], ffn_gain.shape[0])
    mixgain_grad = own(gain_one_sum, mixer_gain.shape[0])
    decay_all = total[ends[3] : ends[4]].reshape(HEADS, RANK + 1, KEY)
    decay_all = decay_all.transpose(1, 0, 2).reshape(RANK + 1, HEADS * KEY)
    decay_own = lax.dynamic_slice(decay_all, (0, me * up_cols), (RANK + 1, up_cols))
    return (
        block_out,
        input_grad,
        inproj_grad,
        outproj_grad,
        decay_own[:RANK],
        decay_own[RANK],
        mixgain_grad,
        headgain_grad,
        ffnin_grad,
        ffnout_grad,
        ffngain_grad,
        root_means,
    )


def mm_nt(left, right, out=f32):
    return dot_nt(left, right).astype(out)


def solution(mesh):
    dp, seq = mesh.shape["dp"], mesh.shape["seq"]
    fine = Mesh(mesh.devices.reshape(dp // 2, 2, seq // 4, 2, 2), AXES)
    batch, spread, whole = ("y", "c"), ("h", "p", "q"), AXES
    placed = (
        P(batch, spread, None),
        P(whole, None),
        P(whole, None),
        P(None, whole),
        P(whole),
        P(whole),
        P(whole),
        P(whole, None),
        P(whole, None),
        P(whole),
        P(batch, spread, None),
        P(batch, spread),
        P(batch, spread),
    )
    return jax.shard_map(
        local,
        mesh=fine,
        in_specs=placed,
        out_specs=(
            P(batch, spread, None),
            P(batch, spread, None),
            P(whole, None),
            P(whole, None),
            P(None, whole),
            P(whole),
            P(whole),
            P(whole),
            P(whole, None),
            P(whole, None),
            P(whole),
            P(),
        ),
        check_vma=False,
    )
```

```python
import jax
import jax.numpy as jnp
from jax import lax
from jax.experimental import pallas as pl
from jax.experimental.pallas import tpu as pltpu
from jax.sharding import Mesh, PartitionSpec as P

HEADS = 4
KEY = 256
VAL = 512
SPAN = 64
RANK = 16
LANES = 128
EPS = 1e-05
FLOOR = 1.0
QSCALE = KEY**-0.5
KEYS, VALUES, GATES, RANKS = KEY, 2 * KEY, 2 * KEY + VAL, 2 * KEY + 2 * VAL

AXES = ("y", "c", "h", "p", "q")
COPIES = ("y", "c", "h")

bf16 = jnp.bfloat16
f32 = jnp.float32


def after(value, *deps):
    return lax.optimization_barrier((value, deps))[0]


def together(*values):
    return lax.optimization_barrier(values)


def swap(value, axis):
    return lax.ppermute(value, axis, [(0, 1), (1, 0)])


def across(value, mask):
    return lax.ppermute(value, ("p", "q"), [(i, i ^ mask) for i in range(4)])


def gather_group(value):
    return [value] + [across(value, mask) for mask in (1, 2, 3)]


def scatter_group(parts):
    received = [across(parts[mask].astype(bf16), mask) for mask in (1, 2, 3)]
    return parts[0] + received[0].astype(f32) + received[1].astype(f32) + received[2].astype(f32)


def stack_axis(value, axis):
    if lax.axis_size(axis) != 2:
        return lax.all_gather(value, axis)
    other = swap(value, axis)
    first = lax.axis_index(axis) == 0
    return jnp.where(first, jnp.stack([value, other]), jnp.stack([other, value]))


def sum_all(value):
    for axis in ("q", "p", "c", "y", "h"):
        if lax.axis_size(axis) == 2:
            value = value + swap(value, axis)
        else:
            value = lax.psum(value, axis)
    return value


def binary_copies():
    return all(lax.axis_size(axis) == 2 for axis in COPIES)


def half_swap(block):
    return swap(block, "h") if binary_copies() else block


def near_copies(block):
    return (swap(block, "y"), swap(block, "c")) if binary_copies() else (block, block)


def core_swap(block):
    return swap(block, "c") if binary_copies() else block


def lay_kernel(count, slots, *refs):
    blocks, whole, sems = refs[:count], refs[count], refs[count + 1]
    copies = [
        pltpu.make_async_copy(blocks[i], whole.at[slots[i]], sems.at[i]) for i in range(count)
    ]
    for copy in copies:
        copy.start()
    for copy in copies:
        copy.wait()


def lay(blocks, slots):
    count, (rows, cols), kind = len(blocks), blocks[0].shape, blocks[0].dtype
    size = count * rows * cols * kind.itemsize
    whole = pl.pallas_call(
        lambda *refs: lay_kernel(count, *refs),
        grid_spec=pltpu.PrefetchScalarGridSpec(
            num_scalar_prefetch=1,
            grid=(1,),
            in_specs=[pl.BlockSpec(memory_space=pl.ANY)] * count,
            out_specs=pl.BlockSpec(memory_space=pl.ANY),
            scratch_shapes=[pltpu.SemaphoreType.DMA((count,))],
        ),
        out_shape=jax.ShapeDtypeStruct((count, rows, cols), kind),
        compiler_params=pltpu.CompilerParams(vmem_limit_bytes=16 * 1024 * 1024),
        cost_estimate=pl.CostEstimate(flops=0, bytes_accessed=2 * size, transcendentals=0),
    )(jnp.stack(slots).astype(jnp.int32), *blocks)
    return whole.reshape(count * rows, cols)


def in_order(blocks):
    return lay(blocks, [jnp.int32(i) for i in range(len(blocks))])


def all_copies(block, parts, tall=False):
    if not binary_copies():
        return lax.all_gather(block, COPIES, axis=0, tiled=True)
    h, c, y = (lax.axis_index(axis) for axis in ("h", "c", "y"))
    flips = [(0, 0, 0), (1, 0, 0), (0, 1, 0), (1, 1, 0), (0, 0, 1), (1, 0, 1), (0, 1, 1), (1, 1, 1)]
    slots = []
    for fy, fc, fh in flips:
        ty, tc, th = y ^ fy, c ^ fc, h ^ fh
        slots.append(th * 4 + ty * 2 + tc if tall else ty * 4 + tc * 2 + th)
    return lay((block,) + tuple(parts), slots)


def pick(value, index, axis):
    return lax.dynamic_index_in_dim(value, index, axis, keepdims=False)


def copies_part(value, y, tall):
    ys, hs = lax.axis_size("y"), lax.axis_size("h")
    c = lax.axis_index("c")
    rows, cols = value.shape
    if tall and binary_copies():
        return pick(pick(value.reshape(hs, ys, 2, -1, cols), y, 1), c, 1)
    part = rows // (2 * ys)
    return lax.dynamic_slice_in_dim(value, (y * 2 + c) * part, part, 0).reshape(hs, -1, cols)


class Summing:
    def __init__(self, grad, tall=False):
        self.grad, self.tall = grad, tall
        self.from_c = swap(grad, "c")

    def of(self, y):
        one = copies_part(self.grad, y, self.tall).astype(f32)
        return one + copies_part(self.from_c, y, self.tall).astype(f32)

    def send_y(self):
        mine = lax.axis_index("y")
        if lax.axis_size("y") == 2:
            self.from_y = swap(self.of(1 - mine).astype(bf16), "y")
        else:
            parts = jnp.stack([self.of(y) for y in range(lax.axis_size("y"))])
            self.from_y = lax.psum_scatter(parts.astype(bf16), "y", scatter_dimension=0)

    def near(self):
        if lax.axis_size("y") == 2:
            return self.of(lax.axis_index("y")) + self.from_y.astype(f32)
        return self.from_y.astype(f32)

    def send_h(self):
        mine = lax.axis_index("h")
        if lax.axis_size("h") == 2:
            self.from_h = swap(pick(self.near(), 1 - mine, 0).astype(bf16), "h")
        else:
            self.from_h = lax.psum_scatter(self.near().astype(bf16), "h", scatter_dimension=0)

    def total(self):
        if lax.axis_size("h") == 2:
            return pick(self.near(), lax.axis_index("h"), 0) + self.from_h.astype(f32)
        return self.from_h.astype(f32)


def share_columns(weight, place, columns):
    pieces = [columns(weight, t) for t in range(4)]
    got = []
    for mask in range(4):
        piece = lax.select_n(place, *[pieces[t ^ mask] for t in range(4)])
        got.append(piece if mask == 0 else across(piece, mask))
    return jnp.concatenate(
        [lax.select_n(place, *[got[t ^ spot] for t in range(4)]) for spot in range(4)]
    )


def return_columns(grad, place):
    value = grad.reshape(4, grad.shape[0] // 4, grad.shape[1])
    got = [pick(value, place, 0).astype(f32)]
    for mask in (1, 2, 3):
        got.append(across(pick(value, place ^ mask, 0).astype(bf16), mask).astype(f32))
    return [lax.select_n(place, *[got[t ^ spot] for t in range(4)]) for spot in range(4)]


def reduce_copies(grad):
    return lax.psum_scatter(grad, COPIES, scatter_dimension=0, tiled=True)


def reduce_tall(grad):
    axes = ("h", "y", "c") if binary_copies() else COPIES
    return lax.psum_scatter(grad, axes, scatter_dimension=0, tiled=True)


def row_owner_moves():
    total = 1
    for axis in AXES:
        total *= lax.axis_size(axis)
    if binary_copies():
        pairs = []
        for g in range(total):
            yc, h, pq = g // 8, g // 4 % 2, g % 4
            pairs.append((g, pq * 8 + h * 4 + yc))
        return pairs
    copies = total // 4
    return [(g, (g % copies) * 4 + g // copies) for g in range(total)]


def dot_nn(a, b):
    return lax.dot_general(a, b, (((1,), (0,)), ((), ())), preferred_element_type=f32)


def dot_nt(a, b):
    return lax.dot_general(a, b, (((1,), (1,)), ((), ())), preferred_element_type=f32)


def dot_tn(a, b):
    return lax.dot_general(a, b, (((0,), (0,)), ((), ())), preferred_element_type=f32)


def two_parts(value):
    high = value.astype(bf16)
    return high, (value - high.astype(f32)).astype(bf16)


def triangle(lower):
    row = lax.broadcasted_iota(jnp.int32, (SPAN, SPAN), 0)
    col = lax.broadcasted_iota(jnp.int32, (SPAN, SPAN), 1)
    return jnp.where(row >= col if lower else row <= col, 1.0, 0.0)


def running_sum(value, lower):
    ones = triangle(lower).astype(bf16)
    high, low = two_parts(value)
    return dot_nn(ones, high) + dot_nn(ones, low)


def pair_mask(meta, rows):
    return jnp.where(meta[:, 0:1] == rows[0:1, :], triangle(True), 0.0)


def states_kernel(
    place, proj, up, bias, meta, rows, sums, raw, prior, through, end, decay, state, total
):
    @pl.when(pl.program_id(0) == 0)
    def _():
        state[...] = jnp.zeros_like(state)
        total[...] = jnp.ones_like(total)

    keys = proj[:, KEYS:VALUES].astype(bf16).astype(f32)
    gate = dot_nn(proj[:, RANKS:].astype(bf16), up[...]) + bias[...]
    log_decay = (jnp.minimum(gate, 0.0) - jnp.log1p(jnp.exp(-jnp.abs(gate)))) * (1.0 / 16.0)
    run = running_sum(log_decay, True)
    raw[...] = gate
    sums[...] = run
    last = run[SPAN - 1 :, :]
    info = meta[...]
    k_final = (keys * jnp.exp(last - run) * (info[:, 1:2] * info[:, 3:4])).astype(bf16)
    step = rows[0, 1:2, 0:1] * jnp.exp(last)
    prior[0] = state[...].astype(bf16)
    through[0] = total[...]
    state[...] = step * state[...] + dot_tn(proj[:, VALUES:GATES].astype(bf16), k_final)
    total[...] = step * total[...]
    end[...] = state[...].astype(bf16)
    decay[...] = total[...]


def mixed_kernel(place, proj, sums, prior, through, entering, gain, meta, rows, gated, mixed):
    info = meta[...]
    run = sums[...]
    query = proj[:, :KEYS].astype(bf16).astype(f32)
    q_decay = (query * QSCALE * jnp.exp(run)).astype(bf16)
    k_decay = (proj[:, KEYS:VALUES].astype(bf16).astype(f32) * info[:, 1:2] * jnp.exp(-run)).astype(bf16)
    scores = (dot_nt(q_decay, k_decay) * pair_mask(info, rows[0])).astype(bf16)
    state = (prior[0].astype(f32) + through[0] * entering[...].astype(f32)).astype(bf16)
    out = dot_nn(scores, proj[:, VALUES:GATES].astype(bf16)) + info[:, 2:3] * dot_nt(q_decay, state)
    mixed[...] = out
    gate = proj[:, GATES:RANKS]
    scale = lax.rsqrt(jnp.mean(out * out, axis=-1, keepdims=True) + FLOOR)
    gated[...] = (out * scale * gain[...] * gate * jax.nn.sigmoid(gate)).astype(bf16)


def gate_grad_kernel(
    place,
    grad_gated,
    proj,
    mixed,
    sums,
    gain,
    meta,
    rows,
    grad_out,
    grad_gate,
    later,
    beyond,
    start,
    decay,
    grad_gain,
    state,
    total,
):
    @pl.when(pl.program_id(0) == 0)
    def _():
        state[...] = jnp.zeros_like(state)
        total[...] = jnp.ones_like(total)
        grad_gain[...] = jnp.zeros_like(grad_gain)

    info = meta[...]
    run = sums[...]
    out = mixed[...]
    gate = proj[:, GATES:RANKS]
    grad = grad_gated[...]
    sig = jax.nn.sigmoid(gate)
    scale = lax.rsqrt(jnp.mean(out * out, axis=-1, keepdims=True) + FLOOR)
    scaled = out * scale
    swish = gate * sig
    weighted = grad * gain[...] * swish
    inner = jnp.mean(scaled * weighted, axis=-1, keepdims=True)
    grad_o = (scale * (weighted - scaled * inner)).astype(bf16)
    grad_out[...] = grad_o
    grad_gate[...] = (grad * scaled * gain[...] * sig * (1.0 + gate * (1.0 - sig))).astype(bf16)
    grad_gain[...] += jnp.sum(grad * scaled * swish, axis=0, keepdims=True)
    query = proj[:, :KEYS].astype(bf16).astype(f32)
    q_enter = (query * QSCALE * jnp.exp(run)).astype(bf16)
    o_enter = jnp.where(info[:, 2:3] > 0.0, grad_o.astype(f32), 0.0).astype(bf16)
    step = rows[0, 1:2, 0:1] * jnp.exp(run[SPAN - 1 :, :])
    later[0] = state[...].astype(bf16)
    beyond[0] = total[...]
    state[...] = step * state[...] + dot_tn(o_enter, q_enter)
    total[...] = step * total[...]
    start[...] = state[...].astype(bf16)
    decay[...] = total[...]


def inputs_grad_kernel(
    place,
    proj,
    sums,
    raw,
    grad_out,
    grad_gate,
    prior,
    through,
    entering,
    later,
    beyond,
    leaving,
    up,
    meta,
    rows,
    grad_proj,
    grad_up,
    grad_bias,
):
    @pl.when(pl.program_id(0) == 0)
    def _():
        grad_up[...] = jnp.zeros_like(grad_up)
        grad_bias[...] = jnp.zeros_like(grad_bias)

    info = meta[...]
    run = sums[...]
    last = run[SPAN - 1 :, :]
    valid, enter, carry = info[:, 1:2], info[:, 2:3], info[:, 3:4]
    grow, shrink, tail = jnp.exp(run), jnp.exp(-run), jnp.exp(last - run) * carry
    query = proj[:, :KEYS].astype(bf16).astype(f32)
    keys = proj[:, KEYS:VALUES].astype(bf16).astype(f32) * valid
    values = proj[:, VALUES:GATES].astype(bf16)
    q_decay = (query * QSCALE * grow).astype(bf16)
    k_decay = (keys * shrink).astype(bf16)
    k_final = (keys * tail).astype(bf16)
    mask = pair_mask(info, rows[0])
    state = prior[0].astype(f32) + through[0] * entering[...].astype(f32)
    state_grad = later[0].astype(f32) + beyond[0] * leaving[...].astype(f32)
    state_b, state_grad_b = state.astype(bf16), state_grad.astype(bf16)
    grad_o = grad_out[...]
    scores = (dot_nt(q_decay, k_decay) * mask).astype(bf16)
    grad_scores = (dot_nt(grad_o, values) * mask).astype(bf16)
    grad_v = dot_tn(scores, grad_o) + dot_nt(k_final, state_grad_b)
    grad_qd = dot_nn(grad_scores, k_decay) + enter * dot_nn(grad_o, state_b)
    grad_kd = dot_tn(grad_scores, q_decay)
    grad_kf = dot_nn(values, state_grad_b)
    step = rows[0, 1:2, 0:1] * jnp.exp(last)
    through_last = step * jnp.sum(state * state_grad, axis=0, keepdims=True)
    final_part = grad_kf * k_final.astype(f32)
    grad_run = grad_qd * q_decay.astype(f32) - grad_kd * k_decay.astype(f32) - final_part
    grad_last = through_last + jnp.sum(final_part, axis=0, keepdims=True)
    grad_log = running_sum(grad_run, False) + grad_last
    grad_raw = grad_log * jax.nn.sigmoid(-raw[...]) * (1.0 / 16.0)
    high, low = two_parts(grad_raw)
    rank = proj[:, RANKS:].astype(bf16)
    grad_up[...] += dot_tn(rank, high) + dot_tn(rank, low)
    grad_bias[...] += jnp.sum(grad_raw, axis=0, keepdims=True)
    grad_rank = dot_nt(high, up[...]) + dot_nt(low, up[...])
    grad_k = (grad_kd * shrink + grad_kf * tail) * valid
    grad_proj[:, KEYS:VALUES] = grad_k.astype(bf16)
    grad_proj[:, VALUES:GATES] = grad_v.astype(bf16)
    grad_proj[:, RANKS:] = grad_rank.astype(bf16)
    grad_proj[:, :KEYS] = (grad_qd * grow * QSCALE).astype(bf16)
    grad_proj[:, GATES:RANKS] = grad_gate[...]


class Mixer:
    def __init__(self, place, blocks, per_device):
        self.place = place.reshape(1)
        self.blocks = blocks
        self.per_device = per_device

    def call(self, kernel, specs, args, outs, scratch=(), reverse=False, flops=0):
        count, per_device = self.blocks, self.per_device

        def at(step):
            return count - 1 - step if reverse else step

        def spec(kind, shape):
            if kind == "rows":
                return pl.BlockSpec(
                    (SPAN, shape[1]),
                    lambda n, place: (
                        lax.bitwise_xor(at(n) // per_device, place[0]) * per_device
                        + at(n) % per_device,
                        0,
                    ),
                )
            if kind == "tokens":
                return pl.BlockSpec((SPAN, shape[1]), lambda n, place: (at(n), 0))
            if kind == "blocks":
                return pl.BlockSpec((1,) + shape[1:], lambda n, place: (at(n), 0, 0))
            return pl.BlockSpec(shape, lambda n, place: (0,) * len(shape))

        size = sum(a.size * a.dtype.itemsize for a in args)
        return pl.pallas_call(
            kernel,
            grid_spec=pltpu.PrefetchScalarGridSpec(
                num_scalar_prefetch=1,
                grid=(count,),
                in_specs=[spec(kind, a.shape) for kind, a in zip(specs, args)],
                out_specs=[spec(kind, shape) for kind, shape, _ in outs],
                scratch_shapes=list(scratch),
            ),
            out_shape=[jax.ShapeDtypeStruct(shape, kind) for _, shape, kind in outs],
            compiler_params=pltpu.CompilerParams(
                dimension_semantics=("arbitrary",), vmem_limit_bytes=48 * 1024 * 1024
            ),
            cost_estimate=pl.CostEstimate(
                flops=flops, bytes_accessed=2 * size, transcendentals=4 * SPAN * KEY * count
            ),
        )(self.place, *args)


def normed(values, gain):
    return values * lax.rsqrt(jnp.mean(values * values, axis=-1, keepdims=True) + EPS) * gain


def normed_grad(values, gain, grad):
    scale = lax.rsqrt(jnp.mean(values * values, axis=-1, keepdims=True) + EPS)
    weighted = grad * gain
    inner = jnp.mean(weighted * values, axis=-1, keepdims=True)
    return (
        scale * weighted - scale * scale * scale * values * inner,
        jnp.sum(grad * values * scale, axis=0),
    )


def mm(left, right, out=f32):
    return jnp.dot(left, right, preferred_element_type=f32).astype(out)


def mm_tn(left, right, out=f32):
    return dot_tn(left, right).astype(out)


def in_columns(weight, t):
    wide, tall = HEADS * KEY, HEADS * VAL
    starts = [(0, KEY), (wide, KEY), (2 * wide, VAL), (2 * wide + tall, VAL)]
    heads = [weight[:, start + t * size : start + (t + 1) * size] for start, size in starts]
    rank = weight[:, 2 * wide + 2 * tall :]
    return jnp.concatenate(heads + [jnp.pad(rank, ((0, 0), (0, LANES - RANK)))], axis=1)


def from_earlier(end, decay):
    count = lax.axis_size("h")
    if count == 2:
        return lax.ppermute(end, "h", [(0, 1)])
    ends, decays = lax.all_gather(end, "h"), lax.all_gather(decay, "h")
    mine = lax.axis_index("h")
    state = jnp.zeros(end.shape, f32)
    for h in range(count - 1):
        state = jnp.where(h < mine, decays[h] * state + ends[h].astype(f32), state)
    return state.astype(bf16)


def from_later(start, decay):
    count = lax.axis_size("h")
    if count == 2:
        return lax.ppermute(start, "h", [(1, 0)])
    starts, decays = lax.all_gather(start, "h"), lax.all_gather(decay, "h")
    mine = lax.axis_index("h")
    state = jnp.zeros(start.shape, f32)
    for h in range(count - 1, 0, -1):
        state = jnp.where(h > mine, decays[h] * state + starts[h].astype(f32), state)
    return state.astype(bf16)


def local(
    hidden_in,
    in_weight,
    out_weight,
    decay_up,
    decay_bias,
    mixer_gain,
    head_gain,
    ffn_in,
    ffn_out,
    ffn_gain,
    out_grad,
    seg_ids,
    valid_mask,
):
    tokens, width = hidden_in.shape[1:]
    place = 2 * lax.axis_index("p") + lax.axis_index("q")
    half = lax.axis_index("h")
    sizes = [lax.axis_size(axis) for axis in AXES]
    devices = sizes[0] * sizes[1] * sizes[2] * 4
    me = place
    stride = 4
    for axis in ("h", "c", "y"):
        me = me + stride * lax.axis_index(axis)
        stride *= lax.axis_size(axis)
    ff = ffn_in.shape[1] // 2
    quarter = ff // 4
    rows_all = 4 * tokens
    count = rows_all // SPAN
    x_own = hidden_in.reshape(tokens, width)
    dy_own = out_grad.reshape(tokens, width)

    small = [
        decay_up.reshape(-1),
        decay_bias,
        mixer_gain,
        head_gain,
        ffn_gain,
        seg_ids.reshape(-1).astype(bf16),
        valid_mask.reshape(-1).astype(bf16),
    ]
    lengths = [part.shape[0] for part in small]
    packed = jnp.concatenate(small)
    padded = -(-packed.shape[0] // 1024) * 1024
    packed = jnp.pad(packed, (0, padded - packed.shape[0])).reshape(-1, 128)
    offset = [sum(lengths[:i]) for i in range(len(lengths) + 1)]

    def gateup_columns(weight, t):
        return jnp.concatenate(
            [
                weight[:, t * quarter : (t + 1) * quarter],
                weight[:, ff + t * quarter : ff + (t + 1) * quarter],
            ],
            axis=1,
        )

    moves = row_owner_moves()
    back = [(b, a) for a, b in moves]

    in_rows = share_columns(in_weight, place, in_columns)
    for axis in ("q", "p", "c", "y", "h"):
        packed = stack_axis(packed, axis)
    packed = jnp.moveaxis(packed, 0, 2)
    in_rows, packed, ffn_in, out_weight = together(in_rows, packed, ffn_in, out_weight)
    in_h = half_swap(in_rows)
    in_y, in_c = near_copies(in_rows)
    gateup_rows = share_columns(ffn_in, place, gateup_columns)
    out_rows = lax.ppermute(out_weight, AXES, moves)
    in_h, in_y, in_c, gateup_rows, out_rows, x_send = together(
        in_h, in_y, in_c, gateup_rows, out_rows, x_own
    )
    in_hy, in_hc = near_copies(in_h)
    in_yc = core_swap(in_y)
    x_group = gather_group(x_send)
    out_h = half_swap(out_rows)
    out_y, out_c = near_copies(out_rows)
    in_hy, in_hc, in_yc, x_group, out_h, out_y, out_c, ffn_out, gateup_rows, dy_send = together(
        in_hy, in_hc, in_yc, x_group, out_h, out_y, out_c, ffn_out, gateup_rows, dy_own
    )
    w_gateup = lax.all_gather(gateup_rows, COPIES, axis=0, tiled=True)
    in_hyc = core_swap(in_hy)
    down_rows = lax.ppermute(ffn_out, AXES, moves)
    dy_group = gather_group(dy_send)
    out_hy, out_hc = near_copies(out_h)
    out_yc = core_swap(out_y)
    everyone = packed.reshape(sizes[0], sizes[1], -1, padded)

    def small_part(i):
        return everyone[..., offset[i] : offset[i + 1]]

    up_cols = decay_up.shape[1]
    up_all = small_part(0).reshape(devices, RANK, up_cols).transpose(1, 0, 2).reshape(RANK, HEADS, KEY)
    up_head = jnp.pad(pick(up_all, place, 1), ((0, LANES - RANK), (0, 0)))
    bias_head = pick(small_part(1).reshape(HEADS, 1, KEY), place, 0).astype(f32)
    gain_one = small_part(2).reshape(-1).astype(f32)
    gain_head = small_part(3).reshape(1, -1).astype(f32)
    gain_two = small_part(4).reshape(-1).astype(f32)

    def of_sequence(value):
        return pick(pick(value, lax.axis_index("y"), 0), lax.axis_index("c"), 0).reshape(-1)

    seg_all = of_sequence(small_part(5)).astype(f32)
    valid_all = of_sequence(small_part(6)).astype(f32)
    valid_count = jnp.sum(small_part(6).astype(f32))
    seg_here = lax.dynamic_slice(
        jnp.concatenate([jnp.full((1,), -1.0, f32), seg_all]), (half * rows_all,), (rows_all + 1,)
    )
    valid_here = lax.dynamic_slice(valid_all, (half * rows_all,), (rows_all,))
    seg_blocks = seg_here[1:].reshape(count, SPAN)
    before = seg_here[:-1].reshape(count, SPAN)[:, :1]
    final = seg_blocks[:, -1:]
    meta = jnp.stack(
        [
            seg_here[1:],
            valid_here,
            (seg_blocks == before).astype(f32).reshape(-1),
            (seg_blocks == final).astype(f32).reshape(-1),
        ]
        + [jnp.zeros((rows_all,), f32)] * 4,
        axis=1,
    )
    keep = jnp.broadcast_to((final == before).astype(f32), (count, SPAN))
    rows = jnp.stack([seg_blocks, keep] + [jnp.zeros((count, SPAN), f32)] * 6, axis=1)

    x_group = in_order(x_group)
    w_in = all_copies(in_rows, (in_y, in_c, in_yc, in_h, in_hy, in_hc, in_hyc))
    n1 = normed(x_group.astype(f32), gain_one).astype(bf16)
    proj = mm(n1, w_in)
    mixer = Mixer(place, count, tokens // SPAN)
    state_shape = (VAL, KEY)
    scratch = [pltpu.VMEM(state_shape, f32), pltpu.VMEM((1, KEY), f32)]
    sums, raw, prior, through, end, decay = mixer.call(
        states_kernel,
        ["rows", "whole", "whole", "tokens", "blocks"],
        [proj, up_head, bias_head, meta, rows],
        [
            ("rows", (rows_all, KEY), f32),
            ("rows", (rows_all, KEY), f32),
            ("blocks", (count,) + state_shape, bf16),
            ("blocks", (count, 1, KEY), f32),
            ("whole", state_shape, bf16),
            ("whole", (1, KEY), f32),
        ],
        scratch,
        flops=2 * rows_all * KEY * VAL,
    )
    end, down_rows, out_hy, out_hc, out_yc, dy_group = together(
        end, down_rows, out_hy, out_hc, out_yc, dy_group
    )
    entering = from_earlier(end, decay)
    out_hyc = core_swap(out_hy)
    entering, out_hyc, down_rows = together(entering, out_hyc, down_rows)
    w_out = all_copies(out_rows, (out_y, out_c, out_yc, out_h, out_hy, out_hc, out_hyc), True)
    down_h = half_swap(down_rows)
    down_y, down_c = near_copies(down_rows)
    gated, mixed = mixer.call(
        mixed_kernel,
        ["rows", "rows", "blocks", "blocks", "whole", "whole", "tokens", "blocks"],
        [proj, sums, prior, through, entering, gain_head, meta, rows],
        [("rows", (rows_all, VAL), bf16), ("rows", (rows_all, VAL), f32)],
        flops=2 * rows_all * (KEY * VAL + SPAN * (KEY + VAL)),
    )
    mix_parts = mm(gated, w_out).reshape(4, tokens, width)
    mix = scatter_group([mix_parts[m] for m in range(4)])
    mix, down_h, down_y, down_c = together(mix, down_h, down_y, down_c)
    h1 = x_own.astype(f32) + mix
    n2_group = gather_group(normed(h1, gain_two).astype(bf16))
    down_hy, down_hc = near_copies(down_h)
    down_yc = core_swap(down_y)
    n2_group, down_hy, down_hc, down_yc = together(n2_group, down_hy, down_hc, down_yc)
    down_hyc = core_swap(down_hy)
    w_down = all_copies(
        down_rows, (down_y, down_c, down_yc, down_h, down_hy, down_hc, down_hyc), True
    )
    n2_group = in_order(n2_group)
    dy_group = in_order(dy_group)
    grad_hidden = mm_nt(dy_group, w_down)

    gateup = mm(n2_group, w_gateup)
    gate, up = gateup[:, :quarter], gateup[:, quarter:]
    sig = jax.nn.sigmoid(gate)
    hidden = (gate * sig * up).astype(bf16)
    grad_gu = jnp.concatenate(
        [grad_hidden * up * sig * (1.0 + gate * (1.0 - sig)), grad_hidden * gate * sig], axis=1
    ).astype(bf16)
    n2_grad_parts = mm_nt(grad_gu, w_gateup).reshape(4, tokens, width)
    grad_gu, hidden, n2_grad_parts = together(grad_gu, hidden, n2_grad_parts)
    n2_grad = scatter_group([n2_grad_parts[m] for m in range(4)])
    y_parts = mm(hidden, w_down).reshape(4, tokens, width)
    gateup_sum = reduce_copies(mm_tn(n2_group, grad_gu, bf16))
    down_sum = reduce_tall(mm_tn(hidden, dy_group, bf16))

    h1_grad_part, gain_two_grad = normed_grad(h1, gain_two, n2_grad)
    h1_grad = dy_own.astype(f32) + h1_grad_part
    mix_grad = in_order(gather_group(h1_grad.astype(bf16)))
    grad_gated = mm_nt(mix_grad, w_out)
    grad_o, grad_gate, later, beyond, start, decay_b, head_grad = mixer.call(
        gate_grad_kernel,
        ["rows", "rows", "rows", "rows", "whole", "tokens", "blocks"],
        [grad_gated, proj, mixed, sums, gain_head, meta, rows],
        [
            ("rows", (rows_all, VAL), bf16),
            ("rows", (rows_all, VAL), bf16),
            ("blocks", (count,) + state_shape, bf16),
            ("blocks", (count, 1, KEY), f32),
            ("whole", state_shape, bf16),
            ("whole", (1, KEY), f32),
            ("whole", (1, VAL), f32),
        ],
        scratch,
        reverse=True,
        flops=2 * rows_all * KEY * VAL,
    )
    leaving = from_later(start, decay_b)
    y = scatter_group([after(y_parts[m], mix_grad) for m in range(4)])
    out_sum = Summing(mm_tn(gated, mix_grad, bf16), True)
    leaving, out_sum.from_c = together(leaving, out_sum.from_c)
    out_sum.send_y()
    grad_proj, rank_grad, bias_grad = mixer.call(
        inputs_grad_kernel,
        ["rows"] * 5 + ["blocks", "blocks", "whole", "blocks", "blocks", "whole", "whole", "tokens", "blocks"],
        [
            proj,
            sums,
            raw,
            grad_o,
            grad_gate,
            prior,
            through,
            entering,
            later,
            beyond,
            leaving,
            up_head,
            meta,
            rows,
        ],
        [
            ("rows", proj.shape, bf16),
            ("whole", (LANES, KEY), f32),
            ("whole", (1, KEY), f32),
        ],
        flops=2 * rows_all * (3 * KEY * VAL + SPAN * (3 * KEY + 2 * VAL)),
    )
    n1_grad_parts = mm_nt(grad_proj, w_in).reshape(4, tokens, width)
    n1_grad_parts, out_sum.from_y, grad_proj, y = together(
        n1_grad_parts, out_sum.from_y, grad_proj, y
    )
    n1_grad = scatter_group([n1_grad_parts[m] for m in range(4)])
    out_sum.send_h()
    in_sum = Summing(mm_tn(n1, grad_proj, bf16))
    n1_grad, in_sum.from_c, out_sum.from_h = together(n1_grad, in_sum.from_c, out_sum.from_h)
    in_sum.send_y()
    outproj_grad = lax.ppermute(out_sum.total().astype(bf16), AXES, back)
    input_part, gain_one_grad = normed_grad(x_own.astype(f32), gain_one, n1_grad)
    input_grad = (h1_grad + input_part).reshape(1, tokens, width)
    in_sum.from_y, outproj_grad, gateup_sum, down_sum = together(
        in_sum.from_y, outproj_grad, gateup_sum, down_sum
    )
    in_sum.send_h()
    gateup_back = return_columns(gateup_sum, place)
    ffnout_grad = lax.ppermute(down_sum, AXES, back)
    in_sum.from_h, gateup_back, ffnout_grad = together(in_sum.from_h, gateup_back, ffnout_grad)
    in_back = return_columns(in_sum.total(), place)
    ffnout_grad, outproj_grad = ffnout_grad.astype(f32), outproj_grad.astype(f32)
    ffnin_grad = jnp.concatenate(
        [part[:, :quarter] for part in gateup_back] + [part[:, quarter:] for part in gateup_back],
        axis=1,
    )
    inproj_grad = jnp.concatenate(
        [part[:, :KEYS] for part in in_back]
        + [part[:, KEYS:VALUES] for part in in_back]
        + [part[:, VALUES:GATES] for part in in_back]
        + [part[:, GATES:RANKS] for part in in_back]
        + [sum(part[:, RANKS : RANKS + RANK] for part in in_back)],
        axis=1,
    )
    result = h1 + y
    block_out = result.astype(bf16).reshape(1, tokens, width)
    live = valid_mask.reshape(tokens, 1).astype(f32)
    squares = jnp.stack(
        [jnp.sum(live * result * result), jnp.sum(live * mix * mix), jnp.sum(live * y * y)]
    )

    head_slot = (lax.broadcasted_iota(jnp.int32, (HEADS, 1, 1), 0) == place).astype(f32)
    decay_part = head_slot * jnp.concatenate([rank_grad[:RANK], bias_grad], axis=0)[None]
    sums_of = [squares, head_grad.reshape(-1), gain_two_grad, decay_part.reshape(-1), gain_one_grad]
    total = jnp.concatenate(sums_of)
    short = -total.shape[0] % 1024
    total = after(jnp.pad(total, (0, short)).reshape(-1, 128), in_sum.from_y)
    total = sum_all(total).reshape(-1)
    ends = [0]
    for part in sums_of:
        ends.append(ends[-1] + part.shape[0])
    squares = total[: ends[1]]
    root_means = jnp.sqrt(squares / (jnp.maximum(valid_count, 1.0) * width))

    def own(value, length):
        return lax.dynamic_slice(value, (me * length,), (length,))

    headgain_grad = own(total[ends[1] : ends[2]], head_gain.shape[0])
    ffngain_grad = own(total[ends[2] : ends[3]], ffn_gain.shape[0])
    mixgain_grad = own(total[ends[4] : ends[5]], mixer_gain.shape[0])
    decay_all = total[ends[3] : ends[4]].reshape(HEADS, RANK + 1, KEY)
    decay_all = decay_all.transpose(1, 0, 2).reshape(RANK + 1, HEADS * KEY)
    decay_own = lax.dynamic_slice(decay_all, (0, me * up_cols), (RANK + 1, up_cols))
    return (
        block_out,
        input_grad,
        inproj_grad,
        outproj_grad,
        decay_own[:RANK],
        decay_own[RANK],
        mixgain_grad,
        headgain_grad,
        ffnin_grad,
        ffnout_grad,
        ffngain_grad,
        root_means,
    )


def mm_nt(left, right, out=f32):
    return dot_nt(left, right).astype(out)


def solution(mesh):
    dp, seq = mesh.shape["dp"], mesh.shape["seq"]
    fine = Mesh(mesh.devices.reshape(dp // 2, 2, seq // 4, 2, 2), AXES)
    batch, spread, whole = ("y", "c"), ("h", "p", "q"), AXES
    placed = (
        P(batch, spread, None),
        P(whole, None),
        P(whole, None),
        P(None, whole),
        P(whole),
        P(whole),
        P(whole),
        P(whole, None),
        P(whole, None),
        P(whole),
        P(batch, spread, None),
        P(batch, spread),
        P(batch, spread),
    )
    return jax.shard_map(
        local,
        mesh=fine,
        in_specs=placed,
        out_specs=(
            P(batch, spread, None),
            P(batch, spread, None),
            P(whole, None),
            P(whole, None),
            P(None, whole),
            P(whole),
            P(whole),
            P(whole),
            P(whole, None),
            P(whole, None),
            P(whole),
            P(),
        ),
        check_vma=False,
    )
```

```python
import jax
import jax.numpy as jnp
from jax import lax
from jax.experimental import pallas as pl
from jax.experimental.pallas import tpu as pltpu
from jax.sharding import Mesh, PartitionSpec as P

HEADS = 4
KEY = 256
VAL = 512
SPAN = 64
RANK = 16
LANES = 128
EPS = 1e-05
FLOOR = 1.0
QSCALE = KEY**-0.5
KEYS, VALUES, GATES, RANKS = KEY, 2 * KEY, 2 * KEY + VAL, 2 * KEY + 2 * VAL

AXES = ("y", "c", "h", "p", "q")
COPIES = ("y", "c", "h")


bf16 = jnp.bfloat16
f32 = jnp.float32


def after(value, *deps):
    return lax.optimization_barrier((value, deps))[0]


def together(*values):
    return lax.optimization_barrier(values)


def swap(value, axis):
    return lax.ppermute(value, axis, [(0, 1), (1, 0)])


def across(value, mask, group=("p", "q")):
    return lax.ppermute(value, group, [(i, i ^ mask) for i in range(4)])


def two_of(value, group=("p", "q")):
    return across(value, 1, group), across(value, 2, group)


def last_of(value, group=("p", "q")):
    return across(value, 3, group)


def shares(parts):
    return [parts[mask].astype(bf16) for mask in range(4)]


def add_shares(own, received):
    return own + received[0].astype(f32) + received[1].astype(f32) + received[2].astype(f32)


def half_swap(block):
    return swap(block, "h") if binary_copies() else block


def stack_axis(value, axis):
    if lax.axis_size(axis) != 2:
        return lax.all_gather(value, axis)
    other = swap(value, axis)
    first = lax.axis_index(axis) == 0
    return jnp.where(first, jnp.stack([value, other]), jnp.stack([other, value]))


def sum_over(value, axis):
    if lax.axis_size(axis) == 2:
        return value + swap(value, axis)
    return lax.psum(value, axis)


def sum_group(value, axes):
    if any(lax.axis_size(axis) != 2 for axis in axes):
        return lax.psum(value, axes)
    return value + across(value, 1, axes) + across(value, 2, axes) + across(value, 3, axes)


def binary_copies():
    return all(lax.axis_size(axis) == 2 for axis in COPIES)


def lay_kernel(offsets, pieces, count, *refs):
    blocks, whole, sems = refs[:count], refs[count], refs[count + 1]
    copies = []
    for i, (block, first, rows) in enumerate(pieces):
        place = pl.ds(pl.multiple_of(offsets[i], 16), rows)
        copies.append(
            pltpu.make_async_copy(
                blocks[block].at[pl.ds(first, rows)], whole.at[place], sems.at[i]
            )
        )
    for copy in copies:
        copy.start()
    for copy in copies:
        copy.wait()


def lay(blocks, pieces, offsets):
    cols, kind = blocks[0].shape[1], blocks[0].dtype
    total = sum(rows for _, _, rows in pieces)
    return pl.pallas_call(
        lambda offsets, *refs: lay_kernel(offsets, pieces, len(blocks), *refs),
        grid_spec=pltpu.PrefetchScalarGridSpec(
            num_scalar_prefetch=1,
            grid=(1,),
            in_specs=[pl.BlockSpec(memory_space=pl.ANY)] * len(blocks),
            out_specs=pl.BlockSpec(memory_space=pl.ANY),
            scratch_shapes=[pltpu.SemaphoreType.DMA((len(pieces),))],
        ),
        out_shape=jax.ShapeDtypeStruct((total, cols), kind),
        compiler_params=pltpu.CompilerParams(vmem_limit_bytes=16 * 1024 * 1024),
        cost_estimate=pl.CostEstimate(
            flops=0, bytes_accessed=2 * total * cols * kind.itemsize, transcendentals=0
        ),
    )(jnp.stack(offsets).astype(jnp.int32), *blocks)


def in_order(blocks):
    rows = blocks[0].shape[0]
    pieces = [(i, 0, rows) for i in range(len(blocks))]
    return lay(blocks, pieces, [jnp.int32(i * rows) for i in range(len(blocks))])


def pick(value, index, axis):
    return lax.dynamic_index_in_dim(value, index, axis, keepdims=False)


class Names:
    def __getattr__(self, name):
        return name


n = Names()


class Live:
    def __init__(self, **values):
        self.v = dict(values)
        self.binary = binary_copies()
        self.at = {axis: lax.axis_index(axis) for axis in AXES}

    def sync(self, *names):
        self.v.update(zip(names, lax.optimization_barrier([self.v[name] for name in names])))

    def swap(self, name, value, axis):
        self.v[name] = swap(value(), axis) if self.binary else jnp.zeros((8, 128), bf16)

    def send(self, *names):
        for name in names:
            weight, way = name.split("__")
            source = weight if len(way) == 1 else weight + "__" + way[:-1]
            axis = "h" if way[-1] == "f" else way[-1]
            self.swap(name, lambda: self.v[source], axis)

    def gathered(self, weight):
        own = self.v[weight]
        if not self.binary:
            return lax.all_gather(own, COPIES, axis=0, tiled=True)
        rows, blocks, pieces, offsets = own.shape[0], [], [], []
        for way in ("", "y", "c", "yc", "f", "fy", "fc", "fyc"):
            y, c = self.at["y"] ^ ("y" in way), self.at["c"] ^ ("c" in way)
            f = self.at["h"] ^ ("f" in way)
            place = f * 4 + y * 2 + c if weight == n.out else y * 4 + c * 2 + f
            pieces.append((len(blocks), 0, rows))
            offsets.append(place * rows)
            blocks.append(self.v[weight + "__" + way] if way else own)
        return lay(blocks, pieces, offsets)

    def near(self, weight, y, f):
        c, total = self.at["c"], 0.0
        for value in (self.v[weight + "_g"], self.v[weight + "_g__c"]):
            rows, cols = value.shape
            place = f * 4 + y * 2 + c if weight == n.out else y * 4 + c * 2 + f
            value = lax.dynamic_slice_in_dim(value, place * (rows // 8), rows // 8, 0)
            total = total + value.astype(f32)
        return total

    def add(self, *names):
        for name in names:
            weight, way = name.split("_g__")
            y, f = self.at["y"], self.at["h"]
            if way == "c":
                self.swap(name, lambda: self.v[weight + "_g"], "c")
            elif way in ("y0", "y1"):
                which = 1 - f if way == "y0" else f
                self.swap(name, lambda: self.near(weight, 1 - y, which).astype(bf16), "y")
            else:
                first = weight + "_g__y0"
                self.swap(
                    name,
                    lambda: (self.near(weight, y, 1 - f) + self.v[first].astype(f32)).astype(bf16),
                    "h",
                )

    def summed(self, weight):
        grad = weight + "_g"
        if not self.binary:
            return lax.psum_scatter(
                self.v[grad], COPIES, scatter_dimension=0, tiled=True
            ).astype(f32)
        value = self.near(weight, self.at["y"], self.at["h"])
        return value + self.v[grad + "__y1"].astype(f32) + self.v[grad + "__f"].astype(f32)


def share_columns(weight, place, columns, group=("p", "q")):
    pieces = [columns(weight, t) for t in range(4)]
    got = []
    for mask in range(4):
        piece = lax.select_n(place, *[pieces[t ^ mask] for t in range(4)])
        got.append(piece if mask == 0 else across(piece, mask, group))
    return jnp.concatenate(
        [lax.select_n(place, *[got[t ^ spot] for t in range(4)]) for spot in range(4)]
    )


def return_columns(grad, place, group=("p", "q")):
    value = grad.reshape(4, grad.shape[0] // 4, grad.shape[1])
    got = [pick(value, place, 0).astype(f32)]
    for mask in (1, 2, 3):
        got.append(across(pick(value, place ^ mask, 0).astype(bf16), mask, group).astype(f32))
    return [lax.select_n(place, *[got[t ^ spot] for t in range(4)]) for spot in range(4)]


def both_halves(own, other):
    first = lax.axis_index("h") == 0
    return jnp.where(first, jnp.concatenate([own, other]), jnp.concatenate([other, own]))


def gather_halves(own, other, tall):
    if not binary_copies():
        return lax.all_gather(own, COPIES, axis=0, tiled=True)
    both = both_halves(own, other)
    if not tall:
        return lax.all_gather(both, ("y", "c"), axis=0, tiled=True)
    both = both.reshape(2, -1, own.shape[1])
    return lax.all_gather(both, ("y", "c"), axis=1, tiled=True).reshape(-1, own.shape[1])


def sum_near(grad, tall):
    if not binary_copies():
        return lax.psum_scatter(grad, COPIES, scatter_dimension=0, tiled=True)
    cols = grad.shape[1]
    if tall:
        grad = grad.reshape(2, -1, cols)
        return lax.psum_scatter(grad, ("y", "c"), scatter_dimension=1, tiled=True)
    return lax.psum_scatter(grad, ("y", "c"), scatter_dimension=0, tiled=True).reshape(2, -1, cols)


def other_half(part):
    if not binary_copies():
        return jnp.zeros((8, 128), bf16)
    return swap(pick(part, 1 - lax.axis_index("h"), 0), "h")


def sum_halves(part, other):
    if not binary_copies():
        return part.astype(f32)
    return pick(part, lax.axis_index("h"), 0).astype(f32) + other.astype(f32)


def row_owner_moves():
    total = 1
    for axis in AXES:
        total *= lax.axis_size(axis)
    if not binary_copies():
        copies = total // 4
        return [(g, (g % copies) * 4 + g // copies) for g in range(total)]
    pairs = []
    for g in range(total):
        y, c, h, p, q = (g >> bit & 1 for bit in (4, 3, 2, 1, 0))
        to = (p, q, h, y, c)
        pairs.append((g, sum(bit << (4 - i) for i, bit in enumerate(to))))
    return pairs


def dot_nn(a, b):
    return lax.dot_general(a, b, (((1,), (0,)), ((), ())), preferred_element_type=f32)


def dot_nt(a, b):
    return lax.dot_general(a, b, (((1,), (1,)), ((), ())), preferred_element_type=f32)


def dot_tn(a, b):
    return lax.dot_general(a, b, (((0,), (0,)), ((), ())), preferred_element_type=f32)


def two_parts(value):
    high = value.astype(bf16)
    return high, (value - high.astype(f32)).astype(bf16)


def triangle(lower):
    row = lax.broadcasted_iota(jnp.int32, (SPAN, SPAN), 0)
    col = lax.broadcasted_iota(jnp.int32, (SPAN, SPAN), 1)
    return jnp.where(row >= col if lower else row <= col, 1.0, 0.0)


def running_sum(value, lower):
    ones = triangle(lower).astype(bf16)
    high, low = two_parts(value)
    return dot_nn(ones, high) + dot_nn(ones, low)


def pair_mask(meta, rows):
    return jnp.where(meta[:, 0:1] == rows[0:1, :], triangle(True), 0.0)


def states_kernel(
    place, proj, up, bias, meta, rows, sums, raw, prior, through, end, decay, state, total
):
    @pl.when(pl.program_id(0) == 0)
    def _():
        state[...] = jnp.zeros_like(state)
        total[...] = jnp.ones_like(total)

    keys = proj[:, KEYS:VALUES].astype(bf16).astype(f32)
    gate = dot_nn(proj[:, RANKS:].astype(bf16), up[...]) + bias[...]
    log_decay = (jnp.minimum(gate, 0.0) - jnp.log1p(jnp.exp(-jnp.abs(gate)))) * (1.0 / 16.0)
    run = running_sum(log_decay, True)
    raw[...] = gate
    sums[...] = run
    last = run[SPAN - 1 :, :]
    info = meta[...]
    k_final = (keys * jnp.exp(last - run) * (info[:, 1:2] * info[:, 3:4])).astype(bf16)
    step = rows[0, 1:2, 0:1] * jnp.exp(last)
    prior[0] = state[...].astype(bf16)
    through[0] = total[...]
    state[...] = step * state[...] + dot_tn(proj[:, VALUES:GATES].astype(bf16), k_final)
    total[...] = step * total[...]
    end[...] = state[...].astype(bf16)
    decay[...] = total[...]


def mixed_kernel(place, proj, sums, prior, through, entering, gain, meta, rows, gated, mixed):
    info = meta[...]
    run = sums[...]
    query = proj[:, :KEYS].astype(bf16).astype(f32)
    q_decay = (query * QSCALE * jnp.exp(run)).astype(bf16)
    k_decay = (proj[:, KEYS:VALUES].astype(bf16).astype(f32) * info[:, 1:2] * jnp.exp(-run)).astype(bf16)
    scores = (dot_nt(q_decay, k_decay) * pair_mask(info, rows[0])).astype(bf16)
    state = (prior[0].astype(f32) + through[0] * entering[...].astype(f32)).astype(bf16)
    out = dot_nn(scores, proj[:, VALUES:GATES].astype(bf16)) + info[:, 2:3] * dot_nt(q_decay, state)
    mixed[...] = out
    gate = proj[:, GATES:RANKS]
    scale = lax.rsqrt(jnp.mean(out * out, axis=-1, keepdims=True) + FLOOR)
    gated[...] = (out * scale * gain[...] * gate * jax.nn.sigmoid(gate)).astype(bf16)


def gate_grad_kernel(
    place,
    grad_gated,
    proj,
    mixed,
    sums,
    gain,
    meta,
    rows,
    grad_out,
    grad_gate,
    later,
    beyond,
    start,
    decay,
    grad_gain,
    state,
    total,
):
    @pl.when(pl.program_id(0) == 0)
    def _():
        state[...] = jnp.zeros_like(state)
        total[...] = jnp.ones_like(total)
        grad_gain[...] = jnp.zeros_like(grad_gain)

    info = meta[...]
    run = sums[...]
    out = mixed[...]
    gate = proj[:, GATES:RANKS]
    grad = grad_gated[...]
    sig = jax.nn.sigmoid(gate)
    scale = lax.rsqrt(jnp.mean(out * out, axis=-1, keepdims=True) + FLOOR)
    scaled = out * scale
    swish = gate * sig
    weighted = grad * gain[...] * swish
    inner = jnp.mean(scaled * weighted, axis=-1, keepdims=True)
    grad_o = (scale * (weighted - scaled * inner)).astype(bf16)
    grad_out[...] = grad_o
    grad_gate[...] = (grad * scaled * gain[...] * sig * (1.0 + gate * (1.0 - sig))).astype(bf16)
    grad_gain[...] += jnp.sum(grad * scaled * swish, axis=0, keepdims=True)
    query = proj[:, :KEYS].astype(bf16).astype(f32)
    q_enter = (query * QSCALE * jnp.exp(run)).astype(bf16)
    o_enter = jnp.where(info[:, 2:3] > 0.0, grad_o.astype(f32), 0.0).astype(bf16)
    step = rows[0, 1:2, 0:1] * jnp.exp(run[SPAN - 1 :, :])
    later[0] = state[...].astype(bf16)
    beyond[0] = total[...]
    state[...] = step * state[...] + dot_tn(o_enter, q_enter)
    total[...] = step * total[...]
    start[...] = state[...].astype(bf16)
    decay[...] = total[...]


def inputs_grad_kernel(
    place,
    proj,
    sums,
    raw,
    grad_out,
    grad_gate,
    prior,
    through,
    entering,
    later,
    beyond,
    leaving,
    up,
    meta,
    rows,
    grad_proj,
    grad_up,
    grad_bias,
):
    @pl.when(pl.program_id(0) == 0)
    def _():
        grad_up[...] = jnp.zeros_like(grad_up)
        grad_bias[...] = jnp.zeros_like(grad_bias)

    info = meta[...]
    run = sums[...]
    last = run[SPAN - 1 :, :]
    valid, enter, carry = info[:, 1:2], info[:, 2:3], info[:, 3:4]
    grow, shrink, tail = jnp.exp(run), jnp.exp(-run), jnp.exp(last - run) * carry
    query = proj[:, :KEYS].astype(bf16).astype(f32)
    keys = proj[:, KEYS:VALUES].astype(bf16).astype(f32) * valid
    values = proj[:, VALUES:GATES].astype(bf16)
    q_decay = (query * QSCALE * grow).astype(bf16)
    k_decay = (keys * shrink).astype(bf16)
    k_final = (keys * tail).astype(bf16)
    mask = pair_mask(info, rows[0])
    state = prior[0].astype(f32) + through[0] * entering[...].astype(f32)
    state_grad = later[0].astype(f32) + beyond[0] * leaving[...].astype(f32)
    state_b, state_grad_b = state.astype(bf16), state_grad.astype(bf16)
    grad_o = grad_out[...]
    scores = (dot_nt(q_decay, k_decay) * mask).astype(bf16)
    grad_scores = (dot_nt(grad_o, values) * mask).astype(bf16)
    grad_v = dot_tn(scores, grad_o) + dot_nt(k_final, state_grad_b)
    grad_qd = dot_nn(grad_scores, k_decay) + enter * dot_nn(grad_o, state_b)
    grad_kd = dot_tn(grad_scores, q_decay)
    grad_kf = dot_nn(values, state_grad_b)
    step = rows[0, 1:2, 0:1] * jnp.exp(last)
    through_last = step * jnp.sum(state * state_grad, axis=0, keepdims=True)
    final_part = grad_kf * k_final.astype(f32)
    grad_run = grad_qd * q_decay.astype(f32) - grad_kd * k_decay.astype(f32) - final_part
    grad_last = through_last + jnp.sum(final_part, axis=0, keepdims=True)
    grad_log = running_sum(grad_run, False) + grad_last
    grad_raw = grad_log * jax.nn.sigmoid(-raw[...]) * (1.0 / 16.0)
    high, low = two_parts(grad_raw)
    rank = proj[:, RANKS:].astype(bf16)
    grad_up[...] += dot_tn(rank, high) + dot_tn(rank, low)
    grad_bias[...] += jnp.sum(grad_raw, axis=0, keepdims=True)
    grad_rank = dot_nt(high, up[...]) + dot_nt(low, up[...])
    grad_k = (grad_kd * shrink + grad_kf * tail) * valid
    grad_proj[:, KEYS:VALUES] = grad_k.astype(bf16)
    grad_proj[:, VALUES:GATES] = grad_v.astype(bf16)
    grad_proj[:, RANKS:] = grad_rank.astype(bf16)
    grad_proj[:, :KEYS] = (grad_qd * grow * QSCALE).astype(bf16)
    grad_proj[:, GATES:RANKS] = grad_gate[...]


class Mixer:
    def __init__(self, place, blocks, per_device):
        self.place = place.reshape(1)
        self.blocks = blocks
        self.per_device = per_device

    def call(self, kernel, specs, args, outs, scratch=(), reverse=False, flops=0):
        count, per_device = self.blocks, self.per_device

        def at(step):
            return count - 1 - step if reverse else step

        def spec(kind, shape):
            if kind == "rows":
                return pl.BlockSpec(
                    (SPAN, shape[1]),
                    lambda n, place: (
                        lax.bitwise_xor(at(n) // per_device, place[0]) * per_device
                        + at(n) % per_device,
                        0,
                    ),
                )
            if kind == "tokens":
                return pl.BlockSpec((SPAN, shape[1]), lambda n, place: (at(n), 0))
            if kind == "blocks":
                return pl.BlockSpec((1,) + shape[1:], lambda n, place: (at(n), 0, 0))
            return pl.BlockSpec(shape, lambda n, place: (0,) * len(shape))

        size = sum(a.size * a.dtype.itemsize for a in args)
        return pl.pallas_call(
            kernel,
            grid_spec=pltpu.PrefetchScalarGridSpec(
                num_scalar_prefetch=1,
                grid=(count,),
                in_specs=[spec(kind, a.shape) for kind, a in zip(specs, args)],
                out_specs=[spec(kind, shape) for kind, shape, _ in outs],
                scratch_shapes=list(scratch),
            ),
            out_shape=[jax.ShapeDtypeStruct(shape, kind) for _, shape, kind in outs],
            compiler_params=pltpu.CompilerParams(
                dimension_semantics=("arbitrary",), vmem_limit_bytes=48 * 1024 * 1024
            ),
            cost_estimate=pl.CostEstimate(
                flops=flops, bytes_accessed=2 * size, transcendentals=4 * SPAN * KEY * count
            ),
        )(self.place, *args)


def normed(values, gain):
    return values * lax.rsqrt(jnp.mean(values * values, axis=-1, keepdims=True) + EPS) * gain


def normed_grad(values, gain, grad):
    scale = lax.rsqrt(jnp.mean(values * values, axis=-1, keepdims=True) + EPS)
    weighted = grad * gain
    inner = jnp.mean(weighted * values, axis=-1, keepdims=True)
    return (
        scale * weighted - scale * scale * scale * values * inner,
        jnp.sum(grad * values * scale, axis=0),
    )


def mm(left, right, out=f32):
    return jnp.dot(left, right, preferred_element_type=f32).astype(out)


def mm_tn(left, right, out=f32):
    return dot_tn(left, right).astype(out)


def in_columns(weight, t):
    wide, tall = HEADS * KEY, HEADS * VAL
    starts = [(0, KEY), (wide, KEY), (2 * wide, VAL), (2 * wide + tall, VAL)]
    heads = [weight[:, start + t * size : start + (t + 1) * size] for start, size in starts]
    rank = weight[:, 2 * wide + 2 * tall :]
    return jnp.concatenate(heads + [jnp.pad(rank, ((0, 0), (0, LANES - RANK)))], axis=1)


def from_earlier(end, decay):
    count = lax.axis_size("h")
    if count == 2:
        return lax.ppermute(end, "h", [(0, 1)])
    ends, decays = lax.all_gather(end, "h"), lax.all_gather(decay, "h")
    mine = lax.axis_index("h")
    state = jnp.zeros(end.shape, f32)
    for h in range(count - 1):
        state = jnp.where(h < mine, decays[h] * state + ends[h].astype(f32), state)
    return state.astype(bf16)


def from_later(start, decay):
    count = lax.axis_size("h")
    if count == 2:
        return lax.ppermute(start, "h", [(1, 0)])
    starts, decays = lax.all_gather(start, "h"), lax.all_gather(decay, "h")
    mine = lax.axis_index("h")
    state = jnp.zeros(start.shape, f32)
    for h in range(count - 1, 0, -1):
        state = jnp.where(h > mine, decays[h] * state + starts[h].astype(f32), state)
    return state.astype(bf16)


def local(
    hidden_in,
    in_weight,
    out_weight,
    decay_up,
    decay_bias,
    mixer_gain,
    head_gain,
    ffn_in,
    ffn_out,
    ffn_gain,
    out_grad,
    seg_ids,
    valid_mask,
):
    tokens, width = hidden_in.shape[1:]
    place = 2 * lax.axis_index("p") + lax.axis_index("q")
    half = lax.axis_index("h")
    sizes = [lax.axis_size(axis) for axis in AXES]
    devices = sizes[0] * sizes[1] * sizes[2] * 4
    me = place
    stride = 4
    for axis in ("h", "c", "y"):
        me = me + stride * lax.axis_index(axis)
        stride *= lax.axis_size(axis)
    ff = ffn_in.shape[1] // 2
    quarter = ff // 4
    rows_all = 4 * tokens
    count = rows_all // SPAN
    x_own = hidden_in.reshape(tokens, width)
    dy_own = out_grad.reshape(tokens, width)

    small = [
        decay_up.reshape(-1),
        decay_bias,
        mixer_gain,
        head_gain,
        ffn_gain,
        seg_ids.reshape(-1).astype(bf16),
        valid_mask.reshape(-1).astype(bf16),
    ]
    lengths = [part.shape[0] for part in small]
    packed = jnp.concatenate(small)
    padded = -(-packed.shape[0] // 1024) * 1024
    packed = jnp.pad(packed, (0, padded - packed.shape[0])).reshape(-1, 128)
    offset = [sum(lengths[:i]) for i in range(len(lengths) + 1)]

    def gateup_columns(weight, t):
        return jnp.concatenate(
            [
                weight[:, t * quarter : (t + 1) * quarter],
                weight[:, ff + t * quarter : ff + (t + 1) * quarter],
            ],
            axis=1,
        )

    def inverse(pairs):
        return [(b, a) for a, b in pairs]

    out_moves, down_moves = row_owner_moves(), row_owner_moves()
    live = Live(x=x_own, dy=dy_own, ffn_in=ffn_in, ffn_out=ffn_out, out_weight=out_weight)
    v, sync, send, add = live.v, live.sync, live.send, live.add

    v[n.inp] = share_columns(in_weight, place, in_columns)
    for axis in ("q", "p", "c", "y"):
        packed = stack_axis(packed, axis)
    sync(n.inp, n.out_weight, n.ffn_in)
    send(n.inp__f, n.inp__y, n.inp__c)
    v[n.gateup] = share_columns(v[n.ffn_in], place, gateup_columns)
    v[n.out] = lax.ppermute(v[n.out_weight], AXES, out_moves)
    v[n.packed] = packed
    sync(n.inp__f, n.inp__y, n.inp__c, n.x, n.out, n.packed)
    send(n.inp__fy, n.inp__fc, n.inp__yc)
    v[n.x1], v[n.x2] = two_of(v[n.x])
    v[n.x3] = last_of(v[n.x])
    send(n.out__f, n.out__y, n.out__c)
    v[n.packed] = jnp.moveaxis(stack_axis(v[n.packed], "h"), 0, 2)
    sync(n.inp__fy, n.inp__fc, n.inp__yc, n.x1, n.x2, n.x3, n.out__f, n.out__y, n.out__c, n.gateup, n.packed)
    send(n.inp__fyc, n.out__fy, n.out__fc, n.out__yc)
    v[n.gate], v[n.up] = v[n.gateup][:, :quarter], v[n.gateup][:, quarter:]
    v[n.gate__f] = half_swap(v[n.gate])
    sync(n.inp__fyc, n.out__fy, n.out__fc, n.out__yc, n.gate, n.up, n.ffn_out, n.dy)
    send(n.out__fyc)
    packed = v[n.packed]
    everyone = packed.reshape(sizes[0], sizes[1], -1, padded)

    def small_part(i):
        return everyone[..., offset[i] : offset[i + 1]]

    up_cols = decay_up.shape[1]
    up_all = small_part(0).reshape(devices, RANK, up_cols).transpose(1, 0, 2).reshape(RANK, HEADS, KEY)
    up_head = jnp.pad(pick(up_all, place, 1), ((0, LANES - RANK), (0, 0)))
    bias_head = pick(small_part(1).reshape(HEADS, 1, KEY), place, 0).astype(f32)
    gain_one = small_part(2).reshape(-1).astype(f32)
    gain_head = small_part(3).reshape(1, -1).astype(f32)
    gain_two = small_part(4).reshape(-1).astype(f32)

    def of_sequence(value):
        return pick(pick(value, lax.axis_index("y"), 0), lax.axis_index("c"), 0).reshape(-1)

    seg_all = of_sequence(small_part(5)).astype(f32)
    valid_all = of_sequence(small_part(6)).astype(f32)
    valid_count = jnp.sum(small_part(6).astype(f32))
    seg_here = lax.dynamic_slice(
        jnp.concatenate([jnp.full((1,), -1.0, f32), seg_all]), (half * rows_all,), (rows_all + 1,)
    )
    valid_here = lax.dynamic_slice(valid_all, (half * rows_all,), (rows_all,))
    seg_blocks = seg_here[1:].reshape(count, SPAN)
    before = seg_here[:-1].reshape(count, SPAN)[:, :1]
    final = seg_blocks[:, -1:]
    meta = jnp.stack(
        [
            seg_here[1:],
            valid_here,
            (seg_blocks == before).astype(f32).reshape(-1),
            (seg_blocks == final).astype(f32).reshape(-1),
        ]
        + [jnp.zeros((rows_all,), f32)] * 4,
        axis=1,
    )
    keep = jnp.broadcast_to((final == before).astype(f32), (count, SPAN))
    rows = jnp.stack([seg_blocks, keep] + [jnp.zeros((count, SPAN), f32)] * 6, axis=1)

    x_group = in_order([x_own, v[n.x1], v[n.x2], v[n.x3]])
    w_in = live.gathered(n.inp)
    n1 = normed(x_group.astype(f32), gain_one).astype(bf16)
    proj = mm(n1, w_in)
    mixer = Mixer(place, count, tokens // SPAN)
    state_shape = (VAL, KEY)
    scratch = [pltpu.VMEM(state_shape, f32), pltpu.VMEM((1, KEY), f32)]
    sums, raw, prior, through, v[n.end], decay = mixer.call(
        states_kernel,
        ["rows", "whole", "whole", "tokens", "blocks"],
        [proj, up_head, bias_head, meta, rows],
        [
            ("rows", (rows_all, KEY), f32),
            ("rows", (rows_all, KEY), f32),
            ("blocks", (count,) + state_shape, bf16),
            ("blocks", (count, 1, KEY), f32),
            ("whole", state_shape, bf16),
            ("whole", (1, KEY), f32),
        ],
        scratch,
        flops=2 * rows_all * KEY * VAL,
    )
    v[n.w_out] = live.gathered(n.out)
    sync(n.end, n.ffn_out, n.w_out)
    w_out = v[n.w_out]
    v[n.entering] = from_earlier(v[n.end], decay)
    v[n.down] = lax.ppermute(v[n.ffn_out], AXES, down_moves)
    entering = v[n.entering]
    sync(n.entering, n.gate, n.gate__f, n.up)
    v[n.up__f] = half_swap(v[n.up])
    w_gate = gather_halves(v[n.gate], v[n.gate__f], False)
    gated, mixed = mixer.call(
        mixed_kernel,
        ["rows", "rows", "blocks", "blocks", "whole", "whole", "tokens", "blocks"],
        [proj, sums, prior, through, entering, gain_head, meta, rows],
        [("rows", (rows_all, VAL), bf16), ("rows", (rows_all, VAL), f32)],
        flops=2 * rows_all * (KEY * VAL + SPAN * (KEY + VAL)),
    )
    mix_parts = mm(gated, w_out).reshape(4, tokens, width)
    mix_own = mix_parts[0]
    v[n.mix_send] = shares(mix_parts)
    sync(n.mix_send)
    v[n.mix1], v[n.mix2] = across(v[n.mix_send][1], 1), across(v[n.mix_send][2], 2)
    sync(n.mix1, n.mix2, n.mix_send, n.down, n.up, n.up__f)
    v[n.down__f] = half_swap(v[n.down])
    v[n.w_up] = gather_halves(v[n.up], v[n.up__f], False)
    v[n.w_gate] = w_gate
    v[n.mix3] = across(v[n.mix_send][3], 3)
    sync(n.mix3)
    mix = add_shares(mix_own, (v[n.mix1], v[n.mix2], v[n.mix3]))
    h1 = x_own.astype(f32) + mix
    v[n.n2] = normed(h1, gain_two).astype(bf16)
    v[n.n21], v[n.n22] = two_of(v[n.n2])
    sync(n.n21, n.n22, n.n2, n.dy, n.down, n.down__f, n.w_gate, n.w_up)
    w_gate, w_up = v[n.w_gate], v[n.w_up]
    w_down = gather_halves(v[n.down], v[n.down__f], True)
    v[n.n23] = last_of(v[n.n2])
    sync(n.n21, n.n22, n.n23, n.n2, n.dy)
    v[n.dy1], v[n.dy2] = two_of(v[n.dy])
    v[n.dy3] = last_of(v[n.dy])
    n2_group = in_order([v[n.n2], v[n.n21], v[n.n22], v[n.n23]])
    dy_group = in_order([dy_own, v[n.dy1], v[n.dy2], v[n.dy3]])
    gate = mm(n2_group, w_gate)
    up = mm(n2_group, w_up)
    grad_hidden = mm_nt(dy_group, w_down)

    sig = jax.nn.sigmoid(gate)
    hidden = (gate * sig * up).astype(bf16)
    grad_g = (grad_hidden * up * sig * (1.0 + gate * (1.0 - sig))).astype(bf16)
    grad_u = (grad_hidden * gate * sig).astype(bf16)
    n2_grad_parts = (mm_nt(grad_g, w_gate) + mm_nt(grad_u, w_up)).reshape(4, tokens, width)
    v[n.n2_send] = shares(n2_grad_parts)
    v[n.grad_g], v[n.grad_u], v[n.hidden] = grad_g, grad_u, hidden
    sync(n.n2_send, n.grad_g, n.grad_u, n.hidden)
    v[n.s1], v[n.s2] = across(v[n.n2_send][1], 1), across(v[n.n2_send][2], 2)
    v[n.gate_g] = mm_tn(n2_group, v[n.grad_g], bf16)
    sync(n.s1, n.s2, n.n2_send, n.hidden, n.grad_u, n.gate_g)
    v[n.gate_part] = sum_near(v[n.gate_g], False)
    v[n.up_g] = mm_tn(n2_group, v[n.grad_u], bf16)
    v[n.s3] = across(v[n.n2_send][3], 3)
    sync(n.s3, n.hidden, n.up_g)
    v[n.up_part] = sum_near(v[n.up_g], False)
    n2_grad = add_shares(n2_grad_parts[0], (v[n.s1], v[n.s2], v[n.s3]))
    h1_grad_part, gain_two_grad = normed_grad(h1, gain_two, n2_grad)
    h1_grad = dy_own.astype(f32) + h1_grad_part
    v[n.dmix] = h1_grad.astype(bf16)
    v[n.dmix1], v[n.dmix2] = two_of(v[n.dmix])
    v[n.down_g] = mm_tn(v[n.hidden], dy_group, bf16)
    sync(n.dmix, n.dmix1, n.dmix2, n.hidden, n.down_g)
    v[n.down_part] = sum_near(v[n.down_g], True)
    v[n.dmix3] = last_of(v[n.dmix])
    sync(n.dmix, n.dmix1, n.dmix2, n.dmix3)
    mix_grad = in_order([v[n.dmix], v[n.dmix1], v[n.dmix2], v[n.dmix3]])
    grad_gated = mm_nt(mix_grad, w_out)
    grad_o, grad_gate, later, beyond, v[n.start], decay_b, head_grad = mixer.call(
        gate_grad_kernel,
        ["rows", "rows", "rows", "rows", "whole", "tokens", "blocks"],
        [grad_gated, proj, mixed, sums, gain_head, meta, rows],
        [
            ("rows", (rows_all, VAL), bf16),
            ("rows", (rows_all, VAL), bf16),
            ("blocks", (count,) + state_shape, bf16),
            ("blocks", (count, 1, KEY), f32),
            ("whole", state_shape, bf16),
            ("whole", (1, KEY), f32),
            ("whole", (1, VAL), f32),
        ],
        scratch,
        reverse=True,
        flops=2 * rows_all * KEY * VAL,
    )
    sync(n.start, n.hidden)
    y_parts = mm(v[n.hidden], w_down).reshape(4, tokens, width)
    v[n.y_send] = shares(y_parts)
    v[n.leaving] = from_later(v[n.start], decay_b)
    v[n.out_g] = mm_tn(gated, mix_grad, bf16)
    sync(n.leaving, n.y_send, n.out_g, n.gate_part)
    v[n.gate_other] = other_half(v[n.gate_part])
    v[n.y1], v[n.y2] = across(v[n.y_send][1], 1), across(v[n.y_send][2], 2)
    add(n.out_g__c)
    leaving = v[n.leaving]
    v[n.grad_proj], rank_grad, bias_grad = mixer.call(
        inputs_grad_kernel,
        ["rows"] * 5 + ["blocks", "blocks", "whole", "blocks", "blocks", "whole", "whole", "tokens", "blocks"],
        [
            proj,
            sums,
            raw,
            grad_o,
            grad_gate,
            prior,
            through,
            entering,
            later,
            beyond,
            leaving,
            up_head,
            meta,
            rows,
        ],
        [
            ("rows", proj.shape, bf16),
            ("whole", (LANES, KEY), f32),
            ("whole", (1, KEY), f32),
        ],
        flops=2 * rows_all * (3 * KEY * VAL + SPAN * (3 * KEY + 2 * VAL)),
    )
    n1_grad_all = mm_nt(v[n.grad_proj], w_in)
    n1_grad_parts = n1_grad_all.reshape(4, tokens, width)
    v[n.n1_send] = shares(n1_grad_parts)
    sync(n.n1_send, n.grad_proj, n.y1, n.y2, n.y_send, n.out_g, n.out_g__c, n.gate_other, n.up_part)
    v[n.up_other] = other_half(v[n.up_part])
    v[n.t1], v[n.t2] = across(v[n.n1_send][1], 1), across(v[n.n1_send][2], 2)
    v[n.y3] = across(v[n.y_send][3], 3)
    add(n.out_g__y0, n.out_g__y1)
    x_all = x_group.astype(f32)
    x_scale = lax.rsqrt(jnp.mean(x_all * x_all, axis=-1, keepdims=True) + EPS)
    gain_one_grad = jnp.sum(n1_grad_all * (x_all * x_scale), axis=0)
    each = width // devices
    decay_part = jnp.concatenate([rank_grad[:RANK], bias_grad], axis=0)
    decay_part = decay_part.reshape(RANK + 1, KEY // up_cols, up_cols).transpose(1, 0, 2)
    decay_part = decay_part.reshape(KEY // up_cols, -1)
    spare = -(-decay_part.shape[1] // each)
    decay_part = jnp.pad(decay_part, ((0, 0), (0, spare * each - decay_part.shape[1])))
    decay_part = decay_part.reshape(KEY // up_cols * each, spare)
    head_slot = lax.broadcasted_iota(jnp.int32, (HEADS, 1, 1), 0) == place
    decay_part = jnp.where(head_slot, decay_part[None], 0.0).reshape(width, spare)
    head_part = head_grad.reshape(devices, -1)
    head_each = head_part.shape[1]
    head_part = jnp.pad(head_part, ((0, 0), (0, each - head_each))).reshape(width)
    singles = jnp.stack([gain_one_grad, gain_two_grad, head_part], axis=1)
    extras = jnp.concatenate([singles, decay_part], axis=1)
    first = RANKS + RANK
    extras = jnp.pad(extras, ((0, 0), (first, RANKS + LANES - first - extras.shape[1])))
    v[n.inp_g] = (mm_tn(n1, v[n.grad_proj]) + extras).astype(bf16)
    sync(n.n1_send, n.t1, n.t2, n.inp_g, n.out_g__y0, n.out_g__y1, n.out_g, n.y3)
    v[n.t3] = across(v[n.n1_send][3], 3)
    add(n.inp_g__c)
    sync(n.inp_g, n.inp_g__c)
    add(n.inp_g__y0, n.inp_g__y1)
    sync(n.t3, n.gate_other, n.gate_part, n.up_other, n.up_part, n.down_part, n.out_g, n.out_g__y0)
    v[n.gate_back] = return_columns(sum_halves(v[n.gate_part], v[n.gate_other]), place)
    v[n.up_back] = return_columns(sum_halves(v[n.up_part], v[n.up_other]), place)
    v[n.down_other] = other_half(v[n.down_part])
    add(n.out_g__f)
    n1_grad = add_shares(n1_grad_parts[0], (v[n.t1], v[n.t2], v[n.t3]))
    input_part, _ = normed_grad(x_own.astype(f32), gain_one, n1_grad)
    input_grad = (h1_grad + input_part).reshape(1, tokens, width)
    sync(n.inp_g, n.inp_g__y0, n.gate_back, n.up_back, n.y1, n.y2, n.y3)
    add(n.inp_g__f)
    y = add_shares(y_parts[0], (v[n.y1], v[n.y2], v[n.y3]))
    result = h1 + y
    block_out = result.astype(bf16).reshape(1, tokens, width)
    kept = valid_mask.reshape(tokens, 1).astype(f32)
    squares = jnp.stack(
        [jnp.sum(kept * result * result), jnp.sum(kept * mix * mix), jnp.sum(kept * y * y)]
    )
    squares = sum_group(jnp.pad(squares, (0, 125)).reshape(1, 128), ("p", "q"))
    v[n.squares] = sum_group(squares, ("y", "c"))
    sync(n.inp_g__f, n.inp_g__y1, n.inp_g, n.out_g, n.out_g__f, n.squares, n.down_other)
    v[n.squares] = sum_over(v[n.squares], "h")
    gate_back, up_back = v[n.gate_back], v[n.up_back]
    in_back = return_columns(live.summed(n.inp), place)
    down_sum = sum_halves(v[n.down_part], v[n.down_other])
    v[n.ffnout] = lax.ppermute(down_sum.astype(bf16), AXES, inverse(down_moves))
    outproj_grad = lax.ppermute(live.summed(n.out).astype(bf16), AXES, inverse(out_moves))
    ffnout_grad = v[n.ffnout]
    ffnout_grad, outproj_grad = ffnout_grad.astype(f32), outproj_grad.astype(f32)
    ffnin_grad = jnp.concatenate(gate_back + up_back, axis=1)
    inproj_grad = jnp.concatenate(
        [part[:, :KEYS] for part in in_back]
        + [part[:, KEYS:VALUES] for part in in_back]
        + [part[:, VALUES:GATES] for part in in_back]
        + [part[:, GATES:RANKS] for part in in_back]
        + [sum(part[:, RANKS : RANKS + RANK] for part in in_back)],
        axis=1,
    )
    squares = v[n.squares].reshape(-1)[:3]
    root_means = jnp.sqrt(squares / (jnp.maximum(valid_count, 1.0) * width))
    spares = sum(part[:, first:] for part in in_back)
    mixgain_grad, ffngain_grad = spares[:, 0], spares[:, 1]
    headgain_grad = spares[:head_each, 2]
    decay_own = spares[:, 3 : 3 + spare].reshape(-1)[: (RANK + 1) * up_cols]
    decay_own = decay_own.reshape(RANK + 1, up_cols)
    return (
        block_out,
        input_grad,
        inproj_grad,
        outproj_grad,
        decay_own[:RANK],
        decay_own[RANK],
        mixgain_grad,
        headgain_grad,
        ffnin_grad,
        ffnout_grad,
        ffngain_grad,
        root_means,
    )


def mm_nt(left, right, out=f32):
    return dot_nt(left, right).astype(out)


def solution(mesh):
    dp, seq = mesh.shape["dp"], mesh.shape["seq"]
    fine = Mesh(mesh.devices.reshape(dp // 2, 2, seq // 4, 2, 2), AXES)
    batch, spread, whole = ("y", "c"), ("h", "p", "q"), AXES
    placed = (
        P(batch, spread, None),
        P(whole, None),
        P(whole, None),
        P(None, whole),
        P(whole),
        P(whole),
        P(whole),
        P(whole, None),
        P(whole, None),
        P(whole),
        P(batch, spread, None),
        P(batch, spread),
        P(batch, spread),
    )
    return jax.shard_map(
        local,
        mesh=fine,
        in_specs=placed,
        out_specs=(
            P(batch, spread, None),
            P(batch, spread, None),
            P(whole, None),
            P(whole, None),
            P(None, whole),
            P(whole),
            P(whole),
            P(whole),
            P(whole, None),
            P(whole, None),
            P(whole),
            P(),
        ),
        check_vma=False,
    )
```

```python
import jax
import jax.numpy as jnp
from jax import lax
from jax.experimental import pallas as pl
from jax.experimental.pallas import tpu as pltpu
from jax.sharding import Mesh, PartitionSpec as P

HEADS = 4
KEY = 256
VAL = 512
SPAN = 64
RANK = 16
LANES = 128
EPS = 1e-05
FLOOR = 1.0
QSCALE = KEY**-0.5
KEYS, VALUES, GATES, RANKS = KEY, 2 * KEY, 2 * KEY + VAL, 2 * KEY + 2 * VAL

AXES = ("y", "c", "h", "p", "q")
COPIES = ("y", "c", "h")


bf16 = jnp.bfloat16
f32 = jnp.float32


def after(value, *deps):
    return lax.optimization_barrier((value, deps))[0]


def together(*values):
    return lax.optimization_barrier(values)


def swap(value, axis):
    return lax.ppermute(value, axis, [(0, 1), (1, 0)])


def across(value, mask, group=("p", "q")):
    return lax.ppermute(value, group, [(i, i ^ mask) for i in range(4)])


def two_of(value, group=("p", "q")):
    return across(value, 1, group), across(value, 2, group)


def last_of(value, group=("p", "q")):
    return across(value, 3, group)


def shares(parts):
    return [parts[mask].astype(bf16) for mask in range(4)]


def add_shares(own, received):
    return own + received[0].astype(f32) + received[1].astype(f32) + received[2].astype(f32)


def half_swap(block):
    return swap(block, "h") if binary_copies() else block


def stack_axis(value, axis):
    if lax.axis_size(axis) != 2:
        return lax.all_gather(value, axis)
    other = swap(value, axis)
    first = lax.axis_index(axis) == 0
    return jnp.where(first, jnp.stack([value, other]), jnp.stack([other, value]))


def sum_over(value, axis):
    if lax.axis_size(axis) == 2:
        return value + swap(value, axis)
    return lax.psum(value, axis)


def sum_group(value, axes):
    if any(lax.axis_size(axis) != 2 for axis in axes):
        return lax.psum(value, axes)
    return value + across(value, 1, axes) + across(value, 2, axes) + across(value, 3, axes)


def binary_copies():
    return all(lax.axis_size(axis) == 2 for axis in COPIES)


def lay_kernel(offsets, pieces, count, *refs):
    blocks, whole, sems = refs[:count], refs[count], refs[count + 1]
    copies = []
    for i, (block, first, rows) in enumerate(pieces):
        place = pl.ds(pl.multiple_of(offsets[i], 16), rows)
        copies.append(
            pltpu.make_async_copy(
                blocks[block].at[pl.ds(first, rows)], whole.at[place], sems.at[i]
            )
        )
    for copy in copies:
        copy.start()
    for copy in copies:
        copy.wait()


def lay(blocks, pieces, offsets):
    cols, kind = blocks[0].shape[1], blocks[0].dtype
    total = sum(rows for _, _, rows in pieces)
    return pl.pallas_call(
        lambda offsets, *refs: lay_kernel(offsets, pieces, len(blocks), *refs),
        grid_spec=pltpu.PrefetchScalarGridSpec(
            num_scalar_prefetch=1,
            grid=(1,),
            in_specs=[pl.BlockSpec(memory_space=pl.ANY)] * len(blocks),
            out_specs=pl.BlockSpec(memory_space=pl.ANY),
            scratch_shapes=[pltpu.SemaphoreType.DMA((len(pieces),))],
        ),
        out_shape=jax.ShapeDtypeStruct((total, cols), kind),
        compiler_params=pltpu.CompilerParams(vmem_limit_bytes=16 * 1024 * 1024),
        cost_estimate=pl.CostEstimate(
            flops=0, bytes_accessed=2 * total * cols * kind.itemsize, transcendentals=0
        ),
    )(jnp.stack(offsets).astype(jnp.int32), *blocks)


def in_order(blocks):
    rows = blocks[0].shape[0]
    pieces = [(i, 0, rows) for i in range(len(blocks))]
    return lay(blocks, pieces, [jnp.int32(i * rows) for i in range(len(blocks))])


def pick(value, index, axis):
    return lax.dynamic_index_in_dim(value, index, axis, keepdims=False)


class Names:
    def __getattr__(self, name):
        return name


n = Names()


class Live:
    def __init__(self, **values):
        self.v = dict(values)
        self.binary = binary_copies()
        self.at = {axis: lax.axis_index(axis) for axis in AXES}

    def sync(self, *names):
        self.v.update(zip(names, lax.optimization_barrier([self.v[name] for name in names])))

    def swap(self, name, value, axis):
        self.v[name] = swap(value(), axis) if self.binary else jnp.zeros((8, 128), bf16)

    def send(self, *names):
        for name in names:
            weight, way = name.split("__")
            source = weight if len(way) == 1 else weight + "__" + way[:-1]
            axis = "h" if way[-1] == "f" else way[-1]
            self.swap(name, lambda: self.v[source], axis)

    def gathered(self, weight):
        own = self.v[weight]
        if not self.binary:
            return lax.all_gather(own, COPIES, axis=0, tiled=True)
        rows, blocks, pieces, offsets = own.shape[0], [], [], []
        for way in ("", "y", "c", "yc", "f", "fy", "fc", "fyc"):
            y, c = self.at["y"] ^ ("y" in way), self.at["c"] ^ ("c" in way)
            f = self.at["h"] ^ ("f" in way)
            place = f * 4 + y * 2 + c if weight == n.out else y * 4 + c * 2 + f
            pieces.append((len(blocks), 0, rows))
            offsets.append(place * rows)
            blocks.append(self.v[weight + "__" + way] if way else own)
        return lay(blocks, pieces, offsets)

    def near(self, weight, y, f):
        c, total = self.at["c"], 0.0
        for value in (self.v[weight + "_g"], self.v[weight + "_g__c"]):
            rows, cols = value.shape
            place = f * 4 + y * 2 + c if weight == n.out else y * 4 + c * 2 + f
            value = lax.dynamic_slice_in_dim(value, place * (rows // 8), rows // 8, 0)
            total = total + value.astype(f32)
        return total

    def add(self, *names):
        for name in names:
            weight, way = name.split("_g__")
            y, f = self.at["y"], self.at["h"]
            if way == "c":
                self.swap(name, lambda: self.v[weight + "_g"], "c")
            elif way in ("y0", "y1"):
                which = 1 - f if way == "y0" else f
                self.swap(name, lambda: self.near(weight, 1 - y, which).astype(bf16), "y")
            else:
                first = weight + "_g__y0"
                self.swap(
                    name,
                    lambda: (self.near(weight, y, 1 - f) + self.v[first].astype(f32)).astype(bf16),
                    "h",
                )

    def summed(self, weight):
        grad = weight + "_g"
        if not self.binary:
            return lax.psum_scatter(
                self.v[grad], COPIES, scatter_dimension=0, tiled=True
            ).astype(f32)
        value = self.near(weight, self.at["y"], self.at["h"])
        return value + self.v[grad + "__y1"].astype(f32) + self.v[grad + "__f"].astype(f32)


def share_columns(weight, place, columns, group=("p", "q")):
    pieces = [columns(weight, t) for t in range(4)]
    got = []
    for mask in range(4):
        piece = lax.select_n(place, *[pieces[t ^ mask] for t in range(4)])
        got.append(piece if mask == 0 else across(piece, mask, group))
    return jnp.concatenate(
        [lax.select_n(place, *[got[t ^ spot] for t in range(4)]) for spot in range(4)]
    )


def return_columns(grad, place, group=("p", "q")):
    value = grad.reshape(4, grad.shape[0] // 4, grad.shape[1])
    got = [pick(value, place, 0).astype(f32)]
    for mask in (1, 2, 3):
        got.append(across(pick(value, place ^ mask, 0).astype(bf16), mask, group).astype(f32))
    return [lax.select_n(place, *[got[t ^ spot] for t in range(4)]) for spot in range(4)]


def both_halves(own, other):
    first = lax.axis_index("h") == 0
    return jnp.where(first, jnp.concatenate([own, other]), jnp.concatenate([other, own]))


def gather_halves(own, other, tall):
    if not binary_copies():
        return lax.all_gather(own, COPIES, axis=0, tiled=True)
    both = both_halves(own, other)
    if not tall:
        return lax.all_gather(both, ("y", "c"), axis=0, tiled=True)
    both = both.reshape(2, -1, own.shape[1])
    return lax.all_gather(both, ("y", "c"), axis=1, tiled=True).reshape(-1, own.shape[1])


def sum_near(grad, tall):
    if not binary_copies():
        return lax.psum_scatter(grad, COPIES, scatter_dimension=0, tiled=True)
    cols = grad.shape[1]
    if tall:
        grad = grad.reshape(2, -1, cols)
        return lax.psum_scatter(grad, ("y", "c"), scatter_dimension=1, tiled=True)
    return lax.psum_scatter(grad, ("y", "c"), scatter_dimension=0, tiled=True).reshape(2, -1, cols)


def other_half(part):
    if not binary_copies():
        return jnp.zeros((8, 128), bf16)
    return swap(pick(part, 1 - lax.axis_index("h"), 0), "h")


def sum_halves(part, other):
    if not binary_copies():
        return part.astype(f32)
    return pick(part, lax.axis_index("h"), 0).astype(f32) + other.astype(f32)


def row_owner_moves():
    total = 1
    for axis in AXES:
        total *= lax.axis_size(axis)
    if not binary_copies():
        copies = total // 4
        return [(g, (g % copies) * 4 + g // copies) for g in range(total)]
    pairs = []
    for g in range(total):
        y, c, h, p, q = (g >> bit & 1 for bit in (4, 3, 2, 1, 0))
        to = (p, q, h, y, c)
        pairs.append((g, sum(bit << (4 - i) for i, bit in enumerate(to))))
    return pairs


def dot_nn(a, b):
    return lax.dot_general(a, b, (((1,), (0,)), ((), ())), preferred_element_type=f32)


def dot_nt(a, b):
    return lax.dot_general(a, b, (((1,), (1,)), ((), ())), preferred_element_type=f32)


def dot_tn(a, b):
    return lax.dot_general(a, b, (((0,), (0,)), ((), ())), preferred_element_type=f32)


def two_parts(value):
    high = value.astype(bf16)
    return high, (value - high.astype(f32)).astype(bf16)


def triangle(lower):
    row = lax.broadcasted_iota(jnp.int32, (SPAN, SPAN), 0)
    col = lax.broadcasted_iota(jnp.int32, (SPAN, SPAN), 1)
    return jnp.where(row >= col if lower else row <= col, 1.0, 0.0)


def running_sum(value, lower):
    ones = triangle(lower).astype(bf16)
    high, low = two_parts(value)
    return dot_nn(ones, high) + dot_nn(ones, low)


def pair_mask(meta, rows):
    return jnp.where(meta[:, 0:1] == rows[0:1, :], triangle(True), 0.0)


def states_kernel(
    place, proj, up, bias, meta, rows, sums, raw, prior, through, end, decay, state, total
):
    @pl.when(pl.program_id(0) == 0)
    def _():
        state[...] = jnp.zeros_like(state)
        total[...] = jnp.ones_like(total)

    keys = proj[:, KEYS:VALUES].astype(bf16).astype(f32)
    gate = dot_nn(proj[:, RANKS:].astype(bf16), up[...]) + bias[...]
    log_decay = (jnp.minimum(gate, 0.0) - jnp.log1p(jnp.exp(-jnp.abs(gate)))) * (1.0 / 16.0)
    run = running_sum(log_decay, True)
    raw[...] = gate
    sums[...] = run
    last = run[SPAN - 1 :, :]
    info = meta[...]
    k_final = (keys * jnp.exp(last - run) * (info[:, 1:2] * info[:, 3:4])).astype(bf16)
    step = rows[0, 1:2, 0:1] * jnp.exp(last)
    prior[0] = state[...].astype(bf16)
    through[0] = total[...]
    state[...] = step * state[...] + dot_tn(proj[:, VALUES:GATES].astype(bf16), k_final)
    total[...] = step * total[...]
    end[...] = state[...].astype(bf16)
    decay[...] = total[...]


def mixed_kernel(place, proj, sums, prior, through, entering, gain, meta, rows, gated, mixed):
    info = meta[...]
    run = sums[...]
    query = proj[:, :KEYS].astype(bf16).astype(f32)
    q_decay = (query * QSCALE * jnp.exp(run)).astype(bf16)
    k_decay = (proj[:, KEYS:VALUES].astype(bf16).astype(f32) * info[:, 1:2] * jnp.exp(-run)).astype(bf16)
    scores = (dot_nt(q_decay, k_decay) * pair_mask(info, rows[0])).astype(bf16)
    state = (prior[0].astype(f32) + through[0] * entering[...].astype(f32)).astype(bf16)
    out = dot_nn(scores, proj[:, VALUES:GATES].astype(bf16)) + info[:, 2:3] * dot_nt(q_decay, state)
    mixed[...] = out
    gate = proj[:, GATES:RANKS]
    scale = lax.rsqrt(jnp.mean(out * out, axis=-1, keepdims=True) + FLOOR)
    gated[...] = (out * scale * gain[...] * gate * jax.nn.sigmoid(gate)).astype(bf16)


def gate_grad_kernel(
    place,
    grad_gated,
    proj,
    mixed,
    sums,
    gain,
    meta,
    rows,
    grad_out,
    grad_gate,
    later,
    beyond,
    start,
    decay,
    grad_gain,
    state,
    total,
):
    @pl.when(pl.program_id(0) == 0)
    def _():
        state[...] = jnp.zeros_like(state)
        total[...] = jnp.ones_like(total)
        grad_gain[...] = jnp.zeros_like(grad_gain)

    info = meta[...]
    run = sums[...]
    out = mixed[...]
    gate = proj[:, GATES:RANKS]
    grad = grad_gated[...]
    sig = jax.nn.sigmoid(gate)
    scale = lax.rsqrt(jnp.mean(out * out, axis=-1, keepdims=True) + FLOOR)
    scaled = out * scale
    swish = gate * sig
    weighted = grad * gain[...] * swish
    inner = jnp.mean(scaled * weighted, axis=-1, keepdims=True)
    grad_o = (scale * (weighted - scaled * inner)).astype(bf16)
    grad_out[...] = grad_o
    grad_gate[...] = (grad * scaled * gain[...] * sig * (1.0 + gate * (1.0 - sig))).astype(bf16)
    grad_gain[...] += jnp.sum(grad * scaled * swish, axis=0, keepdims=True)
    query = proj[:, :KEYS].astype(bf16).astype(f32)
    q_enter = (query * QSCALE * jnp.exp(run)).astype(bf16)
    o_enter = jnp.where(info[:, 2:3] > 0.0, grad_o.astype(f32), 0.0).astype(bf16)
    step = rows[0, 1:2, 0:1] * jnp.exp(run[SPAN - 1 :, :])
    later[0] = state[...].astype(bf16)
    beyond[0] = total[...]
    state[...] = step * state[...] + dot_tn(o_enter, q_enter)
    total[...] = step * total[...]
    start[...] = state[...].astype(bf16)
    decay[...] = total[...]


def inputs_grad_kernel(
    place,
    proj,
    sums,
    raw,
    grad_out,
    grad_gate,
    prior,
    through,
    entering,
    later,
    beyond,
    leaving,
    up,
    meta,
    rows,
    grad_proj,
    grad_up,
    grad_bias,
):
    @pl.when(pl.program_id(0) == 0)
    def _():
        grad_up[...] = jnp.zeros_like(grad_up)
        grad_bias[...] = jnp.zeros_like(grad_bias)

    info = meta[...]
    run = sums[...]
    last = run[SPAN - 1 :, :]
    valid, enter, carry = info[:, 1:2], info[:, 2:3], info[:, 3:4]
    grow, shrink, tail = jnp.exp(run), jnp.exp(-run), jnp.exp(last - run) * carry
    query = proj[:, :KEYS].astype(bf16).astype(f32)
    keys = proj[:, KEYS:VALUES].astype(bf16).astype(f32) * valid
    values = proj[:, VALUES:GATES].astype(bf16)
    q_decay = (query * QSCALE * grow).astype(bf16)
    k_decay = (keys * shrink).astype(bf16)
    k_final = (keys * tail).astype(bf16)
    mask = pair_mask(info, rows[0])
    state = prior[0].astype(f32) + through[0] * entering[...].astype(f32)
    state_grad = later[0].astype(f32) + beyond[0] * leaving[...].astype(f32)
    state_b, state_grad_b = state.astype(bf16), state_grad.astype(bf16)
    grad_o = grad_out[...]
    scores = (dot_nt(q_decay, k_decay) * mask).astype(bf16)
    grad_scores = (dot_nt(grad_o, values) * mask).astype(bf16)
    grad_v = dot_tn(scores, grad_o) + dot_nt(k_final, state_grad_b)
    grad_qd = dot_nn(grad_scores, k_decay) + enter * dot_nn(grad_o, state_b)
    grad_kd = dot_tn(grad_scores, q_decay)
    grad_kf = dot_nn(values, state_grad_b)
    step = rows[0, 1:2, 0:1] * jnp.exp(last)
    through_last = step * jnp.sum(state * state_grad, axis=0, keepdims=True)
    final_part = grad_kf * k_final.astype(f32)
    grad_run = grad_qd * q_decay.astype(f32) - grad_kd * k_decay.astype(f32) - final_part
    grad_last = through_last + jnp.sum(final_part, axis=0, keepdims=True)
    grad_log = running_sum(grad_run, False) + grad_last
    grad_raw = grad_log * jax.nn.sigmoid(-raw[...]) * (1.0 / 16.0)
    high, low = two_parts(grad_raw)
    rank = proj[:, RANKS:].astype(bf16)
    grad_up[...] += dot_tn(rank, high) + dot_tn(rank, low)
    grad_bias[...] += jnp.sum(grad_raw, axis=0, keepdims=True)
    grad_rank = dot_nt(high, up[...]) + dot_nt(low, up[...])
    grad_k = (grad_kd * shrink + grad_kf * tail) * valid
    grad_proj[:, KEYS:VALUES] = grad_k.astype(bf16)
    grad_proj[:, VALUES:GATES] = grad_v.astype(bf16)
    grad_proj[:, RANKS:] = grad_rank.astype(bf16)
    grad_proj[:, :KEYS] = (grad_qd * grow * QSCALE).astype(bf16)
    grad_proj[:, GATES:RANKS] = grad_gate[...]


class Mixer:
    def __init__(self, place, blocks, per_device):
        self.place = place.reshape(1)
        self.blocks = blocks
        self.per_device = per_device

    def call(self, kernel, specs, args, outs, scratch=(), reverse=False, flops=0):
        count, per_device = self.blocks, self.per_device

        def at(step):
            return count - 1 - step if reverse else step

        def spec(kind, shape):
            if kind == "rows":
                return pl.BlockSpec(
                    (SPAN, shape[1]),
                    lambda n, place: (
                        lax.bitwise_xor(at(n) // per_device, place[0]) * per_device
                        + at(n) % per_device,
                        0,
                    ),
                )
            if kind == "tokens":
                return pl.BlockSpec((SPAN, shape[1]), lambda n, place: (at(n), 0))
            if kind == "blocks":
                return pl.BlockSpec((1,) + shape[1:], lambda n, place: (at(n), 0, 0))
            return pl.BlockSpec(shape, lambda n, place: (0,) * len(shape))

        size = sum(a.size * a.dtype.itemsize for a in args)
        return pl.pallas_call(
            kernel,
            grid_spec=pltpu.PrefetchScalarGridSpec(
                num_scalar_prefetch=1,
                grid=(count,),
                in_specs=[spec(kind, a.shape) for kind, a in zip(specs, args)],
                out_specs=[spec(kind, shape) for kind, shape, _ in outs],
                scratch_shapes=list(scratch),
            ),
            out_shape=[jax.ShapeDtypeStruct(shape, kind) for _, shape, kind in outs],
            compiler_params=pltpu.CompilerParams(
                dimension_semantics=("arbitrary",), vmem_limit_bytes=48 * 1024 * 1024
            ),
            cost_estimate=pl.CostEstimate(
                flops=flops, bytes_accessed=2 * size, transcendentals=4 * SPAN * KEY * count
            ),
        )(self.place, *args)


def normed(values, gain):
    return values * lax.rsqrt(jnp.mean(values * values, axis=-1, keepdims=True) + EPS) * gain


def normed_grad(values, gain, grad):
    scale = lax.rsqrt(jnp.mean(values * values, axis=-1, keepdims=True) + EPS)
    weighted = grad * gain
    inner = jnp.mean(weighted * values, axis=-1, keepdims=True)
    return (
        scale * weighted - scale * scale * scale * values * inner,
        jnp.sum(grad * values * scale, axis=0),
    )


def mm(left, right, out=f32):
    return jnp.dot(left, right, preferred_element_type=f32).astype(out)


def mm_tn(left, right, out=f32):
    return dot_tn(left, right).astype(out)


def in_columns(weight, t):
    wide, tall = HEADS * KEY, HEADS * VAL
    starts = [(0, KEY), (wide, KEY), (2 * wide, VAL), (2 * wide + tall, VAL)]
    heads = [weight[:, start + t * size : start + (t + 1) * size] for start, size in starts]
    rank = weight[:, 2 * wide + 2 * tall :]
    return jnp.concatenate(heads + [jnp.pad(rank, ((0, 0), (0, LANES - RANK)))], axis=1)


def from_earlier(end, decay):
    count = lax.axis_size("h")
    if count == 2:
        return lax.ppermute(end, "h", [(0, 1)])
    ends, decays = lax.all_gather(end, "h"), lax.all_gather(decay, "h")
    mine = lax.axis_index("h")
    state = jnp.zeros(end.shape, f32)
    for h in range(count - 1):
        state = jnp.where(h < mine, decays[h] * state + ends[h].astype(f32), state)
    return state.astype(bf16)


def from_later(start, decay):
    count = lax.axis_size("h")
    if count == 2:
        return lax.ppermute(start, "h", [(1, 0)])
    starts, decays = lax.all_gather(start, "h"), lax.all_gather(decay, "h")
    mine = lax.axis_index("h")
    state = jnp.zeros(start.shape, f32)
    for h in range(count - 1, 0, -1):
        state = jnp.where(h > mine, decays[h] * state + starts[h].astype(f32), state)
    return state.astype(bf16)


def local(
    hidden_in,
    in_weight,
    out_weight,
    decay_up,
    decay_bias,
    mixer_gain,
    head_gain,
    ffn_in,
    ffn_out,
    ffn_gain,
    out_grad,
    seg_ids,
    valid_mask,
):
    tokens, width = hidden_in.shape[1:]
    place = 2 * lax.axis_index("p") + lax.axis_index("q")
    half = lax.axis_index("h")
    sizes = [lax.axis_size(axis) for axis in AXES]
    devices = sizes[0] * sizes[1] * sizes[2] * 4
    me = place
    stride = 4
    for axis in ("h", "c", "y"):
        me = me + stride * lax.axis_index(axis)
        stride *= lax.axis_size(axis)
    ff = ffn_in.shape[1] // 2
    quarter = ff // 4
    rows_all = 4 * tokens
    count = rows_all // SPAN
    x_own = hidden_in.reshape(tokens, width)
    dy_own = out_grad.reshape(tokens, width)

    small = [
        decay_up.reshape(-1),
        decay_bias,
        mixer_gain,
        head_gain,
        ffn_gain,
        seg_ids.reshape(-1).astype(bf16),
        valid_mask.reshape(-1).astype(bf16),
    ]
    lengths = [part.shape[0] for part in small]
    packed = jnp.concatenate(small)
    padded = -(-packed.shape[0] // 1024) * 1024
    packed = jnp.pad(packed, (0, padded - packed.shape[0])).reshape(-1, 128)
    offset = [sum(lengths[:i]) for i in range(len(lengths) + 1)]

    def gateup_columns(weight, t):
        return jnp.concatenate(
            [
                weight[:, t * quarter : (t + 1) * quarter],
                weight[:, ff + t * quarter : ff + (t + 1) * quarter],
            ],
            axis=1,
        )

    def inverse(pairs):
        return [(b, a) for a, b in pairs]

    out_moves, down_moves = row_owner_moves(), row_owner_moves()
    live = Live(x=x_own, dy=dy_own, ffn_in=ffn_in, ffn_out=ffn_out, out_weight=out_weight)
    v, sync, send, add = live.v, live.sync, live.send, live.add

    v[n.inp] = share_columns(in_weight, place, in_columns)
    for axis in ("q", "p", "c", "y"):
        packed = stack_axis(packed, axis)
    sync(n.inp, n.out_weight, n.ffn_in)
    send(n.inp__f, n.inp__y, n.inp__c)
    v[n.gateup] = share_columns(v[n.ffn_in], place, gateup_columns)
    v[n.out] = lax.ppermute(v[n.out_weight], AXES, out_moves)
    v[n.packed] = packed
    sync(n.inp__f, n.inp__y, n.inp__c, n.x, n.out, n.packed)
    send(n.inp__fy, n.inp__fc, n.inp__yc)
    v[n.x1], v[n.x2] = two_of(v[n.x])
    v[n.x3] = last_of(v[n.x])
    send(n.out__f, n.out__y, n.out__c)
    v[n.packed] = jnp.moveaxis(stack_axis(v[n.packed], "h"), 0, 2)
    sync(n.inp__fy, n.inp__fc, n.inp__yc, n.x1, n.x2, n.x3, n.out__f, n.out__y, n.out__c, n.gateup, n.packed)
    send(n.inp__fyc, n.out__fy, n.out__fc, n.out__yc)
    v[n.gate], v[n.up] = v[n.gateup][:, :quarter], v[n.gateup][:, quarter:]
    v[n.gate__f] = half_swap(v[n.gate])
    sync(n.inp__fyc, n.out__fy, n.out__fc, n.out__yc, n.gate, n.up, n.ffn_out, n.dy)
    send(n.out__fyc)
    packed = v[n.packed]
    everyone = packed.reshape(sizes[0], sizes[1], -1, padded)

    def small_part(i):
        return everyone[..., offset[i] : offset[i + 1]]

    up_cols = decay_up.shape[1]
    up_all = small_part(0).reshape(devices, RANK, up_cols).transpose(1, 0, 2).reshape(RANK, HEADS, KEY)
    up_head = jnp.pad(pick(up_all, place, 1), ((0, LANES - RANK), (0, 0)))
    bias_head = pick(small_part(1).reshape(HEADS, 1, KEY), place, 0).astype(f32)
    gain_one = small_part(2).reshape(-1).astype(f32)
    gain_head = small_part(3).reshape(1, -1).astype(f32)
    gain_two = small_part(4).reshape(-1).astype(f32)

    def of_sequence(value):
        return pick(pick(value, lax.axis_index("y"), 0), lax.axis_index("c"), 0).reshape(-1)

    seg_all = of_sequence(small_part(5)).astype(f32)
    valid_all = of_sequence(small_part(6)).astype(f32)
    valid_count = jnp.sum(small_part(6).astype(f32))
    seg_here = lax.dynamic_slice(
        jnp.concatenate([jnp.full((1,), -1.0, f32), seg_all]), (half * rows_all,), (rows_all + 1,)
    )
    valid_here = lax.dynamic_slice(valid_all, (half * rows_all,), (rows_all,))
    seg_blocks = seg_here[1:].reshape(count, SPAN)
    before = seg_here[:-1].reshape(count, SPAN)[:, :1]
    final = seg_blocks[:, -1:]
    meta = jnp.stack(
        [
            seg_here[1:],
            valid_here,
            (seg_blocks == before).astype(f32).reshape(-1),
            (seg_blocks == final).astype(f32).reshape(-1),
        ]
        + [jnp.zeros((rows_all,), f32)] * 4,
        axis=1,
    )
    keep = jnp.broadcast_to((final == before).astype(f32), (count, SPAN))
    rows = jnp.stack([seg_blocks, keep] + [jnp.zeros((count, SPAN), f32)] * 6, axis=1)

    x_group = in_order([x_own, v[n.x1], v[n.x2], v[n.x3]])
    w_in = live.gathered(n.inp)
    n1 = normed(x_group.astype(f32), gain_one).astype(bf16)
    proj = mm(n1, w_in)
    mixer = Mixer(place, count, tokens // SPAN)
    state_shape = (VAL, KEY)
    scratch = [pltpu.VMEM(state_shape, f32), pltpu.VMEM((1, KEY), f32)]
    sums, raw, prior, through, v[n.end], decay = mixer.call(
        states_kernel,
        ["rows", "whole", "whole", "tokens", "blocks"],
        [proj, up_head, bias_head, meta, rows],
        [
            ("rows", (rows_all, KEY), f32),
            ("rows", (rows_all, KEY), f32),
            ("blocks", (count,) + state_shape, bf16),
            ("blocks", (count, 1, KEY), f32),
            ("whole", state_shape, bf16),
            ("whole", (1, KEY), f32),
        ],
        scratch,
        flops=2 * rows_all * KEY * VAL,
    )
    v[n.w_out] = live.gathered(n.out)
    sync(n.end, n.ffn_out, n.w_out)
    w_out = v[n.w_out]
    v[n.entering] = from_earlier(v[n.end], decay)
    v[n.down] = lax.ppermute(v[n.ffn_out], AXES, down_moves)
    entering = v[n.entering]
    sync(n.entering, n.gate, n.gate__f, n.up)
    v[n.up__f] = half_swap(v[n.up])
    w_gate = gather_halves(v[n.gate], v[n.gate__f], False)
    gated, mixed = mixer.call(
        mixed_kernel,
        ["rows", "rows", "blocks", "blocks", "whole", "whole", "tokens", "blocks"],
        [proj, sums, prior, through, entering, gain_head, meta, rows],
        [("rows", (rows_all, VAL), bf16), ("rows", (rows_all, VAL), f32)],
        flops=2 * rows_all * (KEY * VAL + SPAN * (KEY + VAL)),
    )
    mix_parts = mm(gated, w_out).reshape(4, tokens, width)
    mix_own = mix_parts[0]
    v[n.mix_send] = shares(mix_parts)
    sync(n.mix_send)
    v[n.mix1], v[n.mix2] = across(v[n.mix_send][1], 1), across(v[n.mix_send][2], 2)
    sync(n.mix1, n.mix2, n.mix_send, n.down, n.up, n.up__f)
    v[n.down__f] = half_swap(v[n.down])
    v[n.w_up] = gather_halves(v[n.up], v[n.up__f], False)
    v[n.w_gate] = w_gate
    v[n.mix3] = across(v[n.mix_send][3], 3)
    sync(n.mix3)
    mix = add_shares(mix_own, (v[n.mix1], v[n.mix2], v[n.mix3]))
    h1 = x_own.astype(f32) + mix
    v[n.n2] = normed(h1, gain_two).astype(bf16)
    v[n.n21], v[n.n22] = two_of(v[n.n2])
    sync(n.n21, n.n22, n.n2, n.dy, n.down, n.down__f, n.w_gate, n.w_up)
    w_gate, w_up = v[n.w_gate], v[n.w_up]
    w_down = gather_halves(v[n.down], v[n.down__f], True)
    v[n.n23] = last_of(v[n.n2])
    sync(n.n21, n.n22, n.n23, n.n2, n.dy)
    v[n.dy1], v[n.dy2] = two_of(v[n.dy])
    v[n.dy3] = last_of(v[n.dy])
    n2_group = in_order([v[n.n2], v[n.n21], v[n.n22], v[n.n23]])
    dy_group = in_order([dy_own, v[n.dy1], v[n.dy2], v[n.dy3]])
    gate = mm(n2_group, w_gate)
    up = mm(n2_group, w_up)
    grad_hidden = mm_nt(dy_group, w_down)

    sig = jax.nn.sigmoid(gate)
    hidden = (gate * sig * up).astype(bf16)
    grad_g = (grad_hidden * up * sig * (1.0 + gate * (1.0 - sig))).astype(bf16)
    grad_u = (grad_hidden * gate * sig).astype(bf16)
    n2_grad_parts = (mm_nt(grad_g, w_gate) + mm_nt(grad_u, w_up)).reshape(4, tokens, width)
    v[n.n2_send] = shares(n2_grad_parts)
    v[n.grad_g], v[n.grad_u], v[n.hidden] = grad_g, grad_u, hidden
    sync(n.n2_send, n.grad_g, n.grad_u, n.hidden)
    v[n.s1], v[n.s2] = across(v[n.n2_send][1], 1), across(v[n.n2_send][2], 2)
    v[n.gate_g] = mm_tn(n2_group, v[n.grad_g], bf16)
    sync(n.s1, n.s2, n.n2_send, n.hidden, n.grad_u, n.gate_g)
    v[n.gate_part] = sum_near(v[n.gate_g], False)
    v[n.up_g] = mm_tn(n2_group, v[n.grad_u], bf16)
    v[n.s3] = across(v[n.n2_send][3], 3)
    sync(n.s3, n.hidden, n.up_g)
    v[n.up_part] = sum_near(v[n.up_g], False)
    n2_grad = add_shares(n2_grad_parts[0], (v[n.s1], v[n.s2], v[n.s3]))
    h1_grad_part, gain_two_grad = normed_grad(h1, gain_two, n2_grad)
    h1_grad = dy_own.astype(f32) + h1_grad_part
    v[n.dmix] = h1_grad.astype(bf16)
    v[n.dmix1], v[n.dmix2] = two_of(v[n.dmix])
    v[n.down_g] = mm_tn(v[n.hidden], dy_group, bf16)
    sync(n.dmix, n.dmix1, n.dmix2, n.hidden, n.down_g)
    v[n.down_part] = sum_near(v[n.down_g], True)
    v[n.dmix3] = last_of(v[n.dmix])
    sync(n.dmix, n.dmix1, n.dmix2, n.dmix3)
    mix_grad = in_order([v[n.dmix], v[n.dmix1], v[n.dmix2], v[n.dmix3]])
    grad_gated = mm_nt(mix_grad, w_out)
    grad_o, grad_gate, later, beyond, v[n.start], decay_b, head_grad = mixer.call(
        gate_grad_kernel,
        ["rows", "rows", "rows", "rows", "whole", "tokens", "blocks"],
        [grad_gated, proj, mixed, sums, gain_head, meta, rows],
        [
            ("rows", (rows_all, VAL), bf16),
            ("rows", (rows_all, VAL), bf16),
            ("blocks", (count,) + state_shape, bf16),
            ("blocks", (count, 1, KEY), f32),
            ("whole", state_shape, bf16),
            ("whole", (1, KEY), f32),
            ("whole", (1, VAL), f32),
        ],
        scratch,
        reverse=True,
        flops=2 * rows_all * KEY * VAL,
    )
    sync(n.start, n.hidden)
    y_parts = mm(v[n.hidden], w_down).reshape(4, tokens, width)
    v[n.y_send] = shares(y_parts)
    v[n.leaving] = from_later(v[n.start], decay_b)
    v[n.out_g] = mm_tn(gated, mix_grad, bf16)
    sync(n.leaving, n.y_send, n.out_g, n.gate_part)
    v[n.gate_other] = other_half(v[n.gate_part])
    v[n.y1], v[n.y2] = across(v[n.y_send][1], 1), across(v[n.y_send][2], 2)
    add(n.out_g__c)
    leaving = v[n.leaving]
    v[n.grad_proj], rank_grad, bias_grad = mixer.call(
        inputs_grad_kernel,
        ["rows"] * 5 + ["blocks", "blocks", "whole", "blocks", "blocks", "whole", "whole", "tokens", "blocks"],
        [
            proj,
            sums,
            raw,
            grad_o,
            grad_gate,
            prior,
            through,
            entering,
            later,
            beyond,
            leaving,
            up_head,
            meta,
            rows,
        ],
        [
            ("rows", proj.shape, bf16),
            ("whole", (LANES, KEY), f32),
            ("whole", (1, KEY), f32),
        ],
        flops=2 * rows_all * (3 * KEY * VAL + SPAN * (3 * KEY + 2 * VAL)),
    )
    n1_grad_all = mm_nt(v[n.grad_proj], w_in)
    n1_grad_parts = n1_grad_all.reshape(4, tokens, width)
    v[n.n1_send] = shares(n1_grad_parts)
    sync(n.n1_send, n.grad_proj, n.y1, n.y2, n.y_send, n.out_g, n.out_g__c, n.up_part)
    v[n.up_other] = other_half(v[n.up_part])
    v[n.t1], v[n.t2] = across(v[n.n1_send][1], 1), across(v[n.n1_send][2], 2)
    v[n.y3] = across(v[n.y_send][3], 3)
    add(n.out_g__y0, n.out_g__y1)
    x_all = x_group.astype(f32)
    x_scale = lax.rsqrt(jnp.mean(x_all * x_all, axis=-1, keepdims=True) + EPS)
    gain_one_grad = jnp.sum(n1_grad_all * (x_all * x_scale), axis=0)
    each = width // devices
    decay_part = jnp.concatenate([rank_grad[:RANK], bias_grad], axis=0)
    decay_part = decay_part.reshape(RANK + 1, KEY // up_cols, up_cols).transpose(1, 0, 2)
    decay_part = decay_part.reshape(KEY // up_cols, -1)
    spare = -(-decay_part.shape[1] // each)
    decay_part = jnp.pad(decay_part, ((0, 0), (0, spare * each - decay_part.shape[1])))
    decay_part = decay_part.reshape(KEY // up_cols * each, spare)
    head_slot = lax.broadcasted_iota(jnp.int32, (HEADS, 1, 1), 0) == place
    decay_part = jnp.where(head_slot, decay_part[None], 0.0).reshape(width, spare)
    head_part = head_grad.reshape(devices, -1)
    head_each = head_part.shape[1]
    head_part = jnp.pad(head_part, ((0, 0), (0, each - head_each))).reshape(width)
    singles = jnp.stack([gain_one_grad, gain_two_grad, head_part], axis=1)
    extras = jnp.concatenate([singles, decay_part], axis=1)
    first = RANKS + RANK
    extras = jnp.pad(extras, ((0, 0), (first, RANKS + LANES - first - extras.shape[1])))
    v[n.inp_g] = (mm_tn(n1, v[n.grad_proj]) + extras).astype(bf16)
    sync(n.n1_send, n.t1, n.t2, n.inp_g, n.out_g__y0, n.out_g__y1, n.out_g, n.y3, n.gate_other)
    v[n.t3] = across(v[n.n1_send][3], 3)
    add(n.inp_g__c)
    sync(n.inp_g, n.inp_g__c)
    add(n.inp_g__y0, n.inp_g__y1)
    sync(n.t3, n.gate_other, n.gate_part, n.down_part, n.out_g, n.out_g__y0)
    v[n.gate_back] = return_columns(sum_halves(v[n.gate_part], v[n.gate_other]), place)
    v[n.down_other] = other_half(v[n.down_part])
    add(n.out_g__f)
    n1_grad = add_shares(n1_grad_parts[0], (v[n.t1], v[n.t2], v[n.t3]))
    input_part, _ = normed_grad(x_own.astype(f32), gain_one, n1_grad)
    input_grad = (h1_grad + input_part).reshape(1, tokens, width)
    sync(n.inp_g, n.inp_g__y0, n.gate_back, n.up_other, n.up_part, n.y1, n.y2, n.y3)
    add(n.inp_g__f)
    v[n.up_back] = return_columns(sum_halves(v[n.up_part], v[n.up_other]), place)
    y = add_shares(y_parts[0], (v[n.y1], v[n.y2], v[n.y3]))
    result = h1 + y
    block_out = result.astype(bf16).reshape(1, tokens, width)
    kept = valid_mask.reshape(tokens, 1).astype(f32)
    squares = jnp.stack(
        [jnp.sum(kept * result * result), jnp.sum(kept * mix * mix), jnp.sum(kept * y * y)]
    )
    squares = sum_group(jnp.pad(squares, (0, 125)).reshape(1, 128), ("p", "q"))
    v[n.squares] = sum_group(squares, ("y", "c"))
    sync(n.inp_g__f, n.inp_g__y1, n.inp_g, n.out_g, n.out_g__f, n.squares, n.down_other)
    v[n.squares] = sum_over(v[n.squares], "h")
    gate_back, up_back = v[n.gate_back], v[n.up_back]
    in_back = return_columns(live.summed(n.inp), place)
    down_sum = sum_halves(v[n.down_part], v[n.down_other])
    v[n.ffnout] = lax.ppermute(down_sum.astype(bf16), AXES, inverse(down_moves))
    outproj_grad = lax.ppermute(live.summed(n.out).astype(bf16), AXES, inverse(out_moves))
    ffnout_grad = v[n.ffnout]
    ffnout_grad, outproj_grad = ffnout_grad.astype(f32), outproj_grad.astype(f32)
    ffnin_grad = jnp.concatenate(gate_back + up_back, axis=1)
    inproj_grad = jnp.concatenate(
        [part[:, :KEYS] for part in in_back]
        + [part[:, KEYS:VALUES] for part in in_back]
        + [part[:, VALUES:GATES] for part in in_back]
        + [part[:, GATES:RANKS] for part in in_back]
        + [sum(part[:, RANKS : RANKS + RANK] for part in in_back)],
        axis=1,
    )
    squares = v[n.squares].reshape(-1)[:3]
    root_means = jnp.sqrt(squares / (jnp.maximum(valid_count, 1.0) * width))
    spares = sum(part[:, first:] for part in in_back)
    mixgain_grad, ffngain_grad = spares[:, 0], spares[:, 1]
    headgain_grad = spares[:head_each, 2]
    decay_own = spares[:, 3 : 3 + spare].reshape(-1)[: (RANK + 1) * up_cols]
    decay_own = decay_own.reshape(RANK + 1, up_cols)
    return (
        block_out,
        input_grad,
        inproj_grad,
        outproj_grad,
        decay_own[:RANK],
        decay_own[RANK],
        mixgain_grad,
        headgain_grad,
        ffnin_grad,
        ffnout_grad,
        ffngain_grad,
        root_means,
    )


def mm_nt(left, right, out=f32):
    return dot_nt(left, right).astype(out)


def solution(mesh):
    dp, seq = mesh.shape["dp"], mesh.shape["seq"]
    fine = Mesh(mesh.devices.reshape(dp // 2, 2, seq // 4, 2, 2), AXES)
    batch, spread, whole = ("y", "c"), ("h", "p", "q"), AXES
    placed = (
        P(batch, spread, None),
        P(whole, None),
        P(whole, None),
        P(None, whole),
        P(whole),
        P(whole),
        P(whole),
        P(whole, None),
        P(whole, None),
        P(whole),
        P(batch, spread, None),
        P(batch, spread),
        P(batch, spread),
    )
    return jax.shard_map(
        local,
        mesh=fine,
        in_specs=placed,
        out_specs=(
            P(batch, spread, None),
            P(batch, spread, None),
            P(whole, None),
            P(whole, None),
            P(None, whole),
            P(whole),
            P(whole),
            P(whole),
            P(whole, None),
            P(whole, None),
            P(whole),
            P(),
        ),
        check_vma=False,
    )
```

```python
import jax
import jax.numpy as jnp
from jax import lax
from jax.experimental import pallas as pl
from jax.experimental.pallas import tpu as pltpu
from jax.sharding import Mesh, PartitionSpec as P

HEADS = 4
KEY = 256
VAL = 512
SPAN = 64
RANK = 16
LANES = 128
EPS = 1e-05
FLOOR = 1.0
QSCALE = KEY**-0.5
KEYS, VALUES, GATES, RANKS = KEY, 2 * KEY, 2 * KEY + VAL, 2 * KEY + 2 * VAL

AXES = ("y", "c", "h", "p", "q")
COPIES = ("y", "c", "h")


bf16 = jnp.bfloat16
f32 = jnp.float32


def after(value, *deps):
    return lax.optimization_barrier((value, deps))[0]


def together(*values):
    return lax.optimization_barrier(values)


def swap(value, axis):
    return lax.ppermute(value, axis, [(0, 1), (1, 0)])


def across(value, mask, group=("p", "q")):
    return lax.ppermute(value, group, [(i, i ^ mask) for i in range(4)])


def two_of(value, group=("p", "q")):
    return across(value, 1, group), across(value, 2, group)


def last_of(value, group=("p", "q")):
    return across(value, 3, group)


def shares(parts):
    return [parts[mask].astype(bf16) for mask in range(4)]


def add_shares(own, received):
    return own + received[0].astype(f32) + received[1].astype(f32) + received[2].astype(f32)


def half_swap(block):
    return swap(block, "h") if binary_copies() else block


def stack_axis(value, axis):
    if lax.axis_size(axis) != 2:
        return lax.all_gather(value, axis)
    other = swap(value, axis)
    first = lax.axis_index(axis) == 0
    return jnp.where(first, jnp.stack([value, other]), jnp.stack([other, value]))


def sum_over(value, axis):
    if lax.axis_size(axis) == 2:
        return value + swap(value, axis)
    return lax.psum(value, axis)


def sum_group(value, axes):
    if any(lax.axis_size(axis) != 2 for axis in axes):
        return lax.psum(value, axes)
    return value + across(value, 1, axes) + across(value, 2, axes) + across(value, 3, axes)


def binary_copies():
    return all(lax.axis_size(axis) == 2 for axis in COPIES)


def lay_kernel(offsets, pieces, count, *refs):
    blocks, whole, sems = refs[:count], refs[count], refs[count + 1]
    copies = []
    for i, (block, first, rows) in enumerate(pieces):
        place = pl.ds(pl.multiple_of(offsets[i], 16), rows)
        copies.append(
            pltpu.make_async_copy(
                blocks[block].at[pl.ds(first, rows)], whole.at[place], sems.at[i]
            )
        )
    for copy in copies:
        copy.start()
    for copy in copies:
        copy.wait()


def lay(blocks, pieces, offsets):
    cols, kind = blocks[0].shape[1], blocks[0].dtype
    total = sum(rows for _, _, rows in pieces)
    return pl.pallas_call(
        lambda offsets, *refs: lay_kernel(offsets, pieces, len(blocks), *refs),
        grid_spec=pltpu.PrefetchScalarGridSpec(
            num_scalar_prefetch=1,
            grid=(1,),
            in_specs=[pl.BlockSpec(memory_space=pl.ANY)] * len(blocks),
            out_specs=pl.BlockSpec(memory_space=pl.ANY),
            scratch_shapes=[pltpu.SemaphoreType.DMA((len(pieces),))],
        ),
        out_shape=jax.ShapeDtypeStruct((total, cols), kind),
        compiler_params=pltpu.CompilerParams(vmem_limit_bytes=16 * 1024 * 1024),
        cost_estimate=pl.CostEstimate(
            flops=0, bytes_accessed=2 * total * cols * kind.itemsize, transcendentals=0
        ),
    )(jnp.stack(offsets).astype(jnp.int32), *blocks)


def in_order(blocks):
    rows = blocks[0].shape[0]
    pieces = [(i, 0, rows) for i in range(len(blocks))]
    return lay(blocks, pieces, [jnp.int32(i * rows) for i in range(len(blocks))])


def pick(value, index, axis):
    return lax.dynamic_index_in_dim(value, index, axis, keepdims=False)


class Names:
    def __getattr__(self, name):
        return name


n = Names()


class Live:
    def __init__(self, **values):
        self.v = dict(values)
        self.binary = binary_copies()
        self.at = {axis: lax.axis_index(axis) for axis in AXES}

    def sync(self, *names):
        self.v.update(zip(names, lax.optimization_barrier([self.v[name] for name in names])))

    def swap(self, name, value, axis):
        self.v[name] = swap(value(), axis) if self.binary else jnp.zeros((8, 128), bf16)

    def send(self, *names):
        for name in names:
            weight, way = name.split("__")
            source = weight if len(way) == 1 else weight + "__" + way[:-1]
            axis = "h" if way[-1] == "f" else way[-1]
            self.swap(name, lambda: self.v[source], axis)

    def gathered(self, weight):
        own = self.v[weight]
        if not self.binary:
            return lax.all_gather(own, COPIES, axis=0, tiled=True)
        rows, blocks, pieces, offsets = own.shape[0], [], [], []
        for way in ("", "y", "c", "yc", "f", "fy", "fc", "fyc"):
            y, c = self.at["y"] ^ ("y" in way), self.at["c"] ^ ("c" in way)
            f = self.at["h"] ^ ("f" in way)
            place = f * 4 + y * 2 + c if weight == n.out else y * 4 + c * 2 + f
            pieces.append((len(blocks), 0, rows))
            offsets.append(place * rows)
            blocks.append(self.v[weight + "__" + way] if way else own)
        return lay(blocks, pieces, offsets)

    def near(self, weight, y, f):
        c, total = self.at["c"], 0.0
        for value in (self.v[weight + "_g"], self.v[weight + "_g__c"]):
            rows, cols = value.shape
            place = f * 4 + y * 2 + c if weight == n.out else y * 4 + c * 2 + f
            value = lax.dynamic_slice_in_dim(value, place * (rows // 8), rows // 8, 0)
            total = total + value.astype(f32)
        return total

    def add(self, *names):
        for name in names:
            weight, way = name.split("_g__")
            y, f = self.at["y"], self.at["h"]
            if way == "c":
                self.swap(name, lambda: self.v[weight + "_g"], "c")
            elif way in ("y0", "y1"):
                which = 1 - f if way == "y0" else f
                self.swap(name, lambda: self.near(weight, 1 - y, which).astype(bf16), "y")
            else:
                first = weight + "_g__y0"
                self.swap(
                    name,
                    lambda: (self.near(weight, y, 1 - f) + self.v[first].astype(f32)).astype(bf16),
                    "h",
                )

    def summed(self, weight):
        grad = weight + "_g"
        if not self.binary:
            return lax.psum_scatter(
                self.v[grad], COPIES, scatter_dimension=0, tiled=True
            ).astype(f32)
        value = self.near(weight, self.at["y"], self.at["h"])
        return value + self.v[grad + "__y1"].astype(f32) + self.v[grad + "__f"].astype(f32)


def share_columns(weight, place, columns, group=("p", "q")):
    pieces = [columns(weight, t) for t in range(4)]
    got = []
    for mask in range(4):
        piece = lax.select_n(place, *[pieces[t ^ mask] for t in range(4)])
        got.append(piece if mask == 0 else across(piece, mask, group))
    return jnp.concatenate(
        [lax.select_n(place, *[got[t ^ spot] for t in range(4)]) for spot in range(4)]
    )


def return_columns(grad, place, group=("p", "q")):
    value = grad.reshape(4, grad.shape[0] // 4, grad.shape[1])
    got = [pick(value, place, 0).astype(f32)]
    for mask in (1, 2, 3):
        got.append(across(pick(value, place ^ mask, 0).astype(bf16), mask, group).astype(f32))
    return [lax.select_n(place, *[got[t ^ spot] for t in range(4)]) for spot in range(4)]


def both_halves(own, other):
    first = lax.axis_index("h") == 0
    return jnp.where(first, jnp.concatenate([own, other]), jnp.concatenate([other, own]))


def gather_halves(own, other, tall):
    if not binary_copies():
        return lax.all_gather(own, COPIES, axis=0, tiled=True)
    both = both_halves(own, other)
    if not tall:
        return lax.all_gather(both, ("y", "c"), axis=0, tiled=True)
    both = both.reshape(2, -1, own.shape[1])
    return lax.all_gather(both, ("y", "c"), axis=1, tiled=True).reshape(-1, own.shape[1])


def sum_near(grad, tall):
    if not binary_copies():
        return lax.psum_scatter(grad, COPIES, scatter_dimension=0, tiled=True)
    cols = grad.shape[1]
    if tall:
        grad = grad.reshape(2, -1, cols)
        return lax.psum_scatter(grad, ("y", "c"), scatter_dimension=1, tiled=True)
    return lax.psum_scatter(grad, ("y", "c"), scatter_dimension=0, tiled=True).reshape(2, -1, cols)


def other_half(part):
    if not binary_copies():
        return jnp.zeros((8, 128), bf16)
    return swap(pick(part, 1 - lax.axis_index("h"), 0), "h")


def sum_halves(part, other):
    if not binary_copies():
        return part.astype(f32)
    return pick(part, lax.axis_index("h"), 0).astype(f32) + other.astype(f32)


def row_owner_moves():
    total = 1
    for axis in AXES:
        total *= lax.axis_size(axis)
    if not binary_copies():
        copies = total // 4
        return [(g, (g % copies) * 4 + g // copies) for g in range(total)]
    pairs = []
    for g in range(total):
        y, c, h, p, q = (g >> bit & 1 for bit in (4, 3, 2, 1, 0))
        to = (p, q, h, y, c)
        pairs.append((g, sum(bit << (4 - i) for i, bit in enumerate(to))))
    return pairs


def dot_nn(a, b):
    return lax.dot_general(a, b, (((1,), (0,)), ((), ())), preferred_element_type=f32)


def dot_nt(a, b):
    return lax.dot_general(a, b, (((1,), (1,)), ((), ())), preferred_element_type=f32)


def dot_tn(a, b):
    return lax.dot_general(a, b, (((0,), (0,)), ((), ())), preferred_element_type=f32)


def two_parts(value):
    high = value.astype(bf16)
    return high, (value - high.astype(f32)).astype(bf16)


def triangle(lower):
    row = lax.broadcasted_iota(jnp.int32, (SPAN, SPAN), 0)
    col = lax.broadcasted_iota(jnp.int32, (SPAN, SPAN), 1)
    return jnp.where(row >= col if lower else row <= col, 1.0, 0.0)


def running_sum(value, lower):
    ones = triangle(lower).astype(bf16)
    high, low = two_parts(value)
    return dot_nn(ones, high) + dot_nn(ones, low)


def pair_mask(meta, rows):
    return jnp.where(meta[:, 0:1] == rows[0:1, :], triangle(True), 0.0)


def states_kernel(
    place, proj, up, bias, meta, rows, sums, raw, prior, through, end, decay, state, total
):
    @pl.when(pl.program_id(0) == 0)
    def _():
        state[...] = jnp.zeros_like(state)
        total[...] = jnp.ones_like(total)

    keys = proj[:, KEYS:VALUES].astype(bf16).astype(f32)
    gate = dot_nn(proj[:, RANKS:].astype(bf16), up[...]) + bias[...]
    log_decay = (jnp.minimum(gate, 0.0) - jnp.log1p(jnp.exp(-jnp.abs(gate)))) * (1.0 / 16.0)
    run = running_sum(log_decay, True)
    raw[...] = gate
    sums[...] = run
    last = run[SPAN - 1 :, :]
    info = meta[...]
    k_final = (keys * jnp.exp(last - run) * (info[:, 1:2] * info[:, 3:4])).astype(bf16)
    step = rows[0, 1:2, 0:1] * jnp.exp(last)
    prior[0] = state[...].astype(bf16)
    through[0] = total[...]
    state[...] = step * state[...] + dot_tn(proj[:, VALUES:GATES].astype(bf16), k_final)
    total[...] = step * total[...]
    end[...] = state[...].astype(bf16)
    decay[...] = total[...]


def mixed_kernel(place, proj, sums, prior, through, entering, gain, meta, rows, gated, mixed):
    info = meta[...]
    run = sums[...]
    query = proj[:, :KEYS].astype(bf16).astype(f32)
    q_decay = (query * QSCALE * jnp.exp(run)).astype(bf16)
    k_decay = (proj[:, KEYS:VALUES].astype(bf16).astype(f32) * info[:, 1:2] * jnp.exp(-run)).astype(bf16)
    scores = (dot_nt(q_decay, k_decay) * pair_mask(info, rows[0])).astype(bf16)
    state = (prior[0].astype(f32) + through[0] * entering[...].astype(f32)).astype(bf16)
    out = dot_nn(scores, proj[:, VALUES:GATES].astype(bf16)) + info[:, 2:3] * dot_nt(q_decay, state)
    mixed[...] = out
    gate = proj[:, GATES:RANKS]
    scale = lax.rsqrt(jnp.mean(out * out, axis=-1, keepdims=True) + FLOOR)
    gated[...] = (out * scale * gain[...] * gate * jax.nn.sigmoid(gate)).astype(bf16)


def gate_grad_kernel(
    place,
    grad_gated,
    proj,
    mixed,
    sums,
    gain,
    meta,
    rows,
    grad_out,
    grad_gate,
    later,
    beyond,
    start,
    decay,
    grad_gain,
    state,
    total,
):
    @pl.when(pl.program_id(0) == 0)
    def _():
        state[...] = jnp.zeros_like(state)
        total[...] = jnp.ones_like(total)
        grad_gain[...] = jnp.zeros_like(grad_gain)

    info = meta[...]
    run = sums[...]
    out = mixed[...]
    gate = proj[:, GATES:RANKS]
    grad = grad_gated[...]
    sig = jax.nn.sigmoid(gate)
    scale = lax.rsqrt(jnp.mean(out * out, axis=-1, keepdims=True) + FLOOR)
    scaled = out * scale
    swish = gate * sig
    weighted = grad * gain[...] * swish
    inner = jnp.mean(scaled * weighted, axis=-1, keepdims=True)
    grad_o = (scale * (weighted - scaled * inner)).astype(bf16)
    grad_out[...] = grad_o
    grad_gate[...] = (grad * scaled * gain[...] * sig * (1.0 + gate * (1.0 - sig))).astype(bf16)
    grad_gain[...] += jnp.sum(grad * scaled * swish, axis=0, keepdims=True)
    query = proj[:, :KEYS].astype(bf16).astype(f32)
    q_enter = (query * QSCALE * jnp.exp(run)).astype(bf16)
    o_enter = jnp.where(info[:, 2:3] > 0.0, grad_o.astype(f32), 0.0).astype(bf16)
    step = rows[0, 1:2, 0:1] * jnp.exp(run[SPAN - 1 :, :])
    later[0] = state[...].astype(bf16)
    beyond[0] = total[...]
    state[...] = step * state[...] + dot_tn(o_enter, q_enter)
    total[...] = step * total[...]
    start[...] = state[...].astype(bf16)
    decay[...] = total[...]


def inputs_grad_kernel(
    place,
    proj,
    sums,
    raw,
    grad_out,
    grad_gate,
    prior,
    through,
    entering,
    later,
    beyond,
    leaving,
    up,
    meta,
    rows,
    grad_proj,
    grad_up,
    grad_bias,
):
    @pl.when(pl.program_id(0) == 0)
    def _():
        grad_up[...] = jnp.zeros_like(grad_up)
        grad_bias[...] = jnp.zeros_like(grad_bias)

    info = meta[...]
    run = sums[...]
    last = run[SPAN - 1 :, :]
    valid, enter, carry = info[:, 1:2], info[:, 2:3], info[:, 3:4]
    grow, shrink, tail = jnp.exp(run), jnp.exp(-run), jnp.exp(last - run) * carry
    query = proj[:, :KEYS].astype(bf16).astype(f32)
    keys = proj[:, KEYS:VALUES].astype(bf16).astype(f32) * valid
    values = proj[:, VALUES:GATES].astype(bf16)
    q_decay = (query * QSCALE * grow).astype(bf16)
    k_decay = (keys * shrink).astype(bf16)
    k_final = (keys * tail).astype(bf16)
    mask = pair_mask(info, rows[0])
    state = prior[0].astype(f32) + through[0] * entering[...].astype(f32)
    state_grad = later[0].astype(f32) + beyond[0] * leaving[...].astype(f32)
    state_b, state_grad_b = state.astype(bf16), state_grad.astype(bf16)
    grad_o = grad_out[...]
    scores = (dot_nt(q_decay, k_decay) * mask).astype(bf16)
    grad_scores = (dot_nt(grad_o, values) * mask).astype(bf16)
    grad_v = dot_tn(scores, grad_o) + dot_nt(k_final, state_grad_b)
    grad_qd = dot_nn(grad_scores, k_decay) + enter * dot_nn(grad_o, state_b)
    grad_kd = dot_tn(grad_scores, q_decay)
    grad_kf = dot_nn(values, state_grad_b)
    step = rows[0, 1:2, 0:1] * jnp.exp(last)
    through_last = step * jnp.sum(state * state_grad, axis=0, keepdims=True)
    final_part = grad_kf * k_final.astype(f32)
    grad_run = grad_qd * q_decay.astype(f32) - grad_kd * k_decay.astype(f32) - final_part
    grad_last = through_last + jnp.sum(final_part, axis=0, keepdims=True)
    grad_log = running_sum(grad_run, False) + grad_last
    grad_raw = grad_log * jax.nn.sigmoid(-raw[...]) * (1.0 / 16.0)
    high, low = two_parts(grad_raw)
    rank = proj[:, RANKS:].astype(bf16)
    grad_up[...] += dot_tn(rank, high) + dot_tn(rank, low)
    grad_bias[...] += jnp.sum(grad_raw, axis=0, keepdims=True)
    grad_rank = dot_nt(high, up[...]) + dot_nt(low, up[...])
    grad_k = (grad_kd * shrink + grad_kf * tail) * valid
    grad_proj[:, KEYS:VALUES] = grad_k.astype(bf16)
    grad_proj[:, VALUES:GATES] = grad_v.astype(bf16)
    grad_proj[:, RANKS:] = grad_rank.astype(bf16)
    grad_proj[:, :KEYS] = (grad_qd * grow * QSCALE).astype(bf16)
    grad_proj[:, GATES:RANKS] = grad_gate[...]


class Mixer:
    def __init__(self, place, blocks, per_device):
        self.place = place.reshape(1)
        self.blocks = blocks
        self.per_device = per_device

    def call(self, kernel, specs, args, outs, scratch=(), reverse=False, flops=0):
        count, per_device = self.blocks, self.per_device

        def at(step):
            return count - 1 - step if reverse else step

        def spec(kind, shape):
            if kind == "rows":
                return pl.BlockSpec(
                    (SPAN, shape[1]),
                    lambda n, place: (
                        lax.bitwise_xor(at(n) // per_device, place[0]) * per_device
                        + at(n) % per_device,
                        0,
                    ),
                )
            if kind == "tokens":
                return pl.BlockSpec((SPAN, shape[1]), lambda n, place: (at(n), 0))
            if kind == "blocks":
                return pl.BlockSpec((1,) + shape[1:], lambda n, place: (at(n), 0, 0))
            return pl.BlockSpec(shape, lambda n, place: (0,) * len(shape))

        size = sum(a.size * a.dtype.itemsize for a in args)
        return pl.pallas_call(
            kernel,
            grid_spec=pltpu.PrefetchScalarGridSpec(
                num_scalar_prefetch=1,
                grid=(count,),
                in_specs=[spec(kind, a.shape) for kind, a in zip(specs, args)],
                out_specs=[spec(kind, shape) for kind, shape, _ in outs],
                scratch_shapes=list(scratch),
            ),
            out_shape=[jax.ShapeDtypeStruct(shape, kind) for _, shape, kind in outs],
            compiler_params=pltpu.CompilerParams(
                dimension_semantics=("arbitrary",), vmem_limit_bytes=48 * 1024 * 1024
            ),
            cost_estimate=pl.CostEstimate(
                flops=flops, bytes_accessed=2 * size, transcendentals=4 * SPAN * KEY * count
            ),
        )(self.place, *args)


def normed(values, gain):
    return values * lax.rsqrt(jnp.mean(values * values, axis=-1, keepdims=True) + EPS) * gain


def normed_grad(values, gain, grad):
    scale = lax.rsqrt(jnp.mean(values * values, axis=-1, keepdims=True) + EPS)
    weighted = grad * gain
    inner = jnp.mean(weighted * values, axis=-1, keepdims=True)
    return (
        scale * weighted - scale * scale * scale * values * inner,
        jnp.sum(grad * values * scale, axis=0),
    )


def mm(left, right, out=f32):
    return jnp.dot(left, right, preferred_element_type=f32).astype(out)


def mm_tn(left, right, out=f32):
    return dot_tn(left, right).astype(out)


def in_columns(weight, t):
    wide, tall = HEADS * KEY, HEADS * VAL
    starts = [(0, KEY), (wide, KEY), (2 * wide, VAL), (2 * wide + tall, VAL)]
    heads = [weight[:, start + t * size : start + (t + 1) * size] for start, size in starts]
    rank = weight[:, 2 * wide + 2 * tall :]
    return jnp.concatenate(heads + [jnp.pad(rank, ((0, 0), (0, LANES - RANK)))], axis=1)


def from_earlier(end, decay):
    count = lax.axis_size("h")
    if count == 2:
        return lax.ppermute(end, "h", [(0, 1)])
    ends, decays = lax.all_gather(end, "h"), lax.all_gather(decay, "h")
    mine = lax.axis_index("h")
    state = jnp.zeros(end.shape, f32)
    for h in range(count - 1):
        state = jnp.where(h < mine, decays[h] * state + ends[h].astype(f32), state)
    return state.astype(bf16)


def from_later(start, decay):
    count = lax.axis_size("h")
    if count == 2:
        return lax.ppermute(start, "h", [(1, 0)])
    starts, decays = lax.all_gather(start, "h"), lax.all_gather(decay, "h")
    mine = lax.axis_index("h")
    state = jnp.zeros(start.shape, f32)
    for h in range(count - 1, 0, -1):
        state = jnp.where(h > mine, decays[h] * state + starts[h].astype(f32), state)
    return state.astype(bf16)


def local(
    hidden_in,
    in_weight,
    out_weight,
    decay_up,
    decay_bias,
    mixer_gain,
    head_gain,
    ffn_in,
    ffn_out,
    ffn_gain,
    out_grad,
    seg_ids,
    valid_mask,
):
    tokens, width = hidden_in.shape[1:]
    place = 2 * lax.axis_index("p") + lax.axis_index("q")
    half = lax.axis_index("h")
    sizes = [lax.axis_size(axis) for axis in AXES]
    devices = sizes[0] * sizes[1] * sizes[2] * 4
    me = place
    stride = 4
    for axis in ("h", "c", "y"):
        me = me + stride * lax.axis_index(axis)
        stride *= lax.axis_size(axis)
    ff = ffn_in.shape[1] // 2
    quarter = ff // 4
    rows_all = 4 * tokens
    count = rows_all // SPAN
    x_own = hidden_in.reshape(tokens, width)
    dy_own = out_grad.reshape(tokens, width)

    small = [
        decay_up.reshape(-1),
        decay_bias,
        mixer_gain,
        head_gain,
        ffn_gain,
        seg_ids.reshape(-1).astype(bf16),
        valid_mask.reshape(-1).astype(bf16),
    ]
    lengths = [part.shape[0] for part in small]
    packed = jnp.concatenate(small)
    padded = -(-packed.shape[0] // 1024) * 1024
    packed = jnp.pad(packed, (0, padded - packed.shape[0])).reshape(-1, 128)
    offset = [sum(lengths[:i]) for i in range(len(lengths) + 1)]

    def gateup_columns(weight, t):
        return jnp.concatenate(
            [
                weight[:, t * quarter : (t + 1) * quarter],
                weight[:, ff + t * quarter : ff + (t + 1) * quarter],
            ],
            axis=1,
        )

    def inverse(pairs):
        return [(b, a) for a, b in pairs]

    out_moves, down_moves = row_owner_moves(), row_owner_moves()
    live = Live(x=x_own, dy=dy_own, ffn_in=ffn_in, ffn_out=ffn_out, out_weight=out_weight)
    v, sync, send, add = live.v, live.sync, live.send, live.add

    v[n.inp] = share_columns(in_weight, place, in_columns)
    for axis in ("q", "p", "c", "y"):
        packed = stack_axis(packed, axis)
    sync(n.inp, n.out_weight, n.ffn_in)
    send(n.inp__f, n.inp__y, n.inp__c)
    v[n.gateup] = share_columns(v[n.ffn_in], place, gateup_columns)
    v[n.out] = lax.ppermute(v[n.out_weight], AXES, out_moves)
    v[n.packed] = packed
    sync(n.inp__f, n.inp__y, n.inp__c, n.x, n.out, n.packed)
    send(n.inp__fy, n.inp__fc, n.inp__yc)
    v[n.x1], v[n.x2] = two_of(v[n.x])
    v[n.x3] = last_of(v[n.x])
    send(n.out__f, n.out__y, n.out__c)
    v[n.packed] = jnp.moveaxis(stack_axis(v[n.packed], "h"), 0, 2)
    sync(n.inp__fy, n.inp__fc, n.inp__yc, n.x1, n.x2, n.x3, n.out__f, n.out__y, n.out__c, n.gateup, n.packed)
    send(n.inp__fyc, n.out__fy, n.out__fc, n.out__yc)
    v[n.gate], v[n.up] = v[n.gateup][:, :quarter], v[n.gateup][:, quarter:]
    v[n.gate__f] = half_swap(v[n.gate])
    sync(n.inp__fyc, n.out__fy, n.out__fc, n.out__yc, n.gate, n.up, n.ffn_out, n.dy)
    send(n.out__fyc)
    packed = v[n.packed]
    everyone = packed.reshape(sizes[0], sizes[1], -1, padded)

    def small_part(i):
        return everyone[..., offset[i] : offset[i + 1]]

    up_cols = decay_up.shape[1]
    up_all = small_part(0).reshape(devices, RANK, up_cols).transpose(1, 0, 2).reshape(RANK, HEADS, KEY)
    up_head = jnp.pad(pick(up_all, place, 1), ((0, LANES - RANK), (0, 0)))
    bias_head = pick(small_part(1).reshape(HEADS, 1, KEY), place, 0).astype(f32)
    gain_one = small_part(2).reshape(-1).astype(f32)
    gain_head = small_part(3).reshape(1, -1).astype(f32)
    gain_two = small_part(4).reshape(-1).astype(f32)

    def of_sequence(value):
        return pick(pick(value, lax.axis_index("y"), 0), lax.axis_index("c"), 0).reshape(-1)

    seg_all = of_sequence(small_part(5)).astype(f32)
    valid_all = of_sequence(small_part(6)).astype(f32)
    valid_count = jnp.sum(small_part(6).astype(f32))
    seg_here = lax.dynamic_slice(
        jnp.concatenate([jnp.full((1,), -1.0, f32), seg_all]), (half * rows_all,), (rows_all + 1,)
    )
    valid_here = lax.dynamic_slice(valid_all, (half * rows_all,), (rows_all,))
    seg_blocks = seg_here[1:].reshape(count, SPAN)
    before = seg_here[:-1].reshape(count, SPAN)[:, :1]
    final = seg_blocks[:, -1:]
    meta = jnp.stack(
        [
            seg_here[1:],
            valid_here,
            (seg_blocks == before).astype(f32).reshape(-1),
            (seg_blocks == final).astype(f32).reshape(-1),
        ]
        + [jnp.zeros((rows_all,), f32)] * 4,
        axis=1,
    )
    keep = jnp.broadcast_to((final == before).astype(f32), (count, SPAN))
    rows = jnp.stack([seg_blocks, keep] + [jnp.zeros((count, SPAN), f32)] * 6, axis=1)

    x_group = in_order([x_own, v[n.x1], v[n.x2], v[n.x3]])
    w_in = live.gathered(n.inp)
    n1 = normed(x_group.astype(f32), gain_one).astype(bf16)
    proj = mm(n1, w_in)
    mixer = Mixer(place, count, tokens // SPAN)
    state_shape = (VAL, KEY)
    scratch = [pltpu.VMEM(state_shape, f32), pltpu.VMEM((1, KEY), f32)]
    sums, raw, prior, through, v[n.end], decay = mixer.call(
        states_kernel,
        ["rows", "whole", "whole", "tokens", "blocks"],
        [proj, up_head, bias_head, meta, rows],
        [
            ("rows", (rows_all, KEY), f32),
            ("rows", (rows_all, KEY), f32),
            ("blocks", (count,) + state_shape, bf16),
            ("blocks", (count, 1, KEY), f32),
            ("whole", state_shape, bf16),
            ("whole", (1, KEY), f32),
        ],
        scratch,
        flops=2 * rows_all * KEY * VAL,
    )
    v[n.w_out] = live.gathered(n.out)
    sync(n.end, n.ffn_out, n.w_out)
    w_out = v[n.w_out]
    v[n.entering] = from_earlier(v[n.end], decay)
    v[n.down] = lax.ppermute(v[n.ffn_out], AXES, down_moves)
    entering = v[n.entering]
    sync(n.entering, n.gate, n.gate__f, n.up)
    v[n.up__f] = half_swap(v[n.up])
    w_gate = gather_halves(v[n.gate], v[n.gate__f], False)
    gated, mixed = mixer.call(
        mixed_kernel,
        ["rows", "rows", "blocks", "blocks", "whole", "whole", "tokens", "blocks"],
        [proj, sums, prior, through, entering, gain_head, meta, rows],
        [("rows", (rows_all, VAL), bf16), ("rows", (rows_all, VAL), f32)],
        flops=2 * rows_all * (KEY * VAL + SPAN * (KEY + VAL)),
    )
    mix_parts = mm(gated, w_out).reshape(4, tokens, width)
    mix_own = mix_parts[0]
    v[n.mix_send] = shares(mix_parts)
    sync(n.mix_send)
    v[n.mix1], v[n.mix2] = across(v[n.mix_send][1], 1), across(v[n.mix_send][2], 2)
    sync(n.mix1, n.mix2, n.mix_send, n.down, n.up, n.up__f)
    v[n.down__f] = half_swap(v[n.down])
    v[n.w_up] = gather_halves(v[n.up], v[n.up__f], False)
    v[n.w_gate] = w_gate
    v[n.mix3] = across(v[n.mix_send][3], 3)
    sync(n.mix3)
    mix = add_shares(mix_own, (v[n.mix1], v[n.mix2], v[n.mix3]))
    h1 = x_own.astype(f32) + mix
    v[n.n2] = normed(h1, gain_two).astype(bf16)
    v[n.n21], v[n.n22] = two_of(v[n.n2])
    sync(n.n21, n.n22, n.n2, n.dy, n.down, n.down__f)
    w_down = gather_halves(v[n.down], v[n.down__f], True)
    v[n.n23] = last_of(v[n.n2])
    sync(n.n21, n.n22, n.n23, n.n2, n.dy, n.w_gate, n.w_up)
    w_gate, w_up = v[n.w_gate], v[n.w_up]
    v[n.dy1], v[n.dy2] = two_of(v[n.dy])
    v[n.dy3] = last_of(v[n.dy])
    n2_group = in_order([v[n.n2], v[n.n21], v[n.n22], v[n.n23]])
    dy_group = in_order([dy_own, v[n.dy1], v[n.dy2], v[n.dy3]])
    gate = mm(n2_group, w_gate)
    up = mm(n2_group, w_up)
    grad_hidden = mm_nt(dy_group, w_down)

    sig = jax.nn.sigmoid(gate)
    hidden = (gate * sig * up).astype(bf16)
    grad_g = (grad_hidden * up * sig * (1.0 + gate * (1.0 - sig))).astype(bf16)
    grad_u = (grad_hidden * gate * sig).astype(bf16)
    n2_grad_parts = (mm_nt(grad_g, w_gate) + mm_nt(grad_u, w_up)).reshape(4, tokens, width)
    v[n.n2_send] = shares(n2_grad_parts)
    v[n.grad_g], v[n.grad_u], v[n.hidden] = grad_g, grad_u, hidden
    sync(n.n2_send, n.grad_g, n.grad_u, n.hidden)
    v[n.s1], v[n.s2] = across(v[n.n2_send][1], 1), across(v[n.n2_send][2], 2)
    v[n.gate_g] = mm_tn(n2_group, v[n.grad_g], bf16)
    sync(n.s1, n.s2, n.n2_send, n.hidden, n.grad_u, n.gate_g)
    v[n.gate_part] = sum_near(v[n.gate_g], False)
    v[n.up_g] = mm_tn(n2_group, v[n.grad_u], bf16)
    v[n.s3] = across(v[n.n2_send][3], 3)
    sync(n.s3, n.hidden, n.up_g)
    v[n.up_part] = sum_near(v[n.up_g], False)
    n2_grad = add_shares(n2_grad_parts[0], (v[n.s1], v[n.s2], v[n.s3]))
    h1_grad_part, gain_two_grad = normed_grad(h1, gain_two, n2_grad)
    h1_grad = dy_own.astype(f32) + h1_grad_part
    v[n.dmix] = h1_grad.astype(bf16)
    v[n.dmix1], v[n.dmix2] = two_of(v[n.dmix])
    v[n.down_g] = mm_tn(v[n.hidden], dy_group, bf16)
    sync(n.dmix, n.dmix1, n.dmix2, n.hidden, n.down_g)
    v[n.down_part] = sum_near(v[n.down_g], True)
    v[n.dmix3] = last_of(v[n.dmix])
    sync(n.dmix, n.dmix1, n.dmix2, n.dmix3)
    mix_grad = in_order([v[n.dmix], v[n.dmix1], v[n.dmix2], v[n.dmix3]])
    grad_gated = mm_nt(mix_grad, w_out)
    grad_o, grad_gate, later, beyond, v[n.start], decay_b, head_grad = mixer.call(
        gate_grad_kernel,
        ["rows", "rows", "rows", "rows", "whole", "tokens", "blocks"],
        [grad_gated, proj, mixed, sums, gain_head, meta, rows],
        [
            ("rows", (rows_all, VAL), bf16),
            ("rows", (rows_all, VAL), bf16),
            ("blocks", (count,) + state_shape, bf16),
            ("blocks", (count, 1, KEY), f32),
            ("whole", state_shape, bf16),
            ("whole", (1, KEY), f32),
            ("whole", (1, VAL), f32),
        ],
        scratch,
        reverse=True,
        flops=2 * rows_all * KEY * VAL,
    )
    sync(n.start, n.hidden)
    y_parts = mm(v[n.hidden], w_down).reshape(4, tokens, width)
    v[n.y_send] = shares(y_parts)
    v[n.leaving] = from_later(v[n.start], decay_b)
    v[n.out_g] = mm_tn(gated, mix_grad, bf16)
    sync(n.leaving, n.y_send, n.out_g, n.gate_part)
    v[n.gate_other] = other_half(v[n.gate_part])
    v[n.y1], v[n.y2] = across(v[n.y_send][1], 1), across(v[n.y_send][2], 2)
    add(n.out_g__c)
    leaving = v[n.leaving]
    v[n.grad_proj], rank_grad, bias_grad = mixer.call(
        inputs_grad_kernel,
        ["rows"] * 5 + ["blocks", "blocks", "whole", "blocks", "blocks", "whole", "whole", "tokens", "blocks"],
        [
            proj,
            sums,
            raw,
            grad_o,
            grad_gate,
            prior,
            through,
            entering,
            later,
            beyond,
            leaving,
            up_head,
            meta,
            rows,
        ],
        [
            ("rows", proj.shape, bf16),
            ("whole", (LANES, KEY), f32),
            ("whole", (1, KEY), f32),
        ],
        flops=2 * rows_all * (3 * KEY * VAL + SPAN * (3 * KEY + 2 * VAL)),
    )
    n1_grad_all = mm_nt(v[n.grad_proj], w_in)
    n1_grad_parts = n1_grad_all.reshape(4, tokens, width)
    v[n.n1_send] = shares(n1_grad_parts)
    sync(n.n1_send, n.grad_proj, n.y1, n.y2, n.y_send, n.out_g, n.out_g__c, n.up_part)
    v[n.up_other] = other_half(v[n.up_part])
    v[n.t1], v[n.t2] = across(v[n.n1_send][1], 1), across(v[n.n1_send][2], 2)
    v[n.y3] = across(v[n.y_send][3], 3)
    add(n.out_g__y0, n.out_g__y1)
    x_all = x_group.astype(f32)
    x_scale = lax.rsqrt(jnp.mean(x_all * x_all, axis=-1, keepdims=True) + EPS)
    gain_one_grad = jnp.sum(n1_grad_all * (x_all * x_scale), axis=0)
    each = width // devices
    decay_part = jnp.concatenate([rank_grad[:RANK], bias_grad], axis=0)
    decay_part = decay_part.reshape(RANK + 1, KEY // up_cols, up_cols).transpose(1, 0, 2)
    decay_part = decay_part.reshape(KEY // up_cols, -1)
    spare = -(-decay_part.shape[1] // each)
    decay_part = jnp.pad(decay_part, ((0, 0), (0, spare * each - decay_part.shape[1])))
    decay_part = decay_part.reshape(KEY // up_cols * each, spare)
    head_slot = lax.broadcasted_iota(jnp.int32, (HEADS, 1, 1), 0) == place
    decay_part = jnp.where(head_slot, decay_part[None], 0.0).reshape(width, spare)
    head_part = head_grad.reshape(devices, -1)
    head_each = head_part.shape[1]
    head_part = jnp.pad(head_part, ((0, 0), (0, each - head_each))).reshape(width)
    singles = jnp.stack([gain_one_grad, gain_two_grad, head_part], axis=1)
    extras = jnp.concatenate([singles, decay_part], axis=1)
    first = RANKS + RANK
    extras = jnp.pad(extras, ((0, 0), (first, RANKS + LANES - first - extras.shape[1])))
    v[n.inp_g] = (mm_tn(n1, v[n.grad_proj]) + extras).astype(bf16)
    sync(n.n1_send, n.t1, n.t2, n.inp_g, n.out_g__y0, n.out_g__y1, n.out_g, n.y3, n.gate_other)
    v[n.t3] = across(v[n.n1_send][3], 3)
    add(n.inp_g__c)
    sync(n.inp_g, n.inp_g__c)
    add(n.inp_g__y0, n.inp_g__y1)
    sync(n.t3, n.gate_other, n.gate_part, n.down_part, n.out_g, n.out_g__y0)
    v[n.gate_back] = return_columns(sum_halves(v[n.gate_part], v[n.gate_other]), place)
    v[n.down_other] = other_half(v[n.down_part])
    add(n.out_g__f)
    n1_grad = add_shares(n1_grad_parts[0], (v[n.t1], v[n.t2], v[n.t3]))
    input_part, _ = normed_grad(x_own.astype(f32), gain_one, n1_grad)
    input_grad = (h1_grad + input_part).reshape(1, tokens, width)
    sync(n.inp_g, n.inp_g__y0, n.gate_back, n.up_other, n.up_part, n.y1, n.y2, n.y3)
    add(n.inp_g__f)
    v[n.up_back] = return_columns(sum_halves(v[n.up_part], v[n.up_other]), place)
    y = add_shares(y_parts[0], (v[n.y1], v[n.y2], v[n.y3]))
    result = h1 + y
    block_out = result.astype(bf16).reshape(1, tokens, width)
    kept = valid_mask.reshape(tokens, 1).astype(f32)
    squares = jnp.stack(
        [jnp.sum(kept * result * result), jnp.sum(kept * mix * mix), jnp.sum(kept * y * y)]
    )
    squares = sum_group(jnp.pad(squares, (0, 125)).reshape(1, 128), ("p", "q"))
    v[n.squares] = sum_group(squares, ("y", "c"))
    sync(n.inp_g__f, n.inp_g__y1, n.inp_g, n.out_g, n.out_g__f, n.squares, n.down_other)
    v[n.squares] = sum_over(v[n.squares], "h")
    gate_back, up_back = v[n.gate_back], v[n.up_back]
    in_back = return_columns(live.summed(n.inp), place)
    down_sum = sum_halves(v[n.down_part], v[n.down_other])
    v[n.ffnout] = lax.ppermute(down_sum.astype(bf16), AXES, inverse(down_moves))
    outproj_grad = lax.ppermute(live.summed(n.out).astype(bf16), AXES, inverse(out_moves))
    ffnout_grad = v[n.ffnout]
    ffnout_grad, outproj_grad = ffnout_grad.astype(f32), outproj_grad.astype(f32)
    ffnin_grad = jnp.concatenate(gate_back + up_back, axis=1)
    inproj_grad = jnp.concatenate(
        [part[:, :KEYS] for part in in_back]
        + [part[:, KEYS:VALUES] for part in in_back]
        + [part[:, VALUES:GATES] for part in in_back]
        + [part[:, GATES:RANKS] for part in in_back]
        + [sum(part[:, RANKS : RANKS + RANK] for part in in_back)],
        axis=1,
    )
    squares = v[n.squares].reshape(-1)[:3]
    root_means = jnp.sqrt(squares / (jnp.maximum(valid_count, 1.0) * width))
    spares = sum(part[:, first:] for part in in_back)
    mixgain_grad, ffngain_grad = spares[:, 0], spares[:, 1]
    headgain_grad = spares[:head_each, 2]
    decay_own = spares[:, 3 : 3 + spare].reshape(-1)[: (RANK + 1) * up_cols]
    decay_own = decay_own.reshape(RANK + 1, up_cols)
    return (
        block_out,
        input_grad,
        inproj_grad,
        outproj_grad,
        decay_own[:RANK],
        decay_own[RANK],
        mixgain_grad,
        headgain_grad,
        ffnin_grad,
        ffnout_grad,
        ffngain_grad,
        root_means,
    )


def mm_nt(left, right, out=f32):
    return dot_nt(left, right).astype(out)


def solution(mesh):
    dp, seq = mesh.shape["dp"], mesh.shape["seq"]
    fine = Mesh(mesh.devices.reshape(dp // 2, 2, seq // 4, 2, 2), AXES)
    batch, spread, whole = ("y", "c"), ("h", "p", "q"), AXES
    placed = (
        P(batch, spread, None),
        P(whole, None),
        P(whole, None),
        P(None, whole),
        P(whole),
        P(whole),
        P(whole),
        P(whole, None),
        P(whole, None),
        P(whole),
        P(batch, spread, None),
        P(batch, spread),
        P(batch, spread),
    )
    return jax.shard_map(
        local,
        mesh=fine,
        in_specs=placed,
        out_specs=(
            P(batch, spread, None),
            P(batch, spread, None),
            P(whole, None),
            P(whole, None),
            P(None, whole),
            P(whole),
            P(whole),
            P(whole),
            P(whole, None),
            P(whole, None),
            P(whole),
            P(),
        ),
        check_vma=False,
    )
```
